32 devices in a mesh: dp: 16 (over z, y, x), seq: 2 (over core).
Axes of the slice: x: 2, y: 2, z: 4, core: 2. Of those that a mesh axis runs over, the one named last changes fastest.
Arguments:
- hidden_in: float32 [16, 512, 1024], P('dp', 'seq'), may hold values from -6 to 6
- upstream: float32 [16, 512, 1024], P('dp', 'seq'), may hold values from -6 to 6
- in_weight: bfloat16 [1024, 4384], P(('dp', 'seq')), may hold values from -0.1875 to 0.1875
- out_weight: bfloat16 [2048, 1024], P(('dp', 'seq')), may hold values from -0.125 to 0.125
- norm_gain: float32 [1024], replicated, may hold values from 0.5 to 1.5
- conv_weight: float32 [4, 2304], replicated, may hold values from -3 to 3
- conv_bias: float32 [2304], replicated, may hold values from -2 to 2
- step_bias: float32 [32], replicated, may hold values from -9 to -2
- log_rate: float32 [32], replicated, may hold values from 0 to 1.5
- skip_weight: float32 [32], replicated, may hold values from 0.5 to 1.5
- gate_gain: float32 [2048], replicated, may hold values from 0.5 to 1.5
Outputs:
- block_out: float32 [16, 512, 1024], P('dp', 'seq')
- grad_hidden: float32 [16, 512, 1024], P('dp', 'seq')
- grad_in_weight: float32 [1024, 4384], P(('dp', 'seq'))
- grad_out_weight: float32 [2048, 1024], P(('dp', 'seq'))
- grad_norm_gain: float32 [1024], replicated
- grad_conv_weight: float32 [4, 2304], replicated
- grad_conv_bias: float32 [2304], replicated
- grad_step_bias: float32 [32], replicated
- grad_log_rate: float32 [32], replicated
- grad_skip_weight: float32 [32], replicated
- grad_gate_gain: float32 [2048], replicated
The draws below stay inside these ranges and needn't reach their ends.
All inputs are finite; a program needn't handle non-finite values.
Results may differ from the reference program's by a relative error of at most 0.0077.
Values may be sent and summed in bfloat16 or wider, within the bound.
No kernel may reach another device: no remote copies, remote signals or barrier semaphores. Data moves between devices by JAX's collectives and lax.ppermute only.
A program may use at most 192 MiB of HBM per device.

```python
import jax
import jax.numpy as jnp
from jax import lax

D = 1024
D_INNER = 2048
HEADS = 32
HEAD_DIM = 64
STATE = 128
CONVK = 4
GROUP = 256
SEQS = 16
LENGTH = 512
CONV_CH = 2304
PROJ = 4384


def steps_of(stream_key, dims, cuts, smallest, high):
    factor_of, own = 1.0, jax.random.fold_in(stream_key, 6)
    for dim, parts in cuts:
        heights = jnp.exp(jax.random.uniform(jax.random.fold_in(own, dim), (parts,), jnp.float32, smallest / len(cuts), high / len(cuts)))
        factor_of = factor_of * jnp.repeat(heights, dims[dim] // parts).reshape([-1 if axis == dim else 1 for axis in range(len(dims))])
    return factor_of


def bell_draw(own_key, dims, width, reach, split=(), held_as=jnp.bfloat16):
    values = jax.random.normal(own_key, dims, jnp.float32) * width
    if len(split) > 0:
        values = steps_of(own_key, dims, split, -0.22, 0.18) * values
    return jnp.clip(values, min=-reach, max=reach).astype(held_as)


def setup_inputs(seed: int = 0) -> dict:
    key_of = jax.random.split(jax.random.key(seed), 12)
    return {
        "hidden_in": bell_draw(key_of[0], (SEQS, LENGTH, D), 1.0, 6.0, ((0, 16), (1, 2)), jnp.float32),
        "upstream": bell_draw(key_of[1], (SEQS, LENGTH, D), 1.0, 6.0, ((0, 16), (1, 2)), jnp.float32),
        "in_weight": bell_draw(key_of[2], (D, PROJ), D ** -0.5, 0.1875, ((0, 32),)),
        "out_weight": bell_draw(key_of[3], (D_INNER, D), D_INNER ** -0.5, 0.125, ((0, 32),)),
        "norm_gain": jnp.clip(1.0 + 0.1 * jax.random.normal(key_of[4], (D,), jnp.float32), 0.5, 1.5),
        "conv_weight": bell_draw(key_of[5], (CONVK, CONV_CH), 0.5, 3.0, (), jnp.float32),
        "conv_bias": bell_draw(key_of[6], (CONV_CH,), 0.3, 2.0, (), jnp.float32),
        "step_bias": jnp.clip(jax.random.uniform(key_of[7], (HEADS,), jnp.float32, -9.0, -2.0), -9.0, -2.0),
        "log_rate": jnp.clip(jax.random.uniform(key_of[8], (HEADS,), jnp.float32, 0.0, 1.5), 0.0, 1.5),
        "skip_weight": jnp.clip(jax.random.uniform(key_of[9], (HEADS,), jnp.float32, 0.5, 1.5), 0.5, 1.5),
        "gate_gain": jnp.clip(1.0 + 0.1 * jax.random.normal(key_of[10], (D_INNER,), jnp.float32), 0.5, 1.5),
    }


EPS = 1e-05
PRECISE = lax.Precision.HIGHEST

def rms_scale(values, gain):
    return values * lax.rsqrt(lax.optimization_barrier(jnp.mean(values * values, axis=-1, keepdims=True)) + EPS) * gain

def group_scan(inputs, b_mat, c_mat, deltas, decay_rates, start_state):
    count = inputs.shape[0] // GROUP
    causal = (jnp.arange(GROUP)[:, None] >= jnp.arange(GROUP)[None, :])[None, :, :]

    def one_group(running, pieces):
        x_piece, b_piece, c_piece, step_piece = pieces
        cumulative = jnp.cumsum(step_piece * decay_rates[None, :], axis=0)
        cum_heads = cumulative.T
        spread_log = jnp.where(causal, cum_heads[:, :, None] - cum_heads[:, None, :], 0.0)
        kernel_decay = jnp.where(causal, jnp.exp(spread_log), 0.0)
        inner_cb = jnp.dot(c_piece, b_piece.T, precision=PRECISE)
        weights = inner_cb[None, :, :] * kernel_decay * step_piece.T[:, None, :]
        intra_out = jnp.einsum('hts,shp->thp', weights, x_piece, precision=PRECISE)
        state_out = jnp.einsum('tn,hpn->thp', c_piece, running, precision=PRECISE) * jnp.exp(cumulative)[:, :, None]
        tail_weight = jnp.exp(cumulative[-1][None, :] - cumulative) * step_piece
        fresh = jnp.einsum('sh,shp,sn->hpn', tail_weight, x_piece, b_piece, precision=PRECISE)
        running = running * jnp.exp(cumulative[-1])[:, None, None] + fresh
        return (running, intra_out + state_out)
    pieces = (inputs.reshape(count, GROUP, HEADS, HEAD_DIM), b_mat.reshape(count, GROUP, STATE), c_mat.reshape(count, GROUP, STATE), deltas.reshape(count, GROUP, HEADS))
    final_state, out_blocks = lax.scan(one_group, start_state, pieces)
    return (out_blocks.reshape(inputs.shape), final_state)

def conv_act(extended, conv_weight, conv_bias):
    count = extended.shape[0] - (CONVK - 1)
    summed = conv_bias[None, :] + conv_weight[0][None, :] * extended[0:count]
    for offset in range(1, CONVK):
        summed = summed + conv_weight[offset][None, :] * extended[offset:offset + count]
    return jax.nn.silu(summed)

def mixer(extended, step_raw, conv_weight, conv_bias, step_bias, log_rate, skip_weight, start_state):
    activated = conv_act(extended, conv_weight, conv_bias)
    count = activated.shape[0]
    inputs = activated[:, :D_INNER].reshape(count, HEADS, HEAD_DIM)
    b_mat = activated[:, D_INNER:D_INNER + STATE]
    c_mat = activated[:, D_INNER + STATE:]
    deltas = jax.nn.softplus(step_raw + step_bias[None, :])
    heads_out, final_state = group_scan(inputs, b_mat, c_mat, deltas, -jnp.exp(log_rate), start_state)
    heads_out = heads_out + skip_weight[None, :, None] * inputs
    return (heads_out.reshape(count, D_INNER), final_state)

def one_sequence(stream, grad_top, in_weight, out_weight, norm_gain, conv_weight, conv_bias, step_bias, log_rate, skip_weight, gate_gain):
    normed = rms_scale(stream, norm_gain).astype(jnp.bfloat16)
    projected = jnp.dot(normed, in_weight, preferred_element_type=jnp.float32)
    gate_part = projected[:, :D_INNER]
    conv_in = projected[:, D_INNER:D_INNER + CONV_CH].astype(jnp.bfloat16)
    step_raw = projected[:, D_INNER + CONV_CH:]
    extended = jnp.concatenate([jnp.zeros((CONVK - 1, CONV_CH), jnp.float32), conv_in.astype(jnp.float32)], axis=0)
    zero_state = jnp.zeros((HEADS, HEAD_DIM, STATE), jnp.float32)

    def local_mix(extended, step_raw, conv_weight, conv_bias, step_bias, log_rate, skip_weight):
        return mixer(extended, step_raw, conv_weight, conv_bias, step_bias, log_rate, skip_weight, zero_state)[0]
    mixed, mix_back = jax.vjp(local_mix, extended, step_raw, conv_weight, conv_bias, step_bias, log_rate, skip_weight)
    gated = mixed * jax.nn.silu(gate_part)
    gated_norm, gated_back = jax.vjp(rms_scale, gated, gate_gain)
    normed_out = gated_norm.astype(jnp.bfloat16)
    block_out = stream + jnp.dot(normed_out, out_weight, preferred_element_type=jnp.float32)
    top = grad_top.astype(jnp.bfloat16)
    grad_out_weight = jnp.dot(normed_out.T, top, preferred_element_type=jnp.float32)
    grad_normed_out = jnp.dot(top, out_weight.T, preferred_element_type=jnp.float32)
    grad_gated, grad_gate_gain = gated_back(grad_normed_out)
    sigma = jax.nn.sigmoid(gate_part)
    grad_mixed = grad_gated * gate_part * sigma
    grad_gate = grad_gated * mixed * sigma * (1.0 + gate_part * (1.0 - sigma))
    grad_extended, grad_step_raw, grad_conv_w, grad_conv_b, grad_step_bias, grad_log_rate, grad_skip = mix_back(grad_mixed)
    grad_projected = jnp.concatenate([grad_gate, grad_extended[CONVK - 1:], grad_step_raw], axis=1).astype(jnp.bfloat16)
    grad_in_weight = jnp.dot(normed.T, grad_projected, preferred_element_type=jnp.float32)
    grad_normed = jnp.dot(grad_projected, in_weight.T, preferred_element_type=jnp.float32)
    _, norm_back = jax.vjp(rms_scale, stream, norm_gain)
    grad_stream, grad_norm_gain = norm_back(grad_normed)
    grads = (grad_in_weight, grad_out_weight, grad_norm_gain, grad_conv_w, grad_conv_b, grad_step_bias, grad_log_rate, grad_skip, grad_gate_gain)
    return (block_out, grad_top + grad_stream, grads)

def reference(hidden_in, upstream, in_weight, out_weight, norm_gain, conv_weight, conv_bias, step_bias, log_rate, skip_weight, gate_gain):

    def per_sequence(totals, paired):
        stream, grad_top = paired
        block_row, grad_row, grads = one_sequence(stream, grad_top, in_weight, out_weight, norm_gain, conv_weight, conv_bias, step_bias, log_rate, skip_weight, gate_gain)
        return (jax.tree.map(jnp.add, totals, grads), (block_row, grad_row))
    starting = (jnp.zeros((D, PROJ), jnp.float32), jnp.zeros((D_INNER, D), jnp.float32), jnp.zeros((D,), jnp.float32), jnp.zeros((CONVK, CONV_CH), jnp.float32), jnp.zeros((CONV_CH,), jnp.float32), jnp.zeros((HEADS,), jnp.float32), jnp.zeros((HEADS,), jnp.float32), jnp.zeros((HEADS,), jnp.float32), jnp.zeros((D_INNER,), jnp.float32))
    totals, outputs = lax.scan(per_sequence, starting, (hidden_in, upstream))
    block_out, grad_hidden = outputs
    return (block_out, grad_hidden, totals[0], totals[1], totals[2], totals[3], totals[4], totals[5], totals[6], totals[7], totals[8])
```

```python
import jax
import jax.numpy as jnp
from jax import lax
from jax.experimental import pallas as pl
from jax.experimental.pallas import tpu as pltpu
from jax.sharding import PartitionSpec as P

D_INNER = 2048
HEADS = 32
HEAD_DIM = 64
STATE = 128
CONVK = 4
GROUP = 256
CONV_CH = 2304
EPS = 1e-05
PRECISE = lax.Precision.HIGHEST
PAD = 8
PLANE = 4
NEVER = -1e30


def pick(x, index, axis):
    return lax.dynamic_index_in_dim(x, index, axis, keepdims=False)


def put(buffer, piece, index, axis):
    return lax.dynamic_update_index_in_dim(buffer, piece, index, axis)


def swapped(x, bit):
    return lax.ppermute(x, "dp", [(i, i ^ bit) for i in range(lax.axis_size("dp"))])


def column_shift(x, steps):
    size = lax.axis_size("dp")
    return lax.ppermute(x, "dp", [(i, (i + PLANE * steps) % size) for i in range(size)])


def seq_shift(x, steps):
    size = lax.axis_size("seq")
    return lax.ppermute(x, "seq", [(i, (i + steps) % size) for i in range(size)])


def seq_sum(x):
    size = lax.axis_size("seq")
    if size == 2:
        return x + seq_shift(x, 1)
    return lax.psum(x, "seq")


def everywhere_sum(x):
    size = lax.axis_size("dp")
    if size & (size - 1) or lax.axis_size("seq") != 2:
        return lax.psum(x, ("dp", "seq"))
    x = seq_sum(x)
    bit = 1
    while bit < size:
        x = x + swapped(x, bit)
        bit *= 2
    return x


def gathered(block, first):
    at = lax.axis_index("dp")
    tall, flat = at // PLANE, at % PLANE
    height = lax.axis_size("dp") // PLANE
    column = jnp.zeros((height,) + block.shape, block.dtype)
    column = put(column, block, tall, 0)
    for steps in range(1, height):
        column = put(column, column_shift(block, steps), (tall - steps) % height, 0)
    second = 3 - first
    one = swapped(column, first)
    two = swapped(column, second)
    three = swapped(one, second)
    plane = jnp.zeros((height, PLANE) + block.shape, block.dtype)
    for bit, piece in ((0, column), (first, one), (second, two), (3, three)):
        plane = put(plane, piece, flat ^ bit, 1)
    return plane.reshape((height * PLANE,) + block.shape)


def scattered(blocks, first):
    at = lax.axis_index("dp")
    tall, flat = at // PLANE, at % PLANE
    size = lax.axis_size("dp")
    height = size // PLANE
    shape = blocks.shape[1:]
    kind = blocks.dtype
    plane = blocks.reshape((height, PLANE) + shape)
    second = 3 - first
    own, one, two, three = (pick(plane, flat ^ bit, 1) for bit in (0, first, second, 3))
    near = swapped(three, second)
    mine = swapped(two, second)
    one = (one.astype(jnp.float32) + near.astype(jnp.float32)).astype(kind)
    other = swapped(one, first)
    column = own.astype(jnp.float32) + mine.astype(jnp.float32) + other.astype(jnp.float32)
    sent = column.astype(kind)
    total = pick(column, tall, 0)
    for steps in range(1, height):
        total = total + column_shift(pick(sent, (tall + steps) % height, 0), steps).astype(jnp.float32)
    return total


def dot(a, b, over):
    return lax.dot_general(a, b, ((over[0], over[1]), ((), ())), preferred_element_type=jnp.float32)


def spread(columns, width):
    lane = lax.broadcasted_iota(jnp.int32, (1, width), 1)
    out = columns[:, 0:1]
    for head in range(1, width // HEAD_DIM):
        out = jnp.where(lane >= head * HEAD_DIM, columns[:, head : head + 1], out)
    return jnp.broadcast_to(out, (columns.shape[0], width))


def conv_pre(padded_ref, weight, bias, count):
    summed = bias
    for offset in range(CONVK):
        start = PAD - (CONVK - 1) + offset
        summed = summed + weight[offset : offset + 1] * padded_ref[start : start + count, :]
    return summed


def sigmoid(v):
    return 1.0 / (1.0 + jnp.exp(-v))


def causal_mask():
    return lax.broadcasted_iota(jnp.int32, (GROUP, GROUP), 0) >= lax.broadcasted_iota(
        jnp.int32, (GROUP, GROUP), 1
    )


def scan_forward(x_ref, bc_ref, delta_ref, cum_ref, cum_t_ref, par_ref, mixed_ref, state_ref, pad_ref):
    count, width = x_ref.shape
    bf = jnp.bfloat16
    pad_ref[0:PAD, :] = jnp.zeros((PAD, width), jnp.float32)
    pad_ref[PAD : PAD + count, :] = x_ref[...].astype(bf).astype(jnp.float32)
    pre = conv_pre(pad_ref, par_ref[0:4, :], par_ref[4:5, :], count)
    acts = pre * sigmoid(pre)
    skip = par_ref[5:6, :]
    causal = causal_mask()
    lane = lax.broadcasted_iota(jnp.int32, (1, 2 * HEAD_DIM), 1)
    state = jnp.zeros((STATE, width), jnp.float32)
    for group in range(count // GROUP):
        rows = slice(group * GROUP, (group + 1) * GROUP)
        state_ref[group] = state
        b_mat = bc_ref[rows, 0:STATE].astype(bf)
        c_mat = bc_ref[rows, STATE : 2 * STATE].astype(bf)
        inner = dot(c_mat, b_mat, ((1,), (1,)))
        x = acts[rows]
        cum = cum_ref[0, rows, :]
        cum_wide = spread(cum, width)
        last = cum_wide[GROUP - 1 : GROUP, :]
        xd = x * spread(delta_ref[0, rows, :], width)
        xdb = xd.astype(bf)
        y = dot(c_mat, state.astype(bf), ((1,), (0,))) * jnp.exp(cum_wide) + skip * x
        intra = []
        for pair in range(width // (2 * HEAD_DIM)):
            lanes = slice(pair * 2 * HEAD_DIM, (pair + 1) * 2 * HEAD_DIM)
            halves = []
            for head in (2 * pair, 2 * pair + 1):
                gap = jnp.where(causal, cum[:, head : head + 1] - cum_t_ref[0, head : head + 1, rows], NEVER)
                halves.append(dot((inner * jnp.exp(gap)).astype(bf), xdb[:, lanes], ((1,), (0,))))
            intra.append(jnp.where(lane < HEAD_DIM, halves[0], halves[1]))
        mixed_ref[rows, :] = y + jnp.concatenate(intra, axis=1)
        tail = (xd * jnp.exp(last - cum_wide)).astype(bf)
        state = state * jnp.exp(last) + dot(b_mat, tail, ((0,), (0,)))


def scan_backward(
    x_ref, bc_ref, delta_ref, cum_ref, cum_t_ref, par_ref, mixed_ref, state_ref, grad_ref,
    gx_ref, gbc_ref, gcum_ref, gdelta_ref, gpar_ref, pad_ref, gpad_ref,
):
    count, width = x_ref.shape
    bf = jnp.bfloat16
    heads = width // HEAD_DIM
    pad_ref[0:PAD, :] = jnp.zeros((PAD, width), jnp.float32)
    pad_ref[PAD : PAD + count, :] = x_ref[...].astype(bf).astype(jnp.float32)
    pre = conv_pre(pad_ref, par_ref[0:4, :], par_ref[4:5, :], count)
    sig = sigmoid(pre)
    acts = pre * sig
    slope = sig * (1.0 + pre * (1.0 - sig))
    skip = par_ref[5:6, :]
    causal = causal_mask()
    lane = lax.broadcasted_iota(jnp.int32, (1, 2 * HEAD_DIM), 1)
    lane_wide = lax.broadcasted_iota(jnp.int32, (1, width), 1) // HEAD_DIM
    grad_state = jnp.zeros((STATE, width), jnp.float32)
    gskip = jnp.zeros((1, width), jnp.float32)

    @pl.when(pl.program_id(0) == 0)
    def _():
        gbc_ref[...] = jnp.zeros(gbc_ref.shape, jnp.float32)

    gpad_ref[count : count + PAD, :] = jnp.zeros((PAD, width), jnp.float32)
    for group in reversed(range(count // GROUP)):
        rows = slice(group * GROUP, (group + 1) * GROUP)
        b_mat = bc_ref[rows, 0:STATE].astype(bf)
        c_mat = bc_ref[rows, STATE : 2 * STATE].astype(bf)
        inner = dot(c_mat, b_mat, ((1,), (1,)))
        x = acts[rows]
        gy = grad_ref[rows, :]
        gyb = gy.astype(bf)
        cum = cum_ref[0, rows, :]
        cum_wide = spread(cum, width)
        last = cum_wide[GROUP - 1 : GROUP, :]
        decay = jnp.exp(last)
        delta = spread(delta_ref[0, rows, :], width)
        xd = x * delta
        xdb = xd.astype(bf)
        tail = jnp.exp(last - cum_wide)
        state = state_ref[group]
        y = mixed_ref[rows, :] - skip * x
        gye = (gy * jnp.exp(cum_wide)).astype(bf)
        gc = dot(gye, state.astype(bf), ((1,), (1,)))
        gsb = grad_state.astype(bf)
        gxd_tail = dot(b_mat, gsb, ((1,), (0,))) * tail
        gb = dot((xd * tail).astype(bf), gsb, ((1,), (1,)))
        xdf = xdb.astype(jnp.float32)
        glast = jnp.sum(xdf * gxd_tail, axis=0, keepdims=True) + decay * jnp.sum(
            grad_state * state, axis=0, keepdims=True
        )
        grad_state = grad_state * decay + dot(c_mat, gye, ((0,), (0,)))
        ginner = jnp.zeros((GROUP, GROUP), jnp.float32)
        intra = []
        for pair in range(width // (2 * HEAD_DIM)):
            lanes = slice(pair * 2 * HEAD_DIM, (pair + 1) * 2 * HEAD_DIM)
            halves = []
            for side in (0, 1):
                head = 2 * pair + side
                gap = jnp.where(causal, cum[:, head : head + 1] - cum_t_ref[0, head : head + 1, rows], NEVER)
                fall = jnp.exp(gap)
                weights = (inner * fall).astype(bf)
                own = (lane < HEAD_DIM) if side == 0 else (lane >= HEAD_DIM)
                gyh = jnp.where(own, gy[:, lanes], 0.0).astype(bf)
                ginner = ginner + dot(gyh, xdb[:, lanes], ((1,), (1,))) * fall
                halves.append(dot(weights, gyb[:, lanes], ((0,), (0,))))
            intra.append(jnp.where(lane < HEAD_DIM, halves[0], halves[1]))
        gxd = jnp.concatenate(intra, axis=1) + gxd_tail
        gib = ginner.astype(bf)
        gbc_ref[rows, 0:STATE] += gb + dot(gib, c_mat, ((0,), (0,)))
        gbc_ref[rows, STATE : 2 * STATE] += gc + dot(gib, b_mat, ((1,), (0,)))
        moved = gyb.astype(jnp.float32) * y - xdf * gxd
        drawn = x * gxd
        at_end = lax.broadcasted_iota(jnp.int32, (GROUP, 1), 0) == GROUP - 1
        cums, deltas = [], []
        for head in range(heads):
            mine = lane_wide == head
            here = jnp.sum(jnp.where(mine, moved, 0.0), axis=1, keepdims=True)
            end = jnp.sum(jnp.where(mine, glast, 0.0), axis=1, keepdims=True)
            cums.append(here + jnp.where(at_end, end, 0.0))
            deltas.append(jnp.sum(jnp.where(mine, drawn, 0.0), axis=1, keepdims=True))
        for head in range(heads):
            gcum_ref[0, rows, head : head + 1] = cums[head]
            gdelta_ref[0, rows, head : head + 1] = deltas[head]
        gskip = gskip + jnp.sum(gy * x, axis=0, keepdims=True)
        gpad_ref[rows, :] = (gxd * delta + skip * gy) * slope[rows]
    gpre = gpad_ref[0:count, :]
    total = jnp.zeros((count, width), jnp.float32)
    for offset in range(CONVK):
        ahead = CONVK - 1 - offset
        total = total + par_ref[offset : offset + 1, :] * gpad_ref[ahead : ahead + count, :]
        start = PAD - ahead
        gpar_ref[offset : offset + 1, :] = jnp.sum(
            gpre * pad_ref[start : start + count, :], axis=0, keepdims=True
        )
    gx_ref[...] = total.astype(gx_ref.dtype)
    gpar_ref[4:5, :] = jnp.sum(gpre, axis=0, keepdims=True)
    gpar_ref[5:6, :] = gskip
    gpar_ref[6:8, :] = jnp.zeros((2, width), jnp.float32)


def head_block(heads):
    return 4 if heads % 4 == 0 else 2


def scan_specs(count, width, at):
    block = width // HEAD_DIM
    return [
        pl.BlockSpec((count, width), lambda i: (0, i + at)),
        pl.BlockSpec((count, 2 * STATE), lambda i: (0, 0)),
        pl.BlockSpec((1, count, block), lambda i: (i, 0, 0)),
        pl.BlockSpec((1, count, block), lambda i: (i, 0, 0)),
        pl.BlockSpec((1, block, count), lambda i: (i, 0, 0)),
        pl.BlockSpec((8, width), lambda i: (0, i)),
    ]


def by_block(values, block):
    count, heads = values.shape
    return values.reshape(count, heads // block, block).transpose(1, 0, 2)


def mix_forward(x, at, heads, bc, delta, cum, params):
    count = x.shape[0]
    block = head_block(heads)
    width = block * HEAD_DIM
    groups = count // GROUP
    return pl.pallas_call(
        scan_forward,
        grid=(heads // block,),
        in_specs=scan_specs(count, width, at // width),
        out_specs=[
            pl.BlockSpec((count, width), lambda i: (0, i)),
            pl.BlockSpec((groups, STATE, width), lambda i: (0, 0, i)),
        ],
        out_shape=[
            jax.ShapeDtypeStruct((count, heads * HEAD_DIM), jnp.float32),
            jax.ShapeDtypeStruct((groups, STATE, heads * HEAD_DIM), jnp.float32),
        ],
        scratch_shapes=[pltpu.VMEM((count + PAD, width), jnp.float32)],
        name="scan_forward",
    )(x, bc, by_block(delta, block), by_block(cum, block), by_block(cum, block).transpose(0, 2, 1), params)


def mix_backward(x, at, heads, bc, delta, cum, params, mixed, states, grad):
    count = x.shape[0]
    block = head_block(heads)
    width = block * HEAD_DIM
    groups = count // GROUP
    wide = pl.BlockSpec((count, width), lambda i: (0, i))
    thin = pl.BlockSpec((1, count, block), lambda i: (i, 0, 0))
    gx, gbc, gcum, gdelta, gpar = pl.pallas_call(
        scan_backward,
        grid=(heads // block,),
        in_specs=scan_specs(count, width, at // width)
        + [wide, pl.BlockSpec((groups, STATE, width), lambda i: (0, 0, i)), wide],
        out_specs=[
            wide,
            pl.BlockSpec((count, 2 * STATE), lambda i: (0, 0)),
            thin,
            thin,
            pl.BlockSpec((8, width), lambda i: (0, i)),
        ],
        out_shape=[
            jax.ShapeDtypeStruct((count, heads * HEAD_DIM), jnp.bfloat16),
            jax.ShapeDtypeStruct((count, 2 * STATE), jnp.float32),
            jax.ShapeDtypeStruct((heads // block, count, block), jnp.float32),
            jax.ShapeDtypeStruct((heads // block, count, block), jnp.float32),
            jax.ShapeDtypeStruct((8, heads * HEAD_DIM), jnp.float32),
        ],
        scratch_shapes=[
            pltpu.VMEM((count + PAD, width), jnp.float32),
            pltpu.VMEM((count + PAD, width), jnp.float32),
        ],
        name="scan_backward",
    )(
        x, bc, by_block(delta, block), by_block(cum, block), by_block(cum, block).transpose(0, 2, 1),
        params, mixed, states, grad,
    )
    back = lambda v: v.transpose(1, 0, 2).reshape(count, heads)
    return gx, gbc, back(gcum), back(gdelta), gpar


def rms_scale(values, gain):
    return values * lax.rsqrt(jnp.mean(values * values, axis=-1, keepdims=True) + EPS) * gain


def conv_act(values, conv_weight, conv_bias):
    count = values.shape[0]
    extended = jnp.concatenate([jnp.zeros((CONVK - 1, values.shape[1]), jnp.float32), values], axis=0)
    summed = conv_bias[None, :] + conv_weight[0][None, :] * extended[0:count]
    for offset in range(1, CONVK):
        summed = summed + conv_weight[offset][None, :] * extended[offset : offset + count]
    return jax.nn.silu(summed)


class Split:
    def __init__(self, out_rows):
        self.peers = lax.axis_size("seq")
        self.at = lax.axis_index("seq")
        blocks = lax.axis_size("dp")
        self.staged = out_rows % HEAD_DIM == 0 and blocks % PLANE == 0
        self.outer = blocks if self.staged else 1

    def view(self, v):
        return v.reshape(v.shape[:-1] + (self.outer, self.peers, v.shape[-1] // (self.outer * self.peers)))

    def own(self, v, at=None):
        part = pick(self.view(v), self.at if at is None else at, v.ndim)
        return part.reshape(v.shape[:-1] + (-1,))

    def place(self, whole, part, at=None):
        view = self.view(whole)
        piece = part.reshape(view.shape[:-2] + view.shape[-1:])
        return put(view, piece, self.at if at is None else at, whole.ndim).reshape(whole.shape)

    def placed(self, part):
        return self.place(jnp.zeros(part.shape[:-1] + (part.shape[-1] * self.peers,), part.dtype), part)

    def exchange(self, piece_for):
        pieces = [(self.at, piece_for(self.at))]
        for steps in range(1, self.peers):
            sent = piece_for((self.at + steps) % self.peers)
            pieces.append(((self.at - steps) % self.peers, seq_shift(sent, steps)))
        return pieces

    def scatter_rows(self, x):
        rows = x.reshape((self.peers, x.shape[0] // self.peers) + x.shape[1:])
        total = 0.0
        for _, piece in self.exchange(lambda to: pick(rows, to, 0)):
            total = total + piece
        return total


def per_device(
    hidden_in, upstream, in_weight, out_weight, norm_gain, conv_weight, conv_bias,
    step_bias, log_rate, skip_weight, gate_gain,
):
    bf = jnp.bfloat16
    split = Split(out_weight.shape[0])
    peers, at = split.peers, split.at
    stream, grad_top = hidden_in[0], upstream[0]
    own_rows, d_model = stream.shape
    count = own_rows * peers
    groups = count // GROUP
    heads = HEADS // peers
    inner = D_INNER // peers
    half_heads = heads // 2
    half = inner // 2
    bc_at = 2 * half
    step_at = bc_at + 2 * STATE
    lanes = -(-heads // 128) * 128

    def in_columns(rows, to):
        x = split.own(rows[:, D_INNER : 2 * D_INNER], to)
        gate = split.own(rows[:, :D_INNER], to)
        bc = rows[:, 2 * D_INNER : D_INNER + CONV_CH]
        steps = split.own(rows[:, D_INNER + CONV_CH :], to)
        blank = jnp.zeros((rows.shape[0], lanes - heads), rows.dtype)
        return jnp.concatenate(
            [x[:, :half], gate[:, :half], bc, steps, blank, x[:, half:], gate[:, half:]], axis=1
        )

    first_width = step_at + lanes
    if split.staged:
        parts = split.exchange(lambda to: in_columns(in_weight, to))
        block = jnp.zeros((peers,) + parts[0][1].shape, bf)
        for origin, part in parts:
            block = put(block, part, origin, 0)
        block = block.reshape(-1, block.shape[-1])
        in_first = gathered(block[:, :first_width], 1).reshape(d_model, -1)
        in_second = gathered(block[:, first_width:], 2).reshape(d_model, -1)
        out_full = gathered(out_weight, 1).reshape(inner, d_model)
    else:
        in_all = lax.all_gather(in_weight, ("dp", "seq"), axis=0, tiled=True)
        in_all = in_columns(in_all, at)
        in_first, in_second = in_all[:, :first_width], in_all[:, first_width:]
        out_full = split.own(lax.all_gather(out_weight, ("dp", "seq"), axis=0, tiled=True).T).T

    normed_own = rms_scale(stream, norm_gain).astype(bf)
    both = jnp.concatenate([normed_own, grad_top.astype(bf)], axis=1)
    tokens = jnp.zeros((peers,) + both.shape, bf)
    for origin, part in split.exchange(lambda to: both):
        tokens = put(tokens, part, origin, 0)
    tokens = tokens.reshape(count, -1)
    normed, top = tokens[:, :d_model], tokens[:, d_model:]

    own_bias = split.own(step_bias)
    rates = -jnp.exp(split.own(log_rate))
    own_gain = split.own(gate_gain)
    conv_x = split.own(conv_weight[:, :D_INNER])
    params = jnp.concatenate(
        [
            conv_x,
            split.own(conv_bias[:D_INNER])[None],
            jnp.repeat(split.own(skip_weight), HEAD_DIM)[None],
            jnp.zeros((2, inner), jnp.float32),
        ],
        axis=0,
    )
    tri = (jnp.arange(GROUP)[:, None] >= jnp.arange(GROUP)[None, :]).astype(jnp.float32)

    first = dot(normed, in_first, ((1,), (0,)))
    step_raw = first[:, step_at : step_at + heads]
    deltas = jax.nn.softplus(step_raw + own_bias[None, :])
    cum = jnp.einsum(
        "ts,gsh->gth", tri, (deltas * rates[None, :]).reshape(groups, GROUP, heads), precision=PRECISE
    ).reshape(count, heads)
    bc_in = first[:, bc_at:step_at].astype(bf).astype(jnp.float32)
    bc, bc_back = jax.vjp(conv_act, bc_in, conv_weight[:, D_INNER:], conv_bias[D_INNER:])

    def forward(projected, part):
        span = slice(part * half_heads, (part + 1) * half_heads)
        return mix_forward(
            projected, 0, half_heads, bc, deltas[:, span], cum[:, span], params[:, part * half : (part + 1) * half]
        )

    grad_normed_out = dot(top, out_full, ((1,), (1,)))
    mixes, gates, gateds, states = [], [], [], []
    squares, pulls = 0.0, 0.0
    projections = []
    for part, weight in enumerate((in_first, in_second)):
        projected = first if part == 0 else dot(normed, weight, ((1,), (0,)))
        mixed, state = forward(projected, part)
        gate = projected[:, half : 2 * half]
        gated = mixed * jax.nn.silu(gate)
        cols = slice(part * half, (part + 1) * half)
        squares = squares + jnp.sum(gated * gated, axis=1)
        pulls = pulls + jnp.sum(grad_normed_out[:, cols] * own_gain[None, cols] * gated, axis=1)
        projections.append(projected)
        mixes.append(mixed)
        gates.append(gate)
        gateds.append(gated)
        states.append(state)
    sums = seq_sum(jnp.stack([squares, pulls]))
    scale = lax.rsqrt(sums[0] / D_INNER + EPS)[:, None]
    lean = sums[1][:, None] * scale * scale * scale / D_INNER

    normed_out = jnp.concatenate(
        [
            (gateds[part] * scale * own_gain[None, part * half : (part + 1) * half]).astype(bf)
            for part in (0, 1)
        ],
        axis=1,
    )
    grad_out = dot(normed_out, top, ((0,), (0,)))
    block_part = dot(normed_out, out_full, ((1,), (0,)))
    block_out = stream + split.scatter_rows(block_part)

    grad_ins = [None, None]
    grad_cums, grad_deltas, grad_pars, gain_parts = [None, None], [None, None], [None, None], [None, None]
    grad_bc = 0.0
    grad_normed = 0.0
    for part in (1, 0):
        cols = slice(part * half, (part + 1) * half)
        span = slice(part * half_heads, (part + 1) * half_heads)
        gate, mixed, gated = gates[part], mixes[part], gateds[part]
        pulled = grad_normed_out[:, cols]
        gain_parts[part] = jnp.sum(pulled * gated * scale, axis=0)
        grad_gated = pulled * own_gain[None, cols] * scale - gated * lean
        sigma = jax.nn.sigmoid(gate)
        grad_mixed = grad_gated * gate * sigma
        grad_gate = (grad_gated * mixed * sigma * (1.0 + gate * (1.0 - sigma))).astype(bf)
        gx, gbc, grad_cums[part], grad_deltas[part], grad_pars[part] = mix_backward(
            projections[part], 0, half_heads, bc, deltas[:, span], cum[:, span], params[:, cols],
            mixed, states[part], grad_mixed,
        )
        grad_bc = grad_bc + gbc
        pieces = [gx, grad_gate]
        if part == 0:
            grad_bc_in, grad_bc_w, grad_bc_b = bc_back(grad_bc)
            grad_rate = jnp.einsum(
                "ts,gth->gsh",
                tri,
                jnp.concatenate(grad_cums, axis=1).reshape(groups, GROUP, heads),
                precision=PRECISE,
            ).reshape(count, heads)
            grad_step = (grad_rate * rates[None, :] + jnp.concatenate(grad_deltas, axis=1)) * jax.nn.sigmoid(
                step_raw + own_bias[None, :]
            )
            pieces += [
                grad_bc_in.astype(bf),
                grad_step.astype(bf),
                jnp.zeros((count, lanes - heads), bf),
            ]
        grad_projected = jnp.concatenate(pieces, axis=1)
        grad_ins[part] = dot(normed, grad_projected, ((0,), (0,)))
        grad_normed = grad_normed + dot(grad_projected, (in_first, in_second)[part], ((1,), (1,)))

    grad_par = jnp.concatenate(grad_pars, axis=1)
    small = [
        jnp.concatenate([split.placed(grad_par[:CONVK]), grad_bc_w], axis=1),
        jnp.concatenate([split.placed(grad_par[CONVK]), grad_bc_b]),
        split.placed(jnp.sum(grad_step, axis=0)),
        split.placed(jnp.sum(grad_rate * deltas, axis=0) * rates),
        split.placed(jnp.sum(grad_par[CONVK + 1].reshape(heads, HEAD_DIM), axis=1)),
        split.placed(jnp.concatenate(gain_parts)),
    ]
    packed = everywhere_sum(jnp.concatenate([v.reshape(-1) for v in small]))
    summed, offset = [], 0
    for v in small:
        summed.append(packed[offset : offset + v.size].reshape(v.shape))
        offset += v.size

    if split.staged:
        blocks = lax.axis_size("dp")
        out_share = scattered(grad_out.astype(bf).reshape(blocks, -1, d_model), 1)
        second = scattered(grad_ins[1].astype(bf).reshape(blocks, -1, 2 * half), 2)
        firsts = scattered(grad_ins[0].astype(bf).reshape(blocks, -1, first_width), 1)
        rows = jnp.concatenate([firsts, second], axis=1).reshape(peers, -1, first_width + 2 * half)
        shares = split.exchange(lambda to: pick(rows, to, 0))
        at_rows = rows.shape[1]
    else:
        shares = [(at, jnp.concatenate(grad_ins, axis=1))]
        at_rows = d_model
        out_share = lax.psum_scatter(
            split.placed(grad_out.T).T, ("dp", "seq"), scatter_dimension=0, tiled=True
        )
    x_cols = jnp.zeros((at_rows, D_INNER), jnp.float32)
    gate_cols, bc_cols, step_cols = x_cols, 0.0, jnp.zeros((at_rows, HEADS), jnp.float32)
    for origin, part in shares:
        low, high = part[:, :first_width], part[:, first_width:]
        x_cols = split.place(x_cols, jnp.concatenate([low[:, :half], high[:, :half]], axis=1), origin)
        gate_cols = split.place(gate_cols, jnp.concatenate([low[:, half : 2 * half], high[:, half:]], axis=1), origin)
        bc_cols = bc_cols + low[:, bc_at:step_at]
        step_cols = split.place(step_cols, low[:, step_at : step_at + heads], origin)
    in_share = jnp.concatenate([gate_cols, x_cols, bc_cols, step_cols], axis=1)
    if not split.staged:
        in_share = lax.psum_scatter(in_share, ("dp", "seq"), scatter_dimension=0, tiled=True)

    _, norm_back = jax.vjp(rms_scale, stream, norm_gain)
    grad_stream, grad_norm_gain = norm_back(split.scatter_rows(grad_normed))
    grad_norm_gain = everywhere_sum(grad_norm_gain)
    return (
        block_out[None], (grad_top + grad_stream)[None], in_share, out_share, grad_norm_gain,
        summed[0], summed[1], summed[2], summed[3], summed[4], summed[5],
    )


def solution(mesh):
    tokens, rows, whole = P("dp", "seq", None), P(("dp", "seq"), None), P()
    return jax.shard_map(
        per_device,
        mesh=mesh,
        in_specs=(tokens, tokens, rows, rows) + (whole,) * 7,
        out_specs=(tokens, tokens, rows, rows) + (whole,) * 7,
        check_vma=False,
    )
```

```python
import functools

import jax
import jax.numpy as jnp
from jax import lax
from jax.experimental import pallas as pl
from jax.experimental.pallas import tpu as pltpu
from jax.sharding import PartitionSpec as P

D_INNER = 2048
HEADS = 32
HEAD_DIM = 64
STATE = 128
CONVK = 4
GROUP = 256
CONV_CH = 2304
EPS = 1e-05
PRECISE = lax.Precision.HIGHEST
PAD = 8
PLANE = 4
NEVER = -1e30


def pick(x, index, axis):
    return lax.dynamic_index_in_dim(x, index, axis, keepdims=False)


def put(buffer, piece, index, axis):
    return lax.dynamic_update_index_in_dim(buffer, piece, index, axis)


def swapped(x, bit):
    return lax.ppermute(x, "dp", [(i, i ^ bit) for i in range(lax.axis_size("dp"))])


def column_shift(x, steps):
    size = lax.axis_size("dp")
    return lax.ppermute(x, "dp", [(i, (i + PLANE * steps) % size) for i in range(size)])


def seq_shift(x, steps):
    size = lax.axis_size("seq")
    return lax.ppermute(x, "seq", [(i, (i + steps) % size) for i in range(size)])


def seq_sum(x):
    size = lax.axis_size("seq")
    if size == 2:
        return x + seq_shift(x, 1)
    return lax.psum(x, "seq")


def everywhere_sum(x):
    size = lax.axis_size("dp")
    if size & (size - 1) or lax.axis_size("seq") != 2:
        return lax.psum(x, ("dp", "seq"))
    x = seq_sum(x)
    bit = 1
    while bit < size:
        x = x + swapped(x, bit)
        bit *= 2
    return x


def joined(pieces):
    (at, piece), (other, arrived) = pieces
    pair = jnp.zeros(piece.shape[:1] + (2,) + piece.shape[1:], piece.dtype)
    return put(put(pair, piece, at, 1), arrived, other, 1)


def gathered(block, cut):
    at = lax.axis_index("dp")
    tall, y, x = at // PLANE, at % PLANE // 2, at % 2
    height = lax.axis_size("dp") // PLANE
    column = jnp.zeros((height,) + block.shape, block.dtype)
    column = put(column, block, tall, 0)
    moved = [column_shift(block, steps) for steps in range(1, height)]
    for steps, piece in enumerate(moved, 1):
        column = put(column, piece, (tall - steps) % height, 0)
    left, right = column[..., :cut], column[..., cut:]
    left_near, right_near = swapped(left, 1), swapped(right, 2)
    left, right = joined(((x, left), (1 - x, left_near))), joined(((y, right), (1 - y, right_near)))
    left_far, right_far = swapped(left, 2), swapped(right, 1)
    left = joined(((y, left), (1 - y, left_far)))
    full = jnp.zeros((height, 2, 2) + right.shape[2:], right.dtype)
    right = put(put(full, right, x, 2), right_far, 1 - x, 2)
    return left.reshape(-1, cut), right.reshape(-1, block.shape[-1] - cut)


def scattered(left, right):
    at = lax.axis_index("dp")
    tall, y, x = at // PLANE, at % PLANE // 2, at % 2
    height = lax.axis_size("dp") // PLANE
    kind = left.dtype
    wide = jnp.float32
    left = left.reshape(height, 2, 2, -1, left.shape[-1])
    right = right.reshape(height, 2, 2, -1, right.shape[-1])
    left_far, right_far = swapped(pick(left, 1 - y, 1), 2), swapped(pick(right, 1 - x, 2), 1)
    left = pick(left, y, 1).astype(wide) + left_far.astype(wide)
    right = pick(right, x, 2).astype(wide) + right_far.astype(wide)
    left_near = swapped(pick(left, 1 - x, 1).astype(kind), 1)
    right_near = swapped(pick(right, 1 - y, 1).astype(kind), 2)
    left = pick(left, x, 1) + left_near.astype(wide)
    right = pick(right, y, 1) + right_near.astype(wide)
    column = jnp.concatenate([left, right], axis=-1)
    sent = column.astype(kind)
    moved = [column_shift(pick(sent, (tall + k) % height, 0), k) for k in range(1, height)]
    total = pick(column, tall, 0)
    for piece in moved:
        total = total + piece.astype(wide)
    return total


def dot(a, b, over):
    return lax.dot_general(a, b, ((over[0], over[1]), ((), ())), preferred_element_type=jnp.float32)


def spread(columns, width):
    lane = lax.broadcasted_iota(jnp.int32, (1, width), 1)
    out = columns[:, 0:1]
    for head in range(1, width // HEAD_DIM):
        out = jnp.where(lane >= head * HEAD_DIM, columns[:, head : head + 1], out)
    return jnp.broadcast_to(out, (columns.shape[0], width))


def conv_pre(padded_ref, weight, bias, count):
    summed = bias
    for offset in range(CONVK):
        start = PAD - (CONVK - 1) + offset
        summed = summed + weight[offset : offset + 1] * padded_ref[start : start + count, :]
    return summed


def sigmoid(v):
    return 1.0 / (1.0 + jnp.exp(-v))


def causal_mask():
    return lax.broadcasted_iota(jnp.int32, (GROUP, GROUP), 0) >= lax.broadcasted_iota(
        jnp.int32, (GROUP, GROUP), 1
    )


def own_lanes(values, lane):
    return pltpu.roll(values, (values.shape[1] - lane) % values.shape[1], 1)


def folded(values):
    total = values[:, :128]
    for at in range(128, values.shape[1], 128):
        total = total + values[:, at : at + 128]
    return total


def scan_forward(
    normed_ref, wx_ref, wg_ref, pulled_ref, bc_ref, delta_ref, cum_ref, cum_t_ref, par_ref,
    x_ref, gate_ref, mixed_ref, state_ref, sums_ref, pad_ref, *, lead,
):
    count, width = mixed_ref.shape
    bf = jnp.bfloat16
    at = lead + pl.program_id(0) * (width // HEAD_DIM)
    normed = normed_ref[...]
    conv_in = dot(normed, wx_ref[...], ((1,), (0,))).astype(bf)
    gate = dot(normed, wg_ref[...], ((1,), (0,)))
    x_ref[...] = conv_in
    gate_ref[...] = gate
    pad_ref[0:PAD, :] = jnp.zeros((PAD, width), jnp.float32)
    pad_ref[PAD : PAD + count, :] = conv_in.astype(jnp.float32)
    pre = conv_pre(pad_ref, par_ref[0:4, :], par_ref[4:5, :], count)
    acts = pre * sigmoid(pre)
    skip = par_ref[5:6, :]
    causal = causal_mask()
    lane = lax.broadcasted_iota(jnp.int32, (1, 2 * HEAD_DIM), 1)
    state = jnp.zeros((STATE, width), jnp.float32)

    @pl.when(pl.program_id(0) == 0)
    def _():
        sums_ref[...] = jnp.zeros(sums_ref.shape, jnp.float32)

    for group in range(count // GROUP):
        rows = slice(group * GROUP, (group + 1) * GROUP)
        state_ref[group] = state
        b_mat = bc_ref[rows, 0:STATE].astype(bf)
        c_mat = bc_ref[rows, STATE : 2 * STATE].astype(bf)
        inner = dot(c_mat, b_mat, ((1,), (1,)))
        x = acts[rows]
        cum = own_lanes(cum_ref[rows, :], at)
        cum_wide = spread(cum, width)
        last = cum_wide[GROUP - 1 : GROUP, :]
        xd = x * spread(own_lanes(delta_ref[rows, :], at), width)
        xdb = xd.astype(bf)
        y = dot(c_mat, state.astype(bf), ((1,), (0,))) * jnp.exp(cum_wide) + skip * x
        intra = []
        for pair in range(width // (2 * HEAD_DIM)):
            lanes = slice(pair * 2 * HEAD_DIM, (pair + 1) * 2 * HEAD_DIM)
            halves = []
            for head in (2 * pair, 2 * pair + 1):
                gap = jnp.where(causal, cum[:, head : head + 1] - cum_t_ref[pl.ds(at + head, 1), rows], NEVER)
                halves.append(dot((inner * jnp.exp(gap)).astype(bf), xdb[:, lanes], ((1,), (0,))))
            intra.append(jnp.where(lane < HEAD_DIM, halves[0], halves[1]))
        mixed = y + jnp.concatenate(intra, axis=1)
        mixed_ref[rows, :] = mixed
        tail = (xd * jnp.exp(last - cum_wide)).astype(bf)
        state = state * jnp.exp(last) + dot(b_mat, tail, ((0,), (0,)))
        part = gate[rows]
        gated = mixed * part * sigmoid(part)
        sums_ref[rows, 0:128] += folded(gated * gated)
        sums_ref[rows, 128:256] += folded(pulled_ref[rows, :] * par_ref[6:7, :] * gated)


def scan_backward(
    x_ref, gate_ref, mixed_ref, state_ref, pulled_ref, norm_ref, bc_ref, delta_ref, cum_ref, cum_t_ref, par_ref,
    gx_ref, ggate_ref, gbc_ref, gcum_ref, gdelta_ref, gpar_ref, pad_ref, gpad_ref, *, lead,
):
    count, width = x_ref.shape
    bf = jnp.bfloat16
    heads = width // HEAD_DIM
    at = lead + pl.program_id(0) * heads
    pad_ref[0:PAD, :] = jnp.zeros((PAD, width), jnp.float32)
    pad_ref[PAD : PAD + count, :] = x_ref[...].astype(jnp.float32)
    pre = conv_pre(pad_ref, par_ref[0:4, :], par_ref[4:5, :], count)
    sig = sigmoid(pre)
    acts = pre * sig
    slope = sig * (1.0 + pre * (1.0 - sig))
    skip = par_ref[5:6, :]
    gain = par_ref[6:7, :]
    causal = causal_mask()
    lane = lax.broadcasted_iota(jnp.int32, (1, 2 * HEAD_DIM), 1)
    lane_wide = lax.broadcasted_iota(jnp.int32, (1, width), 1) // HEAD_DIM
    lane_all = lax.broadcasted_iota(jnp.int32, (1, 128), 1)
    grad_state = jnp.zeros((STATE, width), jnp.float32)
    gskip = jnp.zeros((1, width), jnp.float32)
    ggain = jnp.zeros((1, width), jnp.float32)

    @pl.when(pl.program_id(0) == 0)
    def _():
        gbc_ref[...] = jnp.zeros(gbc_ref.shape, jnp.float32)
        gcum_ref[...] = jnp.zeros(gcum_ref.shape, jnp.float32)
        gdelta_ref[...] = jnp.zeros(gdelta_ref.shape, jnp.float32)

    gpad_ref[count : count + PAD, :] = jnp.zeros((PAD, width), jnp.float32)
    for group in reversed(range(count // GROUP)):
        rows = slice(group * GROUP, (group + 1) * GROUP)
        scale, lean = norm_ref[rows, 0:1], norm_ref[rows, 1:2]
        gate, mixed, pulled = gate_ref[rows, :], mixed_ref[rows, :], pulled_ref[rows, :]
        sigma = sigmoid(gate)
        gated = mixed * gate * sigma
        ggain = ggain + jnp.sum(pulled * gated * scale, axis=0, keepdims=True)
        ggated = pulled * gain * scale - gated * lean
        ggate_ref[rows, :] = (ggated * mixed * sigma * (1.0 + gate * (1.0 - sigma))).astype(bf)
        gy = ggated * gate * sigma
        gyb = gy.astype(bf)
        b_mat = bc_ref[rows, 0:STATE].astype(bf)
        c_mat = bc_ref[rows, STATE : 2 * STATE].astype(bf)
        inner = dot(c_mat, b_mat, ((1,), (1,)))
        x = acts[rows]
        cum = own_lanes(cum_ref[rows, :], at)
        cum_wide = spread(cum, width)
        last = cum_wide[GROUP - 1 : GROUP, :]
        decay = jnp.exp(last)
        delta = spread(own_lanes(delta_ref[rows, :], at), width)
        xd = x * delta
        xdb = xd.astype(bf)
        tail = jnp.exp(last - cum_wide)
        state = state_ref[group]
        y = mixed - skip * x
        gye = (gy * jnp.exp(cum_wide)).astype(bf)
        gc = dot(gye, state.astype(bf), ((1,), (1,)))
        gsb = grad_state.astype(bf)
        gxd_tail = dot(b_mat, gsb, ((1,), (0,))) * tail
        gb = dot((xd * tail).astype(bf), gsb, ((1,), (1,)))
        xdf = xdb.astype(jnp.float32)
        glast = jnp.sum(xdf * gxd_tail, axis=0, keepdims=True) + decay * jnp.sum(
            grad_state * state, axis=0, keepdims=True
        )
        grad_state = grad_state * decay + dot(c_mat, gye, ((0,), (0,)))
        ginner = jnp.zeros((GROUP, GROUP), jnp.float32)
        intra = []
        for pair in range(width // (2 * HEAD_DIM)):
            lanes = slice(pair * 2 * HEAD_DIM, (pair + 1) * 2 * HEAD_DIM)
            halves = []
            for side in (0, 1):
                head = 2 * pair + side
                gap = jnp.where(causal, cum[:, head : head + 1] - cum_t_ref[pl.ds(at + head, 1), rows], NEVER)
                fall = jnp.exp(gap)
                weights = (inner * fall).astype(bf)
                own = (lane < HEAD_DIM) if side == 0 else (lane >= HEAD_DIM)
                gyh = jnp.where(own, gy[:, lanes], 0.0).astype(bf)
                ginner = ginner + dot(gyh, xdb[:, lanes], ((1,), (1,))) * fall
                halves.append(dot(weights, gyb[:, lanes], ((0,), (0,))))
            intra.append(jnp.where(lane < HEAD_DIM, halves[0], halves[1]))
        gxd = jnp.concatenate(intra, axis=1) + gxd_tail
        gib = ginner.astype(bf)
        gbc_ref[rows, 0:STATE] += gb + dot(gib, c_mat, ((0,), (0,)))
        gbc_ref[rows, STATE : 2 * STATE] += gc + dot(gib, b_mat, ((1,), (0,)))
        moved = gyb.astype(jnp.float32) * y - xdf * gxd
        drawn = x * gxd
        at_end = lax.broadcasted_iota(jnp.int32, (GROUP, 1), 0) == GROUP - 1
        cums = jnp.zeros((GROUP, 128), jnp.float32)
        draws = jnp.zeros((GROUP, 128), jnp.float32)
        for head in range(heads):
            mine = lane_wide == head
            here = jnp.sum(jnp.where(mine, moved, 0.0), axis=1, keepdims=True)
            end = jnp.sum(jnp.where(mine, glast, 0.0), axis=1, keepdims=True)
            place = lane_all == at + head
            cums = jnp.where(place, here + jnp.where(at_end, end, 0.0), cums)
            draws = jnp.where(place, jnp.sum(jnp.where(mine, drawn, 0.0), axis=1, keepdims=True), draws)
        gcum_ref[rows, :] += cums
        gdelta_ref[rows, :] += draws
        gskip = gskip + jnp.sum(gy * x, axis=0, keepdims=True)
        gpad_ref[rows, :] = (gxd * delta + skip * gy) * slope[rows]
    gpre = gpad_ref[0:count, :]
    total = jnp.zeros((count, width), jnp.float32)
    for offset in range(CONVK):
        ahead = CONVK - 1 - offset
        total = total + par_ref[offset : offset + 1, :] * gpad_ref[ahead : ahead + count, :]
        start = PAD - ahead
        gpar_ref[offset : offset + 1, :] = jnp.sum(
            gpre * pad_ref[start : start + count, :], axis=0, keepdims=True
        )
    gx_ref[...] = total.astype(bf)
    gpar_ref[4:5, :] = jnp.sum(gpre, axis=0, keepdims=True)
    gpar_ref[5:6, :] = gskip
    gpar_ref[6:7, :] = ggain
    gpar_ref[7:8, :] = jnp.zeros((1, width), jnp.float32)


def head_block(heads):
    return 4 if heads % 4 == 0 else 2


def fixed(shape):
    return pl.BlockSpec(shape, lambda i: (0,) * len(shape))


def moving(rows, width, at=0):
    return pl.BlockSpec((rows, width), lambda i: (0, i + at))


def mix_forward(part, heads, normed, w_x, w_gate, pulled, bc, delta, cum, cum_t, params):
    count, d_model = normed.shape
    block = head_block(heads)
    width = block * HEAD_DIM
    lead = heads // block * part
    groups = count // GROUP
    whole = heads * HEAD_DIM
    return pl.pallas_call(
        functools.partial(scan_forward, lead=heads * part),
        grid=(heads // block,),
        in_specs=[
            fixed((count, d_model)),
            moving(d_model, width),
            moving(d_model, width),
            moving(count, width, lead),
            fixed((count, 2 * STATE)),
            fixed((count, 128)),
            fixed((count, 128)),
            fixed((128, count)),
            moving(8, width, lead),
        ],
        out_specs=[
            moving(count, width),
            moving(count, width),
            moving(count, width),
            pl.BlockSpec((groups, STATE, width), lambda i: (0, 0, i)),
            fixed((count, 256)),
        ],
        out_shape=[
            jax.ShapeDtypeStruct((count, whole), jnp.bfloat16),
            jax.ShapeDtypeStruct((count, whole), jnp.float32),
            jax.ShapeDtypeStruct((count, whole), jnp.float32),
            jax.ShapeDtypeStruct((groups, STATE, whole), jnp.float32),
            jax.ShapeDtypeStruct((count, 256), jnp.float32),
        ],
        scratch_shapes=[pltpu.VMEM((count + PAD, width), jnp.float32)],
        name="scan_forward",
    )(normed, w_x, w_gate, pulled, bc, delta, cum, cum_t, params)


def mix_backward(part, heads, x, gate, mixed, states, pulled, norms, bc, delta, cum, cum_t, params):
    count = x.shape[0]
    block = head_block(heads)
    width = block * HEAD_DIM
    lead = heads // block * part
    groups = count // GROUP
    whole = heads * HEAD_DIM
    return pl.pallas_call(
        functools.partial(scan_backward, lead=heads * part),
        grid=(heads // block,),
        in_specs=[
            moving(count, width),
            moving(count, width),
            moving(count, width),
            pl.BlockSpec((groups, STATE, width), lambda i: (0, 0, i)),
            moving(count, width, lead),
            fixed((count, 128)),
            fixed((count, 2 * STATE)),
            fixed((count, 128)),
            fixed((count, 128)),
            fixed((128, count)),
            moving(8, width, lead),
        ],
        out_specs=[
            moving(count, width),
            moving(count, width),
            fixed((count, 2 * STATE)),
            fixed((count, 128)),
            fixed((count, 128)),
            moving(8, width),
        ],
        out_shape=[
            jax.ShapeDtypeStruct((count, whole), jnp.bfloat16),
            jax.ShapeDtypeStruct((count, whole), jnp.bfloat16),
            jax.ShapeDtypeStruct((count, 2 * STATE), jnp.float32),
            jax.ShapeDtypeStruct((count, 128), jnp.float32),
            jax.ShapeDtypeStruct((count, 128), jnp.float32),
            jax.ShapeDtypeStruct((8, whole), jnp.float32),
        ],
        scratch_shapes=[
            pltpu.VMEM((count + PAD, width), jnp.float32),
            pltpu.VMEM((count + PAD, width), jnp.float32),
        ],
        name="scan_backward",
    )(x, gate, mixed, states, pulled, norms, bc, delta, cum, cum_t, params)


def unzip(at_ref, in_ref, own_ref, other_ref, *, chans, half, heads):
    even = at_ref[0] == 0
    lane = lax.broadcasted_iota(jnp.int32, (1, 128), 1)
    step_at, bc_at = 2 * chans + 2 * STATE, 2 * chans
    kind = own_ref.dtype

    def emit(low, high, to):
        own_ref[:, to : to + 128] = jnp.where(even, low, high).astype(kind)
        other_ref[:, to : to + 128] = jnp.where(even, high, low).astype(kind)

    for source, starts in ((chans, (0, 2 * half + 384)), (0, (half + 128, 3 * half + 384))):
        for at in range(0, chans // 2, 128):
            a = in_ref[:, source + 2 * at : source + 2 * at + 128].astype(jnp.float32)
            b = in_ref[:, source + 2 * at + 128 : source + 2 * at + 256].astype(jnp.float32)
            low = jnp.where(lane < HEAD_DIM, a, pltpu.roll(b, HEAD_DIM, 1))
            high = jnp.where(lane < HEAD_DIM, pltpu.roll(a, HEAD_DIM, 1), b)
            emit(low, high, starts[at // half] + at % half)
    steps = in_ref[:, step_at : step_at + heads]
    row = lax.broadcasted_iota(jnp.int32, (heads, 128), 0)
    col = lax.broadcasted_iota(jnp.int32, (heads, 128), 1)
    sides = [
        dot(steps, jnp.where((row == 2 * col + side) & (col < heads // 2), 1.0, 0.0).astype(kind), ((1,), (0,)))
        for side in (0, 1)
    ]
    emit(sides[0], sides[1], half)
    bc = in_ref[:, bc_at:step_at]
    own_ref[:, 2 * half + 128 : 2 * half + 384] = bc
    other_ref[:, 2 * half + 128 : 2 * half + 384] = bc


def zipped(at_ref, own1_ref, other1_ref, own2_ref, other2_ref, out_ref, *, chans, half, heads):
    even = at_ref[0] == 0
    lane = lax.broadcasted_iota(jnp.int32, (1, 128), 1)
    bc_at, step_at = 2 * chans, 2 * chans + 2 * STATE
    for target, lead in ((chans, 0), (0, 1)):
        for at in range(0, chans // 2, 128):
            second = at >= half
            to = at % half + lead * (half if second else half + 128)
            own_ref, other_ref = (own2_ref, other2_ref) if second else (own1_ref, other1_ref)
            own, other = own_ref[:, to : to + 128], other_ref[:, to : to + 128]
            low, high = jnp.where(even, own, other), jnp.where(even, other, own)
            out_ref[:, target + 2 * at : target + 2 * at + 128] = jnp.where(
                lane < HEAD_DIM, low, pltpu.roll(high, HEAD_DIM, 1)
            )
            out_ref[:, target + 2 * at + 128 : target + 2 * at + 256] = jnp.where(
                lane < HEAD_DIM, pltpu.roll(low, HEAD_DIM, 1), high
            )
    cols = slice(2 * half + 128, 2 * half + 384)
    out_ref[:, bc_at:step_at] = own1_ref[:, cols] + other1_ref[:, cols]
    row = lax.broadcasted_iota(jnp.int32, (128, heads), 0)
    col = lax.broadcasted_iota(jnp.int32, (128, heads), 1)
    own, other = own1_ref[:, half : half + 128], other1_ref[:, half : half + 128]
    total = 0.0
    for side, values in ((0, jnp.where(even, own, other)), (1, jnp.where(even, other, own))):
        choice = jnp.where((col == 2 * row + side) & (row < heads // 2), 1.0, 0.0)
        total = total + lax.dot_general(
            values, choice, (((1,), (0,)), ((), ())), precision=PRECISE, preferred_element_type=jnp.float32
        )
    out_ref[:, step_at : step_at + heads] = total


def scalar():
    return pl.BlockSpec(memory_space=pltpu.SMEM)


def full():
    return pl.BlockSpec(memory_space=pltpu.VMEM)


def unzip_columns(at, rows, half):
    shape = jax.ShapeDtypeStruct((rows.shape[0], 4 * half + 384), rows.dtype)
    return pl.pallas_call(
        functools.partial(unzip, chans=D_INNER, half=half, heads=HEADS),
        in_specs=[scalar(), full()],
        out_specs=[full(), full()],
        out_shape=[shape, shape],
        name="unzip_columns",
    )(at.reshape(1), rows)


def zip_columns(at, own1, other1, own2, other2, half):
    return pl.pallas_call(
        functools.partial(zipped, chans=D_INNER, half=half, heads=HEADS),
        in_specs=[scalar()] + [full()] * 4,
        out_specs=full(),
        out_shape=jax.ShapeDtypeStruct((own1.shape[0], D_INNER + CONV_CH + HEADS), jnp.float32),
        name="zip_columns",
    )(at.reshape(1), own1, other1, own2, other2)


def rms_scale(values, gain):
    return values * lax.rsqrt(jnp.mean(values * values, axis=-1, keepdims=True) + EPS) * gain


def conv_act(values, conv_weight, conv_bias):
    count = values.shape[0]
    extended = jnp.concatenate([jnp.zeros((CONVK - 1, values.shape[1]), jnp.float32), values], axis=0)
    summed = conv_bias[None, :] + conv_weight[0][None, :] * extended[0:count]
    for offset in range(1, CONVK):
        summed = summed + conv_weight[offset][None, :] * extended[offset : offset + count]
    return jax.nn.silu(summed)


class Split:
    def __init__(self, out_rows):
        self.peers = lax.axis_size("seq")
        self.at = lax.axis_index("seq")
        blocks = lax.axis_size("dp")
        self.staged = out_rows == HEAD_DIM and blocks % PLANE == 0 and self.peers == 2
        self.outer = blocks if self.staged else 1

    def view(self, v):
        return v.reshape(v.shape[:-1] + (self.outer, self.peers, v.shape[-1] // (self.outer * self.peers)))

    def own(self, v, at=None):
        part = pick(self.view(v), self.at if at is None else at, v.ndim)
        return part.reshape(v.shape[:-1] + (-1,))

    def place(self, whole, part, at=None):
        view = self.view(whole)
        piece = part.reshape(view.shape[:-2] + view.shape[-1:])
        return put(view, piece, self.at if at is None else at, whole.ndim).reshape(whole.shape)

    def placed(self, part):
        return self.place(jnp.zeros(part.shape[:-1] + (part.shape[-1] * self.peers,), part.dtype), part)

    def exchange(self, piece_for):
        pieces = [(self.at, piece_for(self.at))]
        for steps in range(1, self.peers):
            sent = piece_for((self.at + steps) % self.peers)
            pieces.append(((self.at - steps) % self.peers, seq_shift(sent, steps)))
        return pieces

    def scatter_rows(self, x):
        rows = x.reshape((self.peers, x.shape[0] // self.peers) + x.shape[1:])
        total = 0.0
        for _, piece in self.exchange(lambda to: pick(rows, to, 0)):
            total = total + piece
        return total


def per_device(
    hidden_in, upstream, in_weight, out_weight, norm_gain, conv_weight, conv_bias,
    step_bias, log_rate, skip_weight, gate_gain,
):
    bf = jnp.bfloat16
    split = Split(out_weight.shape[0])
    peers, at = split.peers, split.at
    stream, grad_top = hidden_in[0], upstream[0]
    own_rows, d_model = stream.shape
    count = own_rows * peers
    groups = count // GROUP
    heads = HEADS // peers
    inner = D_INNER // peers
    half_heads = heads // 2
    half = inner // 2
    lanes = -(-heads // 128) * 128

    def in_columns(rows):
        x = split.own(rows[:, D_INNER : 2 * D_INNER])
        gate = split.own(rows[:, :D_INNER])
        bc = rows[:, 2 * D_INNER : D_INNER + CONV_CH]
        steps = split.own(rows[:, D_INNER + CONV_CH :])
        blank = jnp.zeros((rows.shape[0], lanes - heads), rows.dtype)
        return (
            jnp.concatenate([x[:, :half], steps, blank], axis=1),
            jnp.concatenate([gate[:, :half], bc], axis=1),
            x[:, half:],
            gate[:, half:],
        )

    first_cut = half + lanes
    first_width = first_cut + half + 2 * STATE
    if split.staged:
        own, other = unzip_columns(at, in_weight, half)
        arrived = seq_shift(other, 1)
        block = put(put(jnp.zeros((peers,) + own.shape, bf), own, at, 0), arrived, 1 - at, 0)
        block = block.reshape(-1, block.shape[-1])

    normed_own = rms_scale(stream, norm_gain).astype(bf)
    both = jnp.concatenate([normed_own, grad_top.astype(bf)], axis=1)
    tokens = jnp.zeros((peers,) + both.shape, bf)
    arrived_tokens = split.exchange(lambda to: both)
    for origin, part in arrived_tokens:
        tokens = put(tokens, part, origin, 0)
    tokens = tokens.reshape(count, -1)
    normed, top = tokens[:, :d_model], tokens[:, d_model:]

    if split.staged:
        out_left, out_right = gathered(out_weight, d_model // 2)
        x_first, gate_first = gathered(block[:, :first_width], first_cut)
        x_second, gate_second = gathered(block[:, first_width:], half)
    else:
        in_all = lax.all_gather(in_weight, ("dp", "seq"), axis=0, tiled=True)
        x_first, gate_first, x_second, gate_second = in_columns(in_all)
        out_all = split.own(lax.all_gather(out_weight, ("dp", "seq"), axis=0, tiled=True).T).T
        out_left, out_right = out_all[:, : d_model // 2], out_all[:, d_model // 2 :]
    top_left, top_right = top[:, : d_model // 2], top[:, d_model // 2 :]

    own_bias = split.own(step_bias)
    rates = -jnp.exp(split.own(log_rate))
    own_gain = split.own(gate_gain)
    conv_x = split.own(conv_weight[:, :D_INNER])
    params = jnp.concatenate(
        [
            conv_x,
            split.own(conv_bias[:D_INNER])[None],
            jnp.repeat(split.own(skip_weight), HEAD_DIM)[None],
            own_gain[None],
            jnp.zeros((1, inner), jnp.float32),
        ],
        axis=0,
    )
    tri = (jnp.arange(GROUP)[:, None] >= jnp.arange(GROUP)[None, :]).astype(jnp.float32)

    step_raw = dot(normed, x_first[:, half:], ((1,), (0,)))
    step_in = step_raw + jnp.pad(own_bias, (0, lanes - heads))[None, :]
    all_rates = jnp.pad(rates, (0, lanes - heads))[None, :]
    deltas = jax.nn.softplus(step_in)
    cum = jnp.einsum(
        "ts,gsh->gth", tri, (deltas * all_rates).reshape(groups, GROUP, lanes), precision=PRECISE
    ).reshape(count, lanes)
    cum_t = cum.T
    bc_in = dot(normed, gate_first[:, half:], ((1,), (0,))).astype(bf).astype(jnp.float32)
    bc, bc_back = jax.vjp(conv_act, bc_in, conv_weight[:, D_INNER:], conv_bias[D_INNER:])

    pulled = dot(top_left, out_left, ((1,), (1,))) + dot(top_right, out_right, ((1,), (1,)))
    saved = []
    for part, (w_x, w_gate) in enumerate(((x_first, gate_first), (x_second, gate_second))):
        saved.append(mix_forward(part, half_heads, normed, w_x, w_gate, pulled, bc, deltas, cum, cum_t, params))
    sums = jnp.sum((saved[0][4] + saved[1][4]).reshape(count, 2, 128), axis=2)
    sums = seq_sum(sums.T)
    scale = lax.rsqrt(sums[0] / D_INNER + EPS)
    lean = sums[1] * scale * scale * scale / D_INNER
    norms = jnp.pad(jnp.stack([scale, lean], axis=1), ((0, 0), (0, 126)))

    normed_out = jnp.concatenate(
        [
            (mixed * jax.nn.silu(gate) * scale[:, None] * own_gain[None, part * half : (part + 1) * half]).astype(bf)
            for part, (_, gate, mixed, _, _) in enumerate(saved)
        ],
        axis=1,
    )
    grad_out = [dot(normed_out, side, ((0,), (0,))).astype(bf) for side in (top_left, top_right)]
    if split.staged:
        out_share = scattered(*grad_out)

    grad_ins = [None, None]
    shares = [None, None]
    grad_cum = grad_delta = grad_bc = grad_normed = 0.0
    grad_pars = [None, None]
    for part in (1, 0):
        gx, ggate, gbc, gcum, gdelta, grad_pars[part] = mix_backward(
            part, half_heads, *saved[part][:4], pulled, norms, bc, deltas, cum, cum_t, params
        )
        grad_bc, grad_cum, grad_delta = grad_bc + gbc, grad_cum + gcum, grad_delta + gdelta
        if part == 0:
            grad_bc_in, grad_bc_w, grad_bc_b = bc_back(grad_bc)
            grad_rate = jnp.einsum(
                "ts,gth->gsh", tri, grad_cum.reshape(groups, GROUP, lanes), precision=PRECISE
            ).reshape(count, lanes)
            grad_step = (grad_rate * all_rates + grad_delta) * jax.nn.sigmoid(step_in)
            gx = jnp.concatenate([gx, grad_step.astype(bf)], axis=1)
            ggate = jnp.concatenate([ggate, grad_bc_in.astype(bf)], axis=1)
        grad_ins[part] = [dot(normed, side, ((0,), (0,))) for side in (gx, ggate)]
        w_x, w_gate = ((x_first, gate_first), (x_second, gate_second))[part]
        if split.staged:
            share = scattered(*(side.astype(bf) for side in grad_ins[part]))
            pair = share.reshape(peers, -1, share.shape[-1])
            shares[part] = (pick(pair, at, 0), seq_shift(pick(pair, 1 - at, 0), 1))
        grad_normed = grad_normed + dot(gx, w_x, ((1,), (1,))) + dot(ggate, w_gate, ((1,), (1,)))
    block_part = jnp.concatenate(
        [dot(normed_out, out_left, ((1,), (0,))), dot(normed_out, out_right, ((1,), (0,)))], axis=1
    )
    block_out = stream + split.scatter_rows(block_part)

    grad_par = jnp.concatenate(grad_pars, axis=1)
    small = [
        jnp.concatenate([split.placed(grad_par[:CONVK]), grad_bc_w], axis=1),
        jnp.concatenate([split.placed(grad_par[CONVK]), grad_bc_b]),
        split.placed(jnp.sum(grad_step, axis=0)[:heads]),
        split.placed(jnp.sum(grad_rate * deltas, axis=0)[:heads] * rates),
        split.placed(jnp.sum(grad_par[CONVK + 1].reshape(heads, HEAD_DIM), axis=1)),
        split.placed(grad_par[CONVK + 2]),
    ]
    packed = everywhere_sum(jnp.concatenate([v.reshape(-1) for v in small]))
    summed, offset = [], 0
    for v in small:
        summed.append(packed[offset : offset + v.size].reshape(v.shape))
        offset += v.size

    if split.staged:
        in_share = zip_columns(at, *shares[0], *shares[1], half)
    else:
        empty = jnp.zeros((d_model, D_INNER), jnp.float32)
        (x_low, gate_low), (x_high, gate_high) = grad_ins
        in_share = jnp.concatenate(
            [
                split.place(empty, jnp.concatenate([gate_low[:, :half], gate_high], axis=1)),
                split.place(empty, jnp.concatenate([x_low[:, :half], x_high], axis=1)),
                gate_low[:, half:],
                split.placed(x_low[:, half : half + heads]),
            ],
            axis=1,
        )
        in_share = lax.psum_scatter(in_share, ("dp", "seq"), scatter_dimension=0, tiled=True)
        grad_out = jnp.concatenate(grad_out, axis=1).astype(jnp.float32)
        out_share = lax.psum_scatter(
            split.placed(grad_out.T).T, ("dp", "seq"), scatter_dimension=0, tiled=True
        )

    _, norm_back = jax.vjp(rms_scale, stream, norm_gain)
    grad_normed = split.scatter_rows(grad_normed)
    grad_stream, grad_norm_gain = norm_back(grad_normed)
    grad_norm_gain = everywhere_sum(grad_norm_gain)
    return (
        block_out[None], (grad_top + grad_stream)[None], in_share, out_share, grad_norm_gain,
        summed[0], summed[1], summed[2], summed[3], summed[4], summed[5],
    )


def solution(mesh):
    tokens, rows, whole = P("dp", "seq", None), P(("dp", "seq"), None), P()
    return jax.shard_map(
        per_device,
        mesh=mesh,
        in_specs=(tokens, tokens, rows, rows) + (whole,) * 7,
        out_specs=(tokens, tokens, rows, rows) + (whole,) * 7,
        check_vma=False,
    )
```

```python
import functools

import jax
import jax.numpy as jnp
from jax import lax
from jax.experimental import pallas as pl
from jax.experimental.pallas import tpu as pltpu
from jax.sharding import PartitionSpec as P


D_INNER = 2048
HEADS = 32
HEAD_DIM = 64
STATE = 128
CONVK = 4
GROUP = 256
CONV_CH = 2304
EPS = 1e-05
PRECISE = lax.Precision.HIGHEST
PAD = 8
PLANE = 4
NEVER = -1e30


def pick(x, index, axis):
    return lax.dynamic_index_in_dim(x, index, axis, keepdims=False)


def put(buffer, piece, index, axis):
    return lax.dynamic_update_index_in_dim(buffer, piece, index, axis)


def swapped(x, bit):
    return lax.ppermute(x, "dp", [(i, i ^ bit) for i in range(lax.axis_size("dp"))])


def column_shift(x, steps):
    size = lax.axis_size("dp")
    return lax.ppermute(x, "dp", [(i, (i + PLANE * steps) % size) for i in range(size)])


def seq_shift(x, steps):
    size = lax.axis_size("seq")
    return lax.ppermute(x, "seq", [(i, (i + steps) % size) for i in range(size)])


def seq_sum(x):
    size = lax.axis_size("seq")
    if size == 2:
        return x + seq_shift(x, 1)
    return lax.psum(x, "seq")


def everywhere_sum(x):
    size = lax.axis_size("dp")
    if size & (size - 1) or lax.axis_size("seq") != 2:
        return lax.psum(x, ("dp", "seq"))
    x = seq_sum(x)
    bit = size // 2
    while bit:
        x = x + swapped(x, bit)
        bit //= 2
    return x


def joined(pieces):
    (at, piece), (other, arrived) = pieces
    pair = jnp.zeros(piece.shape[:1] + (2,) + piece.shape[1:], piece.dtype)
    return put(put(pair, piece, at, 1), arrived, other, 1)


def gathered(block, cut, gate):
    at = lax.axis_index("dp")
    tall, y, x = at // PLANE, at % PLANE // 2, at % 2
    height = lax.axis_size("dp") // PLANE
    column = jnp.zeros((height,) + block.shape, block.dtype)
    column = put(column, block, tall, 0)
    moved = [column_shift(block, steps) for steps in range(1, height)]
    if gate is not None:
        moved, _ = lax.optimization_barrier((moved, gate))
    for steps, piece in enumerate(moved, 1):
        column = put(column, piece, (tall - steps) % height, 0)
    left, right = column[..., :cut], column[..., cut:]
    left_near, right_near = swapped(left, 1), swapped(right, 2)
    later = (left_near, right_near)
    left, right = joined(((x, left), (1 - x, left_near))), joined(((y, right), (1 - y, right_near)))
    left_far, right_far = swapped(left, 2), swapped(right, 1)
    left = joined(((y, left), (1 - y, left_far)))
    full = jnp.zeros((height, 2, 2) + right.shape[2:], right.dtype)
    right = put(put(full, right, x, 2), right_far, 1 - x, 2)
    return left.reshape(-1, cut), right.reshape(-1, block.shape[-1] - cut), later


def scattered(left, right):
    height = lax.axis_size("dp") // PLANE
    kind = left.dtype
    wide = jnp.float32
    left = left.reshape(height, 2, 2, -1, left.shape[-1])
    right = right.reshape(height, 2, 2, -1, right.shape[-1])
    at, left = lax.optimization_barrier((lax.axis_index("dp"), left))
    at_right, right = lax.optimization_barrier((lax.axis_index("dp"), right))
    tall, y, x = at // PLANE, at % PLANE // 2, at % 2
    x_right = at_right % 2
    left_far, right_far = swapped(pick(left, 1 - y, 1), 2), swapped(pick(right, 1 - x_right, 2), 1)
    left = pick(left, y, 1).astype(wide) + left_far.astype(wide)
    right = pick(right, x_right, 2).astype(wide) + right_far.astype(wide)
    left_near = swapped(pick(left, 1 - x, 1).astype(kind), 1)
    right_near = swapped(pick(right, 1 - y, 1).astype(kind), 2)
    left = pick(left, x, 1) + left_near.astype(wide)
    right = pick(right, y, 1) + right_near.astype(wide)
    column = jnp.concatenate([left, right], axis=-1)
    sent = column.astype(kind)
    moved = [column_shift(pick(sent, (tall + k) % height, 0), k) for k in range(1, height)]
    return moved, pick(column, tall, 0), (left_near, right_near)


def arrived_sum(parts, gate):
    moved, total, _ = parts
    if gate is not None:
        moved, _ = lax.optimization_barrier((moved, gate))
    for piece in moved:
        total = total + piece.astype(jnp.float32)
    return total


def dot(a, b, over):
    return lax.dot_general(a, b, ((over[0], over[1]), ((), ())), preferred_element_type=jnp.float32)


def spread(columns, width):
    lane = lax.broadcasted_iota(jnp.int32, (1, width), 1)
    out = columns[:, 0:1]
    for head in range(1, width // HEAD_DIM):
        out = jnp.where(lane >= head * HEAD_DIM, columns[:, head : head + 1], out)
    return jnp.broadcast_to(out, (columns.shape[0], width))


def conv_pre(padded_ref, weight, bias, count):
    summed = bias
    for offset in range(CONVK):
        start = PAD - (CONVK - 1) + offset
        summed = summed + weight[offset : offset + 1] * padded_ref[start : start + count, :]
    return summed


def sigmoid(v):
    return 1.0 / (1.0 + jnp.exp(-v))


def causal_mask():
    return lax.broadcasted_iota(jnp.int32, (GROUP, GROUP), 0) >= lax.broadcasted_iota(
        jnp.int32, (GROUP, GROUP), 1
    )


def own_lanes(values, lane):
    return pltpu.roll(values, (values.shape[1] - lane) % values.shape[1], 1)


def folded(values):
    total = values[:, :128]
    for at in range(128, values.shape[1], 128):
        total = total + values[:, at : at + 128]
    return total


def scan_forward(
    normed_ref, wx_ref, wg_ref, pulled_ref, bc_ref, delta_ref, cum_ref, cum_t_ref, par_ref,
    x_ref, gate_ref, mixed_ref, state_ref, sums_ref, pad_ref, *, lead,
):
    count, width = mixed_ref.shape
    bf = jnp.bfloat16
    at = lead + pl.program_id(0) * (width // HEAD_DIM)
    normed = normed_ref[...]
    conv_in = dot(normed, wx_ref[...], ((1,), (0,))).astype(bf)
    gate = dot(normed, wg_ref[...], ((1,), (0,)))
    x_ref[...] = conv_in
    gate_ref[...] = gate
    pad_ref[0:PAD, :] = jnp.zeros((PAD, width), jnp.float32)
    pad_ref[PAD : PAD + count, :] = conv_in.astype(jnp.float32)
    pre = conv_pre(pad_ref, par_ref[0:4, :], par_ref[4:5, :], count)
    acts = pre * sigmoid(pre)
    skip = par_ref[5:6, :]
    causal = causal_mask()
    lane = lax.broadcasted_iota(jnp.int32, (1, 2 * HEAD_DIM), 1)
    state = jnp.zeros((STATE, width), jnp.float32)

    @pl.when(pl.program_id(0) == 0)
    def _():
        sums_ref[...] = jnp.zeros(sums_ref.shape, jnp.float32)

    for group in range(count // GROUP):
        rows = slice(group * GROUP, (group + 1) * GROUP)
        state_ref[group] = state
        b_mat = bc_ref[rows, 0:STATE].astype(bf)
        c_mat = bc_ref[rows, STATE : 2 * STATE].astype(bf)
        inner = dot(c_mat, b_mat, ((1,), (1,)))
        x = acts[rows]
        cum = own_lanes(cum_ref[rows, :], at)
        cum_wide = spread(cum, width)
        last = cum_wide[GROUP - 1 : GROUP, :]
        xd = x * spread(own_lanes(delta_ref[rows, :], at), width)
        xdb = xd.astype(bf)
        y = dot(c_mat, state.astype(bf), ((1,), (0,))) * jnp.exp(cum_wide) + skip * x
        intra = []
        for pair in range(width // (2 * HEAD_DIM)):
            lanes = slice(pair * 2 * HEAD_DIM, (pair + 1) * 2 * HEAD_DIM)
            halves = []
            for head in (2 * pair, 2 * pair + 1):
                gap = jnp.where(causal, cum[:, head : head + 1] - cum_t_ref[pl.ds(at + head, 1), rows], NEVER)
                halves.append(dot((inner * jnp.exp(gap)).astype(bf), xdb[:, lanes], ((1,), (0,))))
            intra.append(jnp.where(lane < HEAD_DIM, halves[0], halves[1]))
        mixed = y + jnp.concatenate(intra, axis=1)
        mixed_ref[rows, :] = mixed
        tail = (xd * jnp.exp(last - cum_wide)).astype(bf)
        state = state * jnp.exp(last) + dot(b_mat, tail, ((0,), (0,)))
        part = gate[rows]
        gated = mixed * part * sigmoid(part)
        sums_ref[rows, 0:128] += folded(gated * gated)
        sums_ref[rows, 128:256] += folded(pulled_ref[rows, :] * par_ref[6:7, :] * gated)


def scan_backward(
    x_ref, gate_ref, mixed_ref, state_ref, pulled_ref, norm_ref, bc_ref, delta_ref, cum_ref, cum_t_ref, par_ref,
    gx_ref, ggate_ref, gbc_ref, gcum_ref, gdelta_ref, gpar_ref, pad_ref, gpad_ref, *, lead,
):
    count, width = x_ref.shape
    bf = jnp.bfloat16
    heads = width // HEAD_DIM
    at = lead + pl.program_id(0) * heads
    pad_ref[0:PAD, :] = jnp.zeros((PAD, width), jnp.float32)
    pad_ref[PAD : PAD + count, :] = x_ref[...].astype(jnp.float32)
    pre = conv_pre(pad_ref, par_ref[0:4, :], par_ref[4:5, :], count)
    sig = sigmoid(pre)
    acts = pre * sig
    slope = sig * (1.0 + pre * (1.0 - sig))
    skip = par_ref[5:6, :]
    gain = par_ref[6:7, :]
    causal = causal_mask()
    lane = lax.broadcasted_iota(jnp.int32, (1, 2 * HEAD_DIM), 1)
    lane_wide = lax.broadcasted_iota(jnp.int32, (1, width), 1) // HEAD_DIM
    lane_all = lax.broadcasted_iota(jnp.int32, (1, 128), 1)
    grad_state = jnp.zeros((STATE, width), jnp.float32)
    gskip = jnp.zeros((1, width), jnp.float32)
    ggain = jnp.zeros((1, width), jnp.float32)

    @pl.when(pl.program_id(0) == 0)
    def _():
        gbc_ref[...] = jnp.zeros(gbc_ref.shape, jnp.float32)
        gcum_ref[...] = jnp.zeros(gcum_ref.shape, jnp.float32)
        gdelta_ref[...] = jnp.zeros(gdelta_ref.shape, jnp.float32)

    gpad_ref[count : count + PAD, :] = jnp.zeros((PAD, width), jnp.float32)
    for group in reversed(range(count // GROUP)):
        rows = slice(group * GROUP, (group + 1) * GROUP)
        scale, lean = norm_ref[rows, 0:1], norm_ref[rows, 1:2]
        gate, mixed, pulled = gate_ref[rows, :], mixed_ref[rows, :], pulled_ref[rows, :]
        sigma = sigmoid(gate)
        gated = mixed * gate * sigma
        ggain = ggain + jnp.sum(pulled * gated * scale, axis=0, keepdims=True)
        ggated = pulled * gain * scale - gated * lean
        ggate_ref[rows, :] = (ggated * mixed * sigma * (1.0 + gate * (1.0 - sigma))).astype(bf)
        gy = ggated * gate * sigma
        gyb = gy.astype(bf)
        b_mat = bc_ref[rows, 0:STATE].astype(bf)
        c_mat = bc_ref[rows, STATE : 2 * STATE].astype(bf)
        inner = dot(c_mat, b_mat, ((1,), (1,)))
        x = acts[rows]
        cum = own_lanes(cum_ref[rows, :], at)
        cum_wide = spread(cum, width)
        last = cum_wide[GROUP - 1 : GROUP, :]
        decay = jnp.exp(last)
        delta = spread(own_lanes(delta_ref[rows, :], at), width)
        xd = x * delta
        xdb = xd.astype(bf)
        tail = jnp.exp(last - cum_wide)
        state = state_ref[group]
        y = mixed - skip * x
        gye = (gy * jnp.exp(cum_wide)).astype(bf)
        gc = dot(gye, state.astype(bf), ((1,), (1,)))
        gsb = grad_state.astype(bf)
        gxd_tail = dot(b_mat, gsb, ((1,), (0,))) * tail
        gb = dot((xd * tail).astype(bf), gsb, ((1,), (1,)))
        xdf = xdb.astype(jnp.float32)
        glast = jnp.sum(xdf * gxd_tail, axis=0, keepdims=True) + decay * jnp.sum(
            grad_state * state, axis=0, keepdims=True
        )
        grad_state = grad_state * decay + dot(c_mat, gye, ((0,), (0,)))
        ginner = jnp.zeros((GROUP, GROUP), jnp.float32)
        intra = []
        for pair in range(width // (2 * HEAD_DIM)):
            lanes = slice(pair * 2 * HEAD_DIM, (pair + 1) * 2 * HEAD_DIM)
            halves = []
            for side in (0, 1):
                head = 2 * pair + side
                gap = jnp.where(causal, cum[:, head : head + 1] - cum_t_ref[pl.ds(at + head, 1), rows], NEVER)
                fall = jnp.exp(gap)
                weights = (inner * fall).astype(bf)
                own = (lane < HEAD_DIM) if side == 0 else (lane >= HEAD_DIM)
                gyh = jnp.where(own, gy[:, lanes], 0.0).astype(bf)
                ginner = ginner + dot(gyh, xdb[:, lanes], ((1,), (1,))) * fall
                halves.append(dot(weights, gyb[:, lanes], ((0,), (0,))))
            intra.append(jnp.where(lane < HEAD_DIM, halves[0], halves[1]))
        gxd = jnp.concatenate(intra, axis=1) + gxd_tail
        gib = ginner.astype(bf)
        gbc_ref[rows, 0:STATE] += gb + dot(gib, c_mat, ((0,), (0,)))
        gbc_ref[rows, STATE : 2 * STATE] += gc + dot(gib, b_mat, ((1,), (0,)))
        moved = gyb.astype(jnp.float32) * y - xdf * gxd
        drawn = x * gxd
        at_end = lax.broadcasted_iota(jnp.int32, (GROUP, 1), 0) == GROUP - 1
        cums = jnp.zeros((GROUP, 128), jnp.float32)
        draws = jnp.zeros((GROUP, 128), jnp.float32)
        for head in range(heads):
            mine = lane_wide == head
            here = jnp.sum(jnp.where(mine, moved, 0.0), axis=1, keepdims=True)
            end = jnp.sum(jnp.where(mine, glast, 0.0), axis=1, keepdims=True)
            place = lane_all == at + head
            cums = jnp.where(place, here + jnp.where(at_end, end, 0.0), cums)
            draws = jnp.where(place, jnp.sum(jnp.where(mine, drawn, 0.0), axis=1, keepdims=True), draws)
        gcum_ref[rows, :] += cums
        gdelta_ref[rows, :] += draws
        gskip = gskip + jnp.sum(gy * x, axis=0, keepdims=True)
        gpad_ref[rows, :] = (gxd * delta + skip * gy) * slope[rows]
    gpre = gpad_ref[0:count, :]
    total = jnp.zeros((count, width), jnp.float32)
    for offset in range(CONVK):
        ahead = CONVK - 1 - offset
        total = total + par_ref[offset : offset + 1, :] * gpad_ref[ahead : ahead + count, :]
        start = PAD - ahead
        gpar_ref[offset : offset + 1, :] = jnp.sum(
            gpre * pad_ref[start : start + count, :], axis=0, keepdims=True
        )
    gx_ref[...] = total.astype(bf)
    gpar_ref[4:5, :] = jnp.sum(gpre, axis=0, keepdims=True)
    gpar_ref[5:6, :] = gskip
    gpar_ref[6:7, :] = ggain
    gpar_ref[7:8, :] = jnp.zeros((1, width), jnp.float32)


def head_block(heads):
    return 4 if heads % 4 == 0 else 2


def fixed(shape):
    return pl.BlockSpec(shape, lambda i: (0,) * len(shape))


def moving(rows, width, at=0):
    return pl.BlockSpec((rows, width), lambda i: (0, i + at))


def mix_forward(part, heads, normed, w_x, w_gate, pulled, bc, delta, cum, cum_t, params):
    count, d_model = normed.shape
    block = head_block(heads)
    width = block * HEAD_DIM
    lead = heads // block * part
    groups = count // GROUP
    whole = heads * HEAD_DIM
    return pl.pallas_call(
        functools.partial(scan_forward, lead=heads * part),
        grid=(heads // block,),
        in_specs=[
            fixed((count, d_model)),
            moving(d_model, width),
            moving(d_model, width),
            moving(count, width, lead),
            fixed((count, 2 * STATE)),
            fixed((count, 128)),
            fixed((count, 128)),
            fixed((128, count)),
            moving(8, width, lead),
        ],
        out_specs=[
            moving(count, width),
            moving(count, width),
            moving(count, width),
            pl.BlockSpec((groups, STATE, width), lambda i: (0, 0, i)),
            fixed((count, 256)),
        ],
        out_shape=[
            jax.ShapeDtypeStruct((count, whole), jnp.bfloat16),
            jax.ShapeDtypeStruct((count, whole), jnp.float32),
            jax.ShapeDtypeStruct((count, whole), jnp.float32),
            jax.ShapeDtypeStruct((groups, STATE, whole), jnp.float32),
            jax.ShapeDtypeStruct((count, 256), jnp.float32),
        ],
        scratch_shapes=[pltpu.VMEM((count + PAD, width), jnp.float32)],
        name="scan_forward",
    )(normed, w_x, w_gate, pulled, bc, delta, cum, cum_t, params)


def mix_backward(part, heads, x, gate, mixed, states, pulled, norms, bc, delta, cum, cum_t, params):
    count = x.shape[0]
    block = head_block(heads)
    width = block * HEAD_DIM
    lead = heads // block * part
    groups = count // GROUP
    whole = heads * HEAD_DIM
    return pl.pallas_call(
        functools.partial(scan_backward, lead=heads * part),
        grid=(heads // block,),
        in_specs=[
            moving(count, width),
            moving(count, width),
            moving(count, width),
            pl.BlockSpec((groups, STATE, width), lambda i: (0, 0, i)),
            moving(count, width, lead),
            fixed((count, 128)),
            fixed((count, 2 * STATE)),
            fixed((count, 128)),
            fixed((count, 128)),
            fixed((128, count)),
            moving(8, width, lead),
        ],
        out_specs=[
            moving(count, width),
            moving(count, width),
            fixed((count, 2 * STATE)),
            fixed((count, 128)),
            fixed((count, 128)),
            moving(8, width),
        ],
        out_shape=[
            jax.ShapeDtypeStruct((count, whole), jnp.bfloat16),
            jax.ShapeDtypeStruct((count, whole), jnp.bfloat16),
            jax.ShapeDtypeStruct((count, 2 * STATE), jnp.float32),
            jax.ShapeDtypeStruct((count, 128), jnp.float32),
            jax.ShapeDtypeStruct((count, 128), jnp.float32),
            jax.ShapeDtypeStruct((8, whole), jnp.float32),
        ],
        scratch_shapes=[
            pltpu.VMEM((count + PAD, width), jnp.float32),
            pltpu.VMEM((count + PAD, width), jnp.float32),
        ],
        name="scan_backward",
    )(x, gate, mixed, states, pulled, norms, bc, delta, cum, cum_t, params)


def unzip(at_ref, in_ref, own_ref, other_ref, *, chans, half, heads):
    even = at_ref[0] == 0
    lane = lax.broadcasted_iota(jnp.int32, (1, 128), 1)
    step_at, bc_at = 2 * chans + 2 * STATE, 2 * chans
    kind = own_ref.dtype

    def emit(low, high, to):
        own_ref[:, to : to + 128] = jnp.where(even, low, high).astype(kind)
        other_ref[:, to : to + 128] = jnp.where(even, high, low).astype(kind)

    for source, starts in ((chans, (0, 2 * half + 384)), (0, (half + 128, 3 * half + 384))):
        for at in range(0, chans // 2, 128):
            a = in_ref[:, source + 2 * at : source + 2 * at + 128].astype(jnp.float32)
            b = in_ref[:, source + 2 * at + 128 : source + 2 * at + 256].astype(jnp.float32)
            low = jnp.where(lane < HEAD_DIM, a, pltpu.roll(b, HEAD_DIM, 1))
            high = jnp.where(lane < HEAD_DIM, pltpu.roll(a, HEAD_DIM, 1), b)
            emit(low, high, starts[at // half] + at % half)
    steps = in_ref[:, step_at : step_at + heads]
    row = lax.broadcasted_iota(jnp.int32, (heads, 128), 0)
    col = lax.broadcasted_iota(jnp.int32, (heads, 128), 1)
    sides = [
        dot(steps, jnp.where((row == 2 * col + side) & (col < heads // 2), 1.0, 0.0).astype(kind), ((1,), (0,)))
        for side in (0, 1)
    ]
    emit(sides[0], sides[1], half)
    bc = in_ref[:, bc_at:step_at]
    own_ref[:, 2 * half + 128 : 2 * half + 384] = bc
    other_ref[:, 2 * half + 128 : 2 * half + 384] = bc


def zipped(at_ref, own1_ref, other1_ref, own2_ref, other2_ref, out_ref, *, chans, half, heads):
    even = at_ref[0] == 0
    lane = lax.broadcasted_iota(jnp.int32, (1, 128), 1)
    bc_at, step_at = 2 * chans, 2 * chans + 2 * STATE
    for target, lead in ((chans, 0), (0, 1)):
        for at in range(0, chans // 2, 128):
            second = at >= half
            to = at % half + lead * (half if second else half + 128)
            own_ref, other_ref = (own2_ref, other2_ref) if second else (own1_ref, other1_ref)
            own, other = own_ref[:, to : to + 128], other_ref[:, to : to + 128]
            low, high = jnp.where(even, own, other), jnp.where(even, other, own)
            out_ref[:, target + 2 * at : target + 2 * at + 128] = jnp.where(
                lane < HEAD_DIM, low, pltpu.roll(high, HEAD_DIM, 1)
            )
            out_ref[:, target + 2 * at + 128 : target + 2 * at + 256] = jnp.where(
                lane < HEAD_DIM, pltpu.roll(low, HEAD_DIM, 1), high
            )
    cols = slice(2 * half + 128, 2 * half + 384)
    out_ref[:, bc_at:step_at] = own1_ref[:, cols] + other1_ref[:, cols]
    row = lax.broadcasted_iota(jnp.int32, (128, heads), 0)
    col = lax.broadcasted_iota(jnp.int32, (128, heads), 1)
    own, other = own1_ref[:, half : half + 128], other1_ref[:, half : half + 128]
    total = 0.0
    for side, values in ((0, jnp.where(even, own, other)), (1, jnp.where(even, other, own))):
        choice = jnp.where((col == 2 * row + side) & (row < heads // 2), 1.0, 0.0)
        total = total + lax.dot_general(
            values, choice, (((1,), (0,)), ((), ())), precision=PRECISE, preferred_element_type=jnp.float32
        )
    out_ref[:, step_at : step_at + heads] = total


def scalar():
    return pl.BlockSpec(memory_space=pltpu.SMEM)


def full():
    return pl.BlockSpec(memory_space=pltpu.VMEM)


def unzip_columns(at, rows, half):
    shape = jax.ShapeDtypeStruct((rows.shape[0], 4 * half + 384), rows.dtype)
    return pl.pallas_call(
        functools.partial(unzip, chans=D_INNER, half=half, heads=HEADS),
        in_specs=[scalar(), full()],
        out_specs=[full(), full()],
        out_shape=[shape, shape],
        name="unzip_columns",
    )(at.reshape(1), rows)


def zip_columns(at, own1, other1, own2, other2, half):
    return pl.pallas_call(
        functools.partial(zipped, chans=D_INNER, half=half, heads=HEADS),
        in_specs=[scalar()] + [full()] * 4,
        out_specs=full(),
        out_shape=jax.ShapeDtypeStruct((own1.shape[0], D_INNER + CONV_CH + HEADS), jnp.float32),
        name="zip_columns",
    )(at.reshape(1), own1, other1, own2, other2)


def rms_scale(values, gain):
    return values * lax.rsqrt(jnp.mean(values * values, axis=-1, keepdims=True) + EPS) * gain


def conv_act(values, conv_weight, conv_bias):
    count = values.shape[0]
    extended = jnp.concatenate([jnp.zeros((CONVK - 1, values.shape[1]), jnp.float32), values], axis=0)
    summed = conv_bias[None, :] + conv_weight[0][None, :] * extended[0:count]
    for offset in range(1, CONVK):
        summed = summed + conv_weight[offset][None, :] * extended[offset : offset + count]
    return jax.nn.silu(summed)


class Split:
    def __init__(self, out_rows):
        self.peers = lax.axis_size("seq")
        self.at = lax.axis_index("seq")
        blocks = lax.axis_size("dp")
        self.staged = out_rows == HEAD_DIM and blocks % PLANE == 0 and self.peers == 2
        self.outer = blocks if self.staged else 1

    def view(self, v):
        return v.reshape(v.shape[:-1] + (self.outer, self.peers, v.shape[-1] // (self.outer * self.peers)))

    def own(self, v, at=None):
        part = pick(self.view(v), self.at if at is None else at, v.ndim)
        return part.reshape(v.shape[:-1] + (-1,))

    def place(self, whole, part, at=None):
        view = self.view(whole)
        piece = part.reshape(view.shape[:-2] + view.shape[-1:])
        return put(view, piece, self.at if at is None else at, whole.ndim).reshape(whole.shape)

    def placed(self, part):
        return self.place(jnp.zeros(part.shape[:-1] + (part.shape[-1] * self.peers,), part.dtype), part)

    def exchange(self, piece_for):
        pieces = [(self.at, piece_for(self.at))]
        for steps in range(1, self.peers):
            sent = piece_for((self.at + steps) % self.peers)
            pieces.append(((self.at - steps) % self.peers, seq_shift(sent, steps)))
        return pieces

    def scatter_rows(self, x):
        rows = x.reshape((self.peers, x.shape[0] // self.peers) + x.shape[1:])
        total = 0.0
        for _, piece in self.exchange(lambda to: pick(rows, to, 0)):
            total = total + piece
        return total


def per_device(
    hidden_in, upstream, in_weight, out_weight, norm_gain, conv_weight, conv_bias,
    step_bias, log_rate, skip_weight, gate_gain,
):
    bf = jnp.bfloat16
    split = Split(out_weight.shape[0])
    peers, at = split.peers, split.at
    stream, grad_top = hidden_in[0], upstream[0]
    own_rows, d_model = stream.shape
    count = own_rows * peers
    groups = count // GROUP
    heads = HEADS // peers
    inner = D_INNER // peers
    half_heads = heads // 2
    half = inner // 2
    lanes = -(-heads // 128) * 128

    def in_columns(rows):
        x = split.own(rows[:, D_INNER : 2 * D_INNER])
        gate = split.own(rows[:, :D_INNER])
        bc = rows[:, 2 * D_INNER : D_INNER + CONV_CH]
        steps = split.own(rows[:, D_INNER + CONV_CH :])
        blank = jnp.zeros((rows.shape[0], lanes - heads), rows.dtype)
        return (
            jnp.concatenate([x[:, :half], steps, blank], axis=1),
            jnp.concatenate([gate[:, :half], bc], axis=1),
            x[:, half:],
            gate[:, half:],
        )

    first_cut = half + lanes
    first_width = first_cut + half + 2 * STATE
    if split.staged:
        own, other = unzip_columns(at, in_weight, half)
        arrived = seq_shift(other, 1)
        block = put(put(jnp.zeros((peers,) + own.shape, bf), own, at, 0), arrived, 1 - at, 0)
        block = block.reshape(-1, block.shape[-1])

    normed_own = rms_scale(stream, norm_gain).astype(bf)
    both = jnp.concatenate([normed_own, grad_top.astype(bf)], axis=1)
    tokens = jnp.zeros((peers,) + both.shape, bf)
    arrived_tokens = split.exchange(lambda to: both)
    for origin, part in arrived_tokens:
        tokens = put(tokens, part, origin, 0)
    tokens = tokens.reshape(count, -1)
    normed, top = tokens[:, :d_model], tokens[:, d_model:]

    if split.staged:
        out_left, out_right, gate = gathered(out_weight, d_model // 2, None)
        x_first, gate_first, gate = gathered(block[:, :first_width], first_cut, gate)
        x_second, gate_second, _ = gathered(block[:, first_width:], half, gate)
    else:
        in_all = lax.all_gather(in_weight, ("dp", "seq"), axis=0, tiled=True)
        x_first, gate_first, x_second, gate_second = in_columns(in_all)
        out_all = split.own(lax.all_gather(out_weight, ("dp", "seq"), axis=0, tiled=True).T).T
        out_left, out_right = out_all[:, : d_model // 2], out_all[:, d_model // 2 :]
    top_left, top_right = top[:, : d_model // 2], top[:, d_model // 2 :]

    own_bias = split.own(step_bias)
    rates = -jnp.exp(split.own(log_rate))
    own_gain = split.own(gate_gain)
    conv_x = split.own(conv_weight[:, :D_INNER])
    params = jnp.concatenate(
        [
            conv_x,
            split.own(conv_bias[:D_INNER])[None],
            jnp.repeat(split.own(skip_weight), HEAD_DIM)[None],
            own_gain[None],
            jnp.zeros((1, inner), jnp.float32),
        ],
        axis=0,
    )
    tri = (jnp.arange(GROUP)[:, None] >= jnp.arange(GROUP)[None, :]).astype(jnp.float32)

    step_raw = dot(normed, x_first[:, half:], ((1,), (0,)))
    step_in = step_raw + jnp.pad(own_bias, (0, lanes - heads))[None, :]
    all_rates = jnp.pad(rates, (0, lanes - heads))[None, :]
    deltas = jax.nn.softplus(step_in)
    cum = jnp.einsum(
        "ts,gsh->gth", tri, (deltas * all_rates).reshape(groups, GROUP, lanes), precision=PRECISE
    ).reshape(count, lanes)
    cum_t = cum.T
    bc_in = dot(normed, gate_first[:, half:], ((1,), (0,))).astype(bf).astype(jnp.float32)
    bc, bc_back = jax.vjp(conv_act, bc_in, conv_weight[:, D_INNER:], conv_bias[D_INNER:])

    pulled = dot(top_left, out_left, ((1,), (1,))) + dot(top_right, out_right, ((1,), (1,)))
    saved = []
    for part, (w_x, w_gate) in enumerate(((x_first, gate_first), (x_second, gate_second))):
        saved.append(mix_forward(part, half_heads, normed, w_x, w_gate, pulled, bc, deltas, cum, cum_t, params))
    sums = saved[0][4] + saved[1][4]
    sums = jnp.stack([jnp.sum(sums[:, :128], axis=1), jnp.sum(sums[:, 128:], axis=1)])
    sums = seq_sum(sums)
    scale = lax.rsqrt(sums[0] / D_INNER + EPS)
    lean = sums[1] * scale * scale * scale / D_INNER
    norms = jnp.pad(jnp.stack([scale, lean], axis=1), ((0, 0), (0, 126)))

    normed_out = jnp.concatenate(
        [
            (mixed * jax.nn.silu(gate) * scale[:, None] * own_gain[None, part * half : (part + 1) * half]).astype(bf)
            for part, (_, gate, mixed, _, _) in enumerate(saved)
        ],
        axis=1,
    )
    grad_out = [dot(normed_out, side, ((0,), (0,))).astype(bf) for side in (top_left, top_right)]
    if split.staged:
        out_parts = scattered(*grad_out)

    grad_ins = [None, None]
    shares = [None, None]
    grad_cum = grad_delta = grad_bc = grad_normed = 0.0
    grad_pars = [None, None]
    for part in (1, 0):
        gx, ggate, gbc, gcum, gdelta, grad_pars[part] = mix_backward(
            part, half_heads, *saved[part][:4], pulled, norms, bc, deltas, cum, cum_t, params
        )
        grad_bc, grad_cum, grad_delta = grad_bc + gbc, grad_cum + gcum, grad_delta + gdelta
        if part == 0:
            grad_bc_in, grad_bc_w, grad_bc_b = bc_back(grad_bc)
            grad_rate = jnp.einsum(
                "ts,gth->gsh", tri, grad_cum.reshape(groups, GROUP, lanes), precision=PRECISE
            ).reshape(count, lanes)
            grad_step = (grad_rate * all_rates + grad_delta) * jax.nn.sigmoid(step_in)
            gx = jnp.concatenate([gx, grad_step.astype(bf)], axis=1)
            ggate = jnp.concatenate([ggate, grad_bc_in.astype(bf)], axis=1)
        grad_ins[part] = [dot(normed, side, ((0,), (0,))).astype(bf) for side in (gx, ggate)]
        w_x, w_gate = ((x_first, gate_first), (x_second, gate_second))[part]
        if split.staged:
            shares[part] = scattered(*grad_ins[part])
        grad_normed = grad_normed + dot(gx, w_x, ((1,), (1,))) + dot(ggate, w_gate, ((1,), (1,)))

    def block_rows(to):
        rows = lax.dynamic_slice_in_dim(normed_out, to * own_rows, own_rows, 0)
        return jnp.concatenate([dot(rows, side, ((1,), (0,))) for side in (out_left, out_right)], axis=1)

    block_out = stream
    for _, piece in split.exchange(block_rows):
        block_out = block_out + piece
    grad_normed = split.scatter_rows(grad_normed)
    _, norm_back = jax.vjp(rms_scale, stream, norm_gain)
    grad_stream, grad_norm_gain = norm_back(grad_normed)

    grad_par = jnp.concatenate(grad_pars, axis=1)
    small = [
        jnp.concatenate([split.placed(grad_par[:CONVK]), grad_bc_w], axis=1),
        jnp.concatenate([split.placed(grad_par[CONVK]), grad_bc_b]),
        split.placed(jnp.sum(grad_step, axis=0)[:heads]),
        split.placed(jnp.sum(grad_rate * deltas, axis=0)[:heads] * rates),
        split.placed(jnp.sum(grad_par[CONVK + 1].reshape(heads, HEAD_DIM), axis=1)),
        split.placed(grad_par[CONVK + 2]),
        grad_norm_gain,
    ]
    packed = everywhere_sum(jnp.concatenate([v.reshape(-1) for v in small]))
    summed, offset = [], 0
    for v in small:
        summed.append(packed[offset : offset + v.size].reshape(v.shape))
        offset += v.size

    if split.staged:
        gate = shares[0][2]
        out_share = arrived_sum(out_parts, gate)
        pairs = []
        for part, after in ((shares[0], None), (shares[1], gate)):
            share = arrived_sum(part, after)
            pair = share.reshape(peers, -1, share.shape[-1])
            pairs += [pick(pair, at, 0), seq_shift(pick(pair, 1 - at, 0), 1)]
        in_share = zip_columns(at, *pairs, half)
    else:
        empty = jnp.zeros((d_model, D_INNER), jnp.float32)
        (x_low, gate_low), (x_high, gate_high) = ([v.astype(jnp.float32) for v in pair] for pair in grad_ins)
        in_share = jnp.concatenate(
            [
                split.place(empty, jnp.concatenate([gate_low[:, :half], gate_high], axis=1)),
                split.place(empty, jnp.concatenate([x_low[:, :half], x_high], axis=1)),
                gate_low[:, half:],
                split.placed(x_low[:, half : half + heads]),
            ],
            axis=1,
        )
        in_share = lax.psum_scatter(in_share, ("dp", "seq"), scatter_dimension=0, tiled=True)
        grad_out = jnp.concatenate(grad_out, axis=1).astype(jnp.float32)
        out_share = lax.psum_scatter(
            split.placed(grad_out.T).T, ("dp", "seq"), scatter_dimension=0, tiled=True
        )

    return (
        block_out[None], (grad_top + grad_stream)[None], in_share, out_share, summed[6],
        summed[0], summed[1], summed[2], summed[3], summed[4], summed[5],
    )


def solution(mesh):
    tokens, rows, whole = P("dp", "seq", None), P(("dp", "seq"), None), P()
    return jax.shard_map(
        per_device,
        mesh=mesh,
        in_specs=(tokens, tokens, rows, rows) + (whole,) * 7,
        out_specs=(tokens, tokens, rows, rows) + (whole,) * 7,
        check_vma=False,
    )
```

```python
import functools

import jax
import jax.numpy as jnp
from jax import lax
from jax.experimental import pallas as pl
from jax.experimental.pallas import tpu as pltpu
from jax.sharding import PartitionSpec as P


D_INNER = 2048
HEADS = 32
HEAD_DIM = 64
STATE = 128
CONVK = 4
GROUP = 256
CONV_CH = 2304
EPS = 1e-05
PRECISE = lax.Precision.HIGHEST
PAD = 8
PLANE = 4
NEVER = -1e30


def pick(x, index, axis):
    return lax.dynamic_index_in_dim(x, index, axis, keepdims=False)


def put(buffer, piece, index, axis):
    return lax.dynamic_update_index_in_dim(buffer, piece, index, axis)


def swapped(x, bit):
    return lax.ppermute(x, "dp", [(i, i ^ bit) for i in range(lax.axis_size("dp"))])


def column_shift(x, steps):
    size = lax.axis_size("dp")
    return lax.ppermute(x, "dp", [(i, (i + PLANE * steps) % size) for i in range(size)])


def seq_shift(x, steps):
    size = lax.axis_size("seq")
    return lax.ppermute(x, "seq", [(i, (i + steps) % size) for i in range(size)])


def seq_sum(x):
    size = lax.axis_size("seq")
    if size == 2:
        return x + seq_shift(x, 1)
    return lax.psum(x, "seq")


def everywhere_sum(x):
    size = lax.axis_size("dp")
    if size & (size - 1) or lax.axis_size("seq") != 2:
        return lax.psum(x, ("dp", "seq"))
    x = seq_sum(x)
    bit = size // 2
    while bit:
        x = x + swapped(x, bit)
        bit //= 2
    return x


def joined(pieces):
    (at, piece), (other, arrived) = pieces
    pair = jnp.zeros(piece.shape[:1] + (2,) + piece.shape[1:], piece.dtype)
    return put(put(pair, piece, at, 1), arrived, other, 1)


def gathered(block, cut, gate):
    at = lax.axis_index("dp")
    tall, y, x = at // PLANE, at % PLANE // 2, at % 2
    height = lax.axis_size("dp") // PLANE
    column = jnp.zeros((height,) + block.shape, block.dtype)
    column = put(column, block, tall, 0)
    moved = [column_shift(block, steps) for steps in range(1, height)]
    if gate is not None:
        moved, _ = lax.optimization_barrier((moved, gate))
    for steps, piece in enumerate(moved, 1):
        column = put(column, piece, (tall - steps) % height, 0)
    left, right = column[..., :cut], column[..., cut:]
    left_near, right_near = swapped(left, 1), swapped(right, 2)
    later = (left_near, right_near)
    x, left_near = lax.optimization_barrier((x, left_near))
    y, right_near = lax.optimization_barrier((y, right_near))
    left, right = joined(((x, left), (1 - x, left_near))), joined(((y, right), (1 - y, right_near)))
    left_far, right_far = swapped(left, 2), swapped(right, 1)
    y, left_far = lax.optimization_barrier((y, left_far))
    x, right_far = lax.optimization_barrier((x, right_far))
    left = joined(((y, left), (1 - y, left_far)))
    full = jnp.zeros((height, 2, 2) + right.shape[2:], right.dtype)
    right = put(put(full, right, x, 2), right_far, 1 - x, 2)
    return left.reshape(-1, cut), right.reshape(-1, block.shape[-1] - cut), later


def plane_sum(sent, kept, bit):
    at = lax.axis_index("dp")
    height = lax.axis_size("dp") // PLANE
    wide = jnp.float32
    near_bit = 3 - bit
    place = at % PLANE // near_bit % 2
    far = swapped(sent, bit)
    half = (kept.astype(wide) + far.astype(wide)).reshape(height, 2, -1, kept.shape[-1])
    near = swapped(pick(half, 1 - place, 1).astype(sent.dtype), near_bit)
    return pick(half, place, 1) + near.astype(wide), near


def column_sum(column, gate):
    height = lax.axis_size("dp") // PLANE
    tall = lax.axis_index("dp") // PLANE
    sent = column.astype(jnp.bfloat16)
    moved = [column_shift(pick(sent, (tall + k) % height, 0), k) for k in range(1, height)]
    return moved, pick(column, tall, 0), gate


def arrived_sum(parts, gate):
    moved, total, _ = parts
    if gate is not None:
        moved, _ = lax.optimization_barrier((moved, gate))
    for piece in moved:
        total = total + piece.astype(jnp.float32)
    return total


def dot(a, b, over):
    return lax.dot_general(a, b, ((over[0], over[1]), ((), ())), preferred_element_type=jnp.float32)


def spread(columns, width):
    lane = lax.broadcasted_iota(jnp.int32, (1, width), 1)
    out = columns[:, 0:1]
    for head in range(1, width // HEAD_DIM):
        out = jnp.where(lane >= head * HEAD_DIM, columns[:, head : head + 1], out)
    return jnp.broadcast_to(out, (columns.shape[0], width))


def conv_pre(padded_ref, weight, bias, count):
    summed = bias
    for offset in range(CONVK):
        start = PAD - (CONVK - 1) + offset
        summed = summed + weight[offset : offset + 1] * padded_ref[start : start + count, :]
    return summed


def sigmoid(v):
    return 1.0 / (1.0 + jnp.exp(-v))


def causal_mask():
    return lax.broadcasted_iota(jnp.int32, (GROUP, GROUP), 0) >= lax.broadcasted_iota(
        jnp.int32, (GROUP, GROUP), 1
    )


def own_lanes(values, lane):
    return pltpu.roll(values, (values.shape[1] - lane) % values.shape[1], 1)


def folded(values):
    total = values[:, :128]
    for at in range(128, values.shape[1], 128):
        total = total + values[:, at : at + 128]
    return total


def scan_forward(
    normed_ref, wx_ref, wg_ref, pulled_ref, bc_ref, delta_ref, cum_ref, cum_t_ref, par_ref,
    x_ref, gate_ref, mixed_ref, state_ref, sums_ref, pad_ref, *, lead,
):
    count, width = mixed_ref.shape
    bf = jnp.bfloat16
    at = lead + pl.program_id(0) * (width // HEAD_DIM)
    normed = normed_ref[...]
    conv_in = dot(normed, wx_ref[...], ((1,), (0,))).astype(bf)
    gate = dot(normed, wg_ref[...], ((1,), (0,)))
    x_ref[...] = conv_in
    gate_ref[...] = gate
    pad_ref[0:PAD, :] = jnp.zeros((PAD, width), jnp.float32)
    pad_ref[PAD : PAD + count, :] = conv_in.astype(jnp.float32)
    pre = conv_pre(pad_ref, par_ref[0:4, :], par_ref[4:5, :], count)
    acts = pre * sigmoid(pre)
    skip = par_ref[5:6, :]
    causal = causal_mask()
    lane = lax.broadcasted_iota(jnp.int32, (1, 2 * HEAD_DIM), 1)
    state = jnp.zeros((STATE, width), jnp.float32)

    @pl.when(pl.program_id(0) == 0)
    def _():
        sums_ref[...] = jnp.zeros(sums_ref.shape, jnp.float32)

    for group in range(count // GROUP):
        rows = slice(group * GROUP, (group + 1) * GROUP)
        state_ref[group] = state
        b_mat = bc_ref[rows, 0:STATE].astype(bf)
        c_mat = bc_ref[rows, STATE : 2 * STATE].astype(bf)
        inner = dot(c_mat, b_mat, ((1,), (1,)))
        x = acts[rows]
        cum = own_lanes(cum_ref[rows, :], at)
        cum_wide = spread(cum, width)
        last = cum_wide[GROUP - 1 : GROUP, :]
        xd = x * spread(own_lanes(delta_ref[rows, :], at), width)
        xdb = xd.astype(bf)
        y = dot(c_mat, state.astype(bf), ((1,), (0,))) * jnp.exp(cum_wide) + skip * x
        intra = []
        for pair in range(width // (2 * HEAD_DIM)):
            lanes = slice(pair * 2 * HEAD_DIM, (pair + 1) * 2 * HEAD_DIM)
            halves = []
            for head in (2 * pair, 2 * pair + 1):
                gap = jnp.where(causal, cum[:, head : head + 1] - cum_t_ref[pl.ds(at + head, 1), rows], NEVER)
                halves.append(dot((inner * jnp.exp(gap)).astype(bf), xdb[:, lanes], ((1,), (0,))))
            intra.append(jnp.where(lane < HEAD_DIM, halves[0], halves[1]))
        mixed = y + jnp.concatenate(intra, axis=1)
        mixed_ref[rows, :] = mixed
        tail = (xd * jnp.exp(last - cum_wide)).astype(bf)
        state = state * jnp.exp(last) + dot(b_mat, tail, ((0,), (0,)))
        part = gate[rows]
        gated = mixed * part * sigmoid(part)
        sums_ref[rows, 0:128] += folded(gated * gated)
        sums_ref[rows, 128:256] += folded(pulled_ref[rows, :] * par_ref[6:7, :] * gated)


def scan_backward(
    x_ref, gate_ref, mixed_ref, state_ref, pulled_ref, norm_ref, bc_ref, delta_ref, cum_ref, cum_t_ref, par_ref,
    *refs, lead, final,
):
    if final:
        gbc0_ref, gcum0_ref, gdelta0_ref, bcin_ref, step_ref, rate_ref, bcpar_ref = refs[:7]
        refs = refs[7:]
    gx_ref, ggate_ref, gbc_ref, gcum_ref, gdelta_ref, gpar_ref = refs[:6]
    if final:
        gstep_ref, gbcin_ref, gheads_ref, gbcpar_ref = refs[6:10]
    pad_ref, gpad_ref = refs[-2:]
    count, width = x_ref.shape
    bf = jnp.bfloat16
    heads = width // HEAD_DIM
    at = lead + pl.program_id(0) * heads
    pad_ref[0:PAD, :] = jnp.zeros((PAD, width), jnp.float32)
    pad_ref[PAD : PAD + count, :] = x_ref[...].astype(jnp.float32)
    pre = conv_pre(pad_ref, par_ref[0:4, :], par_ref[4:5, :], count)
    sig = sigmoid(pre)
    acts = pre * sig
    slope = sig * (1.0 + pre * (1.0 - sig))
    skip = par_ref[5:6, :]
    gain = par_ref[6:7, :]
    causal = causal_mask()
    lane = lax.broadcasted_iota(jnp.int32, (1, 2 * HEAD_DIM), 1)
    lane_wide = lax.broadcasted_iota(jnp.int32, (1, width), 1) // HEAD_DIM
    lane_all = lax.broadcasted_iota(jnp.int32, (1, 128), 1)
    grad_state = jnp.zeros((STATE, width), jnp.float32)
    gskip = jnp.zeros((1, width), jnp.float32)
    ggain = jnp.zeros((1, width), jnp.float32)

    @pl.when(pl.program_id(0) == 0)
    def _():
        gbc_ref[...] = gbc0_ref[...] if final else jnp.zeros(gbc_ref.shape, jnp.float32)
        gcum_ref[...] = gcum0_ref[...] if final else jnp.zeros(gcum_ref.shape, jnp.float32)
        gdelta_ref[...] = gdelta0_ref[...] if final else jnp.zeros(gdelta_ref.shape, jnp.float32)

    gpad_ref[count : count + PAD, :] = jnp.zeros((PAD, width), jnp.float32)
    for group in reversed(range(count // GROUP)):
        rows = slice(group * GROUP, (group + 1) * GROUP)
        scale, lean = norm_ref[rows, 0:1], norm_ref[rows, 1:2]
        gate, mixed, pulled = gate_ref[rows, :], mixed_ref[rows, :], pulled_ref[rows, :]
        sigma = sigmoid(gate)
        gated = mixed * gate * sigma
        ggain = ggain + jnp.sum(pulled * gated * scale, axis=0, keepdims=True)
        ggated = pulled * gain * scale - gated * lean
        ggate_ref[rows, :] = (ggated * mixed * sigma * (1.0 + gate * (1.0 - sigma))).astype(bf)
        gy = ggated * gate * sigma
        gyb = gy.astype(bf)
        b_mat = bc_ref[rows, 0:STATE].astype(bf)
        c_mat = bc_ref[rows, STATE : 2 * STATE].astype(bf)
        inner = dot(c_mat, b_mat, ((1,), (1,)))
        x = acts[rows]
        cum = own_lanes(cum_ref[rows, :], at)
        cum_wide = spread(cum, width)
        last = cum_wide[GROUP - 1 : GROUP, :]
        decay = jnp.exp(last)
        delta = spread(own_lanes(delta_ref[rows, :], at), width)
        xd = x * delta
        xdb = xd.astype(bf)
        tail = jnp.exp(last - cum_wide)
        state = state_ref[group]
        y = mixed - skip * x
        gye = (gy * jnp.exp(cum_wide)).astype(bf)
        gc = dot(gye, state.astype(bf), ((1,), (1,)))
        gsb = grad_state.astype(bf)
        gxd_tail = dot(b_mat, gsb, ((1,), (0,))) * tail
        gb = dot((xd * tail).astype(bf), gsb, ((1,), (1,)))
        xdf = xdb.astype(jnp.float32)
        glast = jnp.sum(xdf * gxd_tail, axis=0, keepdims=True) + decay * jnp.sum(
            grad_state * state, axis=0, keepdims=True
        )
        grad_state = grad_state * decay + dot(c_mat, gye, ((0,), (0,)))
        ginner = jnp.zeros((GROUP, GROUP), jnp.float32)
        intra = []
        for pair in range(width // (2 * HEAD_DIM)):
            lanes = slice(pair * 2 * HEAD_DIM, (pair + 1) * 2 * HEAD_DIM)
            halves = []
            for side in (0, 1):
                head = 2 * pair + side
                gap = jnp.where(causal, cum[:, head : head + 1] - cum_t_ref[pl.ds(at + head, 1), rows], NEVER)
                fall = jnp.exp(gap)
                weights = (inner * fall).astype(bf)
                own = (lane < HEAD_DIM) if side == 0 else (lane >= HEAD_DIM)
                gyh = jnp.where(own, gy[:, lanes], 0.0).astype(bf)
                ginner = ginner + dot(gyh, xdb[:, lanes], ((1,), (1,))) * fall
                halves.append(dot(weights, gyb[:, lanes], ((0,), (0,))))
            intra.append(jnp.where(lane < HEAD_DIM, halves[0], halves[1]))
        gxd = jnp.concatenate(intra, axis=1) + gxd_tail
        gib = ginner.astype(bf)
        gbc_ref[rows, 0:STATE] += gb + dot(gib, c_mat, ((0,), (0,)))
        gbc_ref[rows, STATE : 2 * STATE] += gc + dot(gib, b_mat, ((1,), (0,)))
        moved = gyb.astype(jnp.float32) * y - xdf * gxd
        drawn = x * gxd
        at_end = lax.broadcasted_iota(jnp.int32, (GROUP, 1), 0) == GROUP - 1
        cums = jnp.zeros((GROUP, 128), jnp.float32)
        draws = jnp.zeros((GROUP, 128), jnp.float32)
        for head in range(heads):
            mine = lane_wide == head
            here = jnp.sum(jnp.where(mine, moved, 0.0), axis=1, keepdims=True)
            end = jnp.sum(jnp.where(mine, glast, 0.0), axis=1, keepdims=True)
            place = lane_all == at + head
            cums = jnp.where(place, here + jnp.where(at_end, end, 0.0), cums)
            draws = jnp.where(place, jnp.sum(jnp.where(mine, drawn, 0.0), axis=1, keepdims=True), draws)
        gcum_ref[rows, :] += cums
        gdelta_ref[rows, :] += draws
        gskip = gskip + jnp.sum(gy * x, axis=0, keepdims=True)
        gpad_ref[rows, :] = (gxd * delta + skip * gy) * slope[rows]
    gpre = gpad_ref[0:count, :]
    total = jnp.zeros((count, width), jnp.float32)
    for offset in range(CONVK):
        ahead = CONVK - 1 - offset
        total = total + par_ref[offset : offset + 1, :] * gpad_ref[ahead : ahead + count, :]
        start = PAD - ahead
        gpar_ref[offset : offset + 1, :] = jnp.sum(
            gpre * pad_ref[start : start + count, :], axis=0, keepdims=True
        )
    gx_ref[...] = total.astype(bf)
    gpar_ref[4:5, :] = jnp.sum(gpre, axis=0, keepdims=True)
    gpar_ref[5:6, :] = gskip
    gpar_ref[6:7, :] = ggain
    gpar_ref[7:8, :] = jnp.zeros((1, width), jnp.float32)
    if not final:
        return

    @pl.when(pl.program_id(0) == pl.num_programs(0) - 1)
    def _():
        below = jnp.where(causal, 1.0, 0.0)
        step_sum = jnp.zeros((1, 128), jnp.float32)
        rate_sum = jnp.zeros((1, 128), jnp.float32)
        for group in range(count // GROUP):
            rows = slice(group * GROUP, (group + 1) * GROUP)
            ga = lax.dot_general(
                below, gcum_ref[rows, :], (((0,), (0,)), ((), ())), precision=PRECISE,
                preferred_element_type=jnp.float32,
            )
            gstep = (ga * rate_ref[0:1, :] + gdelta_ref[rows, :]) * sigmoid(step_ref[rows, :])
            gstep_ref[rows, :] = gstep.astype(bf)
            step_sum = step_sum + jnp.sum(gstep, axis=0, keepdims=True)
            rate_sum = rate_sum + jnp.sum(ga * delta_ref[rows, :], axis=0, keepdims=True)
        gheads_ref[0:1, :] = step_sum
        gheads_ref[1:2, :] = rate_sum * rate_ref[0:1, :]
        gheads_ref[2:8, :] = jnp.zeros((6, 128), jnp.float32)
        for lanes in range(0, 2 * STATE, width):
            cols = slice(lanes, lanes + width)
            pad_ref[PAD : PAD + count, :] = bcin_ref[:, cols].astype(jnp.float32)
            pre = conv_pre(pad_ref, bcpar_ref[0:4, cols], bcpar_ref[4:5, cols], count)
            sig = sigmoid(pre)
            gpre = gbc_ref[:, cols] * sig * (1.0 + pre * (1.0 - sig))
            gpad_ref[0:count, :] = gpre
            total = jnp.zeros((count, width), jnp.float32)
            for offset in range(CONVK):
                ahead = CONVK - 1 - offset
                total = total + bcpar_ref[offset : offset + 1, cols] * gpad_ref[ahead : ahead + count, :]
                start = PAD - ahead
                gbcpar_ref[offset : offset + 1, cols] = jnp.sum(
                    gpre * pad_ref[start : start + count, :], axis=0, keepdims=True
                )
            gbcin_ref[:, cols] = total.astype(bf)
            gbcpar_ref[4:5, cols] = jnp.sum(gpre, axis=0, keepdims=True)
            gbcpar_ref[5:8, cols] = jnp.zeros((3, width), jnp.float32)


def head_block(heads):
    return 4 if heads % 4 == 0 else 2


def fixed(shape):
    return pl.BlockSpec(shape, lambda i: (0,) * len(shape))


def moving(rows, width, at=0):
    return pl.BlockSpec((rows, width), lambda i: (0, i + at))


def mix_forward(part, heads, normed, w_x, w_gate, pulled, bc, delta, cum, cum_t, params):
    count, d_model = normed.shape
    block = head_block(heads)
    width = block * HEAD_DIM
    lead = heads // block * part
    groups = count // GROUP
    whole = heads * HEAD_DIM
    return pl.pallas_call(
        functools.partial(scan_forward, lead=heads * part),
        grid=(heads // block,),
        in_specs=[
            fixed((count, d_model)),
            moving(d_model, width),
            moving(d_model, width),
            moving(count, width, lead),
            fixed((count, 2 * STATE)),
            fixed((count, 128)),
            fixed((count, 128)),
            fixed((128, count)),
            moving(8, width, lead),
        ],
        out_specs=[
            moving(count, width),
            moving(count, width),
            moving(count, width),
            pl.BlockSpec((groups, STATE, width), lambda i: (0, 0, i)),
            fixed((count, 256)),
        ],
        out_shape=[
            jax.ShapeDtypeStruct((count, whole), jnp.bfloat16),
            jax.ShapeDtypeStruct((count, whole), jnp.float32),
            jax.ShapeDtypeStruct((count, whole), jnp.float32),
            jax.ShapeDtypeStruct((groups, STATE, whole), jnp.float32),
            jax.ShapeDtypeStruct((count, 256), jnp.float32),
        ],
        scratch_shapes=[pltpu.VMEM((count + PAD, width), jnp.float32)],
        name="scan",
    )(normed, w_x, w_gate, pulled, bc, delta, cum, cum_t, params)


def mix_backward(part, heads, x, gate, mixed, states, pulled, norms, bc, delta, cum, cum_t, params, *rest):
    count = x.shape[0]
    block = head_block(heads)
    width = block * HEAD_DIM
    lead = heads // block * part
    groups = count // GROUP
    whole = heads * HEAD_DIM
    f32, bf = jnp.float32, jnp.bfloat16
    in_specs = [
        moving(count, width),
        moving(count, width),
        moving(count, width),
        pl.BlockSpec((groups, STATE, width), lambda i: (0, 0, i)),
        moving(count, width, lead),
        fixed((count, 128)),
        fixed((count, 2 * STATE)),
        fixed((count, 128)),
        fixed((count, 128)),
        fixed((128, count)),
        moving(8, width, lead),
    ]
    out_specs = [moving(count, width)] * 2 + [fixed((count, 2 * STATE))] + [fixed((count, 128))] * 2
    out_specs += [moving(8, width)]
    shapes = [((count, whole), bf)] * 2 + [((count, 2 * STATE), f32)] + [((count, 128), f32)] * 2
    shapes += [((8, whole), f32)]
    if rest:
        in_specs += [fixed(v.shape) for v in rest]
        extra = [((count, 128), bf), ((count, 2 * STATE), bf), ((8, 128), f32), ((8, 2 * STATE), f32)]
        out_specs += [fixed(shape) for shape, _ in extra]
        shapes += extra
    return pl.pallas_call(
        functools.partial(scan_backward, lead=heads * part, final=bool(rest)),
        grid=(heads // block,),
        in_specs=in_specs,
        out_specs=out_specs,
        out_shape=[jax.ShapeDtypeStruct(*shape) for shape in shapes],
        scratch_shapes=[pltpu.VMEM((count + PAD, width), f32)] * 2,
        name="unscan",
    )(x, gate, mixed, states, pulled, norms, bc, delta, cum, cum_t, params, *rest)


def halves_kernel(at_ref, *refs, parts, tall):
    left, rights, (sent_ref, kept_ref) = refs[:-parts - 2], refs[-parts - 2 : -2], refs[-2:]
    low = at_ref[0] == 0
    lanes = 0
    for right_ref in rights:
        right = right_ref[...]
        cols = slice(lanes, lanes + right.shape[1])
        lanes += right.shape[1]
        if tall:
            sent_ref[:, cols] = dot(left[0][...], right, ((0,), (0,))).astype(sent_ref.dtype)
            kept_ref[:, cols] = dot(left[1][...], right, ((0,), (0,))).astype(sent_ref.dtype)
        else:
            rows = dot(left[0][...], right, ((0,), (0,)))
            for y in (0, 1):
                first = rows[128 * y : 128 * y + 64]
                second = rows[128 * y + 64 : 128 * y + 128]
                to = slice(64 * y, 64 * y + 64)
                sent_ref[to, cols] = jnp.where(low, second, first).astype(sent_ref.dtype)
                kept_ref[to, cols] = jnp.where(low, first, second).astype(sent_ref.dtype)


def halves(left, rights, bit):
    count, rows = left.shape
    tall = bit == 2
    at = (lax.axis_index("dp") % PLANE // bit % 2).reshape(1)
    if tall:
        lefts = [
            pl.BlockSpec((count, 128), lambda i, at: (0, 2 * i + 1 - at[0])),
            pl.BlockSpec((count, 128), lambda i, at: (0, 2 * i + at[0])),
        ]
    else:
        lefts = [pl.BlockSpec((count, 256), lambda i, at: (0, i))]
    width = sum(v.shape[1] for v in rights)
    shape = jax.ShapeDtypeStruct((rows // 2, width), jnp.bfloat16)
    return pl.pallas_call(
        functools.partial(halves_kernel, parts=len(rights), tall=tall),
        grid_spec=pltpu.PrefetchScalarGridSpec(
            num_scalar_prefetch=1,
            grid=(rows // 256,),
            in_specs=lefts + [pl.BlockSpec(v.shape, lambda i, at: (0, 0)) for v in rights],
            out_specs=[pl.BlockSpec((128, width), lambda i, at: (i, 0))] * 2,
        ),
        out_shape=[shape, shape],
        name="halves",
    )(at, *([left] * len(lefts)), *rights)


def product_kernel(at_ref, *refs, parts):
    lefts, rights, outs = refs[:parts], refs[parts : 2 * parts], refs[2 * parts :]
    rows = outs[0].shape[0]
    for out_ref, place in ((outs[0], at_ref[0]), (outs[1], 1 - at_ref[0])):
        total = 0.0
        for left_ref, right_ref in zip(lefts, rights):
            total = total + dot(left_ref[pl.ds(place * rows, rows), :], right_ref[...], ((1,), (1,)))
        out_ref[...] = total


def product(at, lefts, rights):
    count, width = lefts[0].shape[0], rights[0].shape[0]
    block = 256
    shape = jax.ShapeDtypeStruct((count // 2, width), jnp.float32)
    return pl.pallas_call(
        functools.partial(product_kernel, parts=len(lefts)),
        grid_spec=pltpu.PrefetchScalarGridSpec(
            num_scalar_prefetch=1,
            grid=(width // block,),
            in_specs=[pl.BlockSpec(v.shape, lambda i, at: (0, 0)) for v in lefts]
            + [pl.BlockSpec((block, v.shape[1]), lambda i, at: (i, 0)) for v in rights],
            out_specs=[pl.BlockSpec((count // 2, block), lambda i, at: (0, i))] * 2,
        ),
        out_shape=[shape, shape],
        name="product",
    )(at.reshape(1), *lefts, *rights)


def unzip(at_ref, in_ref, own_ref, other_ref, *, chans, half, heads):
    even = at_ref[0] == 0
    lane = lax.broadcasted_iota(jnp.int32, (1, 128), 1)
    step_at, bc_at = 2 * chans + 2 * STATE, 2 * chans
    kind = own_ref.dtype

    def emit(low, high, to):
        own_ref[:, to : to + 128] = jnp.where(even, low, high).astype(kind)
        other_ref[:, to : to + 128] = jnp.where(even, high, low).astype(kind)

    for source, starts in ((chans, (0, 2 * half + 384)), (0, (half + 128, 3 * half + 384))):
        for at in range(0, chans // 2, 128):
            a = in_ref[:, source + 2 * at : source + 2 * at + 128].astype(jnp.float32)
            b = in_ref[:, source + 2 * at + 128 : source + 2 * at + 256].astype(jnp.float32)
            low = jnp.where(lane < HEAD_DIM, a, pltpu.roll(b, HEAD_DIM, 1))
            high = jnp.where(lane < HEAD_DIM, pltpu.roll(a, HEAD_DIM, 1), b)
            emit(low, high, starts[at // half] + at % half)
    steps = in_ref[:, step_at : step_at + heads]
    row = lax.broadcasted_iota(jnp.int32, (heads, 128), 0)
    col = lax.broadcasted_iota(jnp.int32, (heads, 128), 1)
    sides = [
        dot(steps, jnp.where((row == 2 * col + side) & (col < heads // 2), 1.0, 0.0).astype(kind), ((1,), (0,)))
        for side in (0, 1)
    ]
    emit(sides[0], sides[1], half)
    bc = in_ref[:, bc_at:step_at]
    own_ref[:, 2 * half + 128 : 2 * half + 384] = bc
    other_ref[:, 2 * half + 128 : 2 * half + 384] = bc


def zipped(at_ref, own1_ref, other1_ref, own2_ref, other2_ref, out_ref, *, chans, half, heads):
    even = at_ref[0] == 0
    lane = lax.broadcasted_iota(jnp.int32, (1, 128), 1)
    bc_at, step_at = 2 * chans, 2 * chans + 2 * STATE
    for target, lead in ((chans, 0), (0, 1)):
        for at in range(0, chans // 2, 128):
            second = at >= half
            to = at % half + lead * (half if second else half + 128)
            own_ref, other_ref = (own2_ref, other2_ref) if second else (own1_ref, other1_ref)
            own, other = own_ref[:, to : to + 128], other_ref[:, to : to + 128]
            low, high = jnp.where(even, own, other), jnp.where(even, other, own)
            out_ref[:, target + 2 * at : target + 2 * at + 128] = jnp.where(
                lane < HEAD_DIM, low, pltpu.roll(high, HEAD_DIM, 1)
            )
            out_ref[:, target + 2 * at + 128 : target + 2 * at + 256] = jnp.where(
                lane < HEAD_DIM, pltpu.roll(low, HEAD_DIM, 1), high
            )
    cols = slice(2 * half + 128, 2 * half + 384)
    out_ref[:, bc_at:step_at] = own1_ref[:, cols] + other1_ref[:, cols]
    row = lax.broadcasted_iota(jnp.int32, (128, heads), 0)
    col = lax.broadcasted_iota(jnp.int32, (128, heads), 1)
    own, other = own1_ref[:, half : half + 128], other1_ref[:, half : half + 128]
    total = 0.0
    for side, values in ((0, jnp.where(even, own, other)), (1, jnp.where(even, other, own))):
        choice = jnp.where((col == 2 * row + side) & (row < heads // 2), 1.0, 0.0)
        total = total + lax.dot_general(
            values, choice, (((1,), (0,)), ((), ())), precision=PRECISE, preferred_element_type=jnp.float32
        )
    out_ref[:, step_at : step_at + heads] = total


def scalar():
    return pl.BlockSpec(memory_space=pltpu.SMEM)


def full():
    return pl.BlockSpec(memory_space=pltpu.VMEM)


def unzip_columns(at, rows, half):
    shape = jax.ShapeDtypeStruct((rows.shape[0], 4 * half + 384), rows.dtype)
    return pl.pallas_call(
        functools.partial(unzip, chans=D_INNER, half=half, heads=HEADS),
        in_specs=[scalar(), full()],
        out_specs=[full(), full()],
        out_shape=[shape, shape],
        name="unzip",
    )(at.reshape(1), rows)


def zip_columns(at, own1, other1, own2, other2, half):
    return pl.pallas_call(
        functools.partial(zipped, chans=D_INNER, half=half, heads=HEADS),
        in_specs=[scalar()] + [full()] * 4,
        out_specs=full(),
        out_shape=jax.ShapeDtypeStruct((own1.shape[0], D_INNER + CONV_CH + HEADS), jnp.float32),
        name="zip",
    )(at.reshape(1), own1, other1, own2, other2)


def rms_scale(values, gain):
    return values * lax.rsqrt(jnp.mean(values * values, axis=-1, keepdims=True) + EPS) * gain


def conv_act(values, conv_weight, conv_bias):
    count = values.shape[0]
    extended = jnp.concatenate([jnp.zeros((CONVK - 1, values.shape[1]), jnp.float32), values], axis=0)
    summed = conv_bias[None, :] + conv_weight[0][None, :] * extended[0:count]
    for offset in range(1, CONVK):
        summed = summed + conv_weight[offset][None, :] * extended[offset : offset + count]
    return jax.nn.silu(summed)


class Split:
    def __init__(self, out_rows, d_model):
        self.peers = lax.axis_size("seq")
        self.at = lax.axis_index("seq")
        blocks = lax.axis_size("dp")
        self.staged = out_rows == HEAD_DIM and blocks * HEAD_DIM == d_model and blocks % PLANE == 0 and self.peers == 2
        self.outer = blocks if self.staged else 1

    def view(self, v):
        return v.reshape(v.shape[:-1] + (self.outer, self.peers, v.shape[-1] // (self.outer * self.peers)))

    def own(self, v, at=None):
        part = pick(self.view(v), self.at if at is None else at, v.ndim)
        return part.reshape(v.shape[:-1] + (-1,))

    def place(self, whole, part, at=None):
        view = self.view(whole)
        piece = part.reshape(view.shape[:-2] + view.shape[-1:])
        return put(view, piece, self.at if at is None else at, whole.ndim).reshape(whole.shape)

    def placed(self, part):
        return self.place(jnp.zeros(part.shape[:-1] + (part.shape[-1] * self.peers,), part.dtype), part)

    def exchange(self, piece_for):
        pieces = [(self.at, piece_for(self.at))]
        for steps in range(1, self.peers):
            sent = piece_for((self.at + steps) % self.peers)
            pieces.append(((self.at - steps) % self.peers, seq_shift(sent, steps)))
        return pieces

    def scatter_rows(self, x):
        rows = x.reshape((self.peers, x.shape[0] // self.peers) + x.shape[1:])
        total = 0.0
        for _, piece in self.exchange(lambda to: pick(rows, to, 0)):
            total = total + piece
        return total


def per_device(
    hidden_in, upstream, in_weight, out_weight, norm_gain, conv_weight, conv_bias,
    step_bias, log_rate, skip_weight, gate_gain,
):
    bf = jnp.bfloat16
    split = Split(*out_weight.shape)
    peers, at = split.peers, split.at
    stream, grad_top = hidden_in[0], upstream[0]
    own_rows, d_model = stream.shape
    count = own_rows * peers
    groups = count // GROUP
    heads = HEADS // peers
    inner = D_INNER // peers
    half_heads = heads // 2
    half = inner // 2
    lanes = -(-heads // 128) * 128

    def in_columns(rows):
        x = split.own(rows[:, D_INNER : 2 * D_INNER])
        gate = split.own(rows[:, :D_INNER])
        bc = rows[:, 2 * D_INNER : D_INNER + CONV_CH]
        steps = split.own(rows[:, D_INNER + CONV_CH :])
        blank = jnp.zeros((rows.shape[0], lanes - heads), rows.dtype)
        return (
            jnp.concatenate([x[:, :half], steps, blank], axis=1),
            jnp.concatenate([gate[:, :half], bc], axis=1),
            x[:, half:],
            gate[:, half:],
        )

    first_cut = half + lanes
    first_width = first_cut + half + 2 * STATE
    if split.staged:
        own, other = unzip_columns(at, in_weight, half)
        arrived = seq_shift(other, 1)
        block = put(put(jnp.zeros((peers,) + own.shape, bf), own, at, 0), arrived, 1 - at, 0)
        block = block.reshape(-1, block.shape[-1])

    normed_own = rms_scale(stream, norm_gain).astype(bf)
    both = jnp.concatenate([normed_own, grad_top.astype(bf)], axis=1)
    tokens = jnp.zeros((peers,) + both.shape, bf)
    arrived_tokens = split.exchange(lambda to: both)
    for origin, part in arrived_tokens:
        tokens = put(tokens, part, origin, 0)
    tokens = tokens.reshape(count, -1)
    normed, top = tokens[:, :d_model], tokens[:, d_model:]

    if split.staged:
        out_left, out_right, gate = gathered(out_weight, d_model // 2, None)
        x_first, gate_first, gate = gathered(block[:, :first_width], first_cut, gate)
        x_second, gate_second, _ = gathered(block[:, first_width:], half, gate)
    else:
        in_all = lax.all_gather(in_weight, ("dp", "seq"), axis=0, tiled=True)
        x_first, gate_first, x_second, gate_second = in_columns(in_all)
        out_all = split.own(lax.all_gather(out_weight, ("dp", "seq"), axis=0, tiled=True).T).T
        out_left, out_right = out_all[:, : d_model // 2], out_all[:, d_model // 2 :]
    top_left, top_right = top[:, : d_model // 2], top[:, d_model // 2 :]

    own_bias = split.own(step_bias)
    rates = -jnp.exp(split.own(log_rate))
    own_gain = split.own(gate_gain)
    conv_x = split.own(conv_weight[:, :D_INNER])
    params = jnp.concatenate(
        [
            conv_x,
            split.own(conv_bias[:D_INNER])[None],
            jnp.repeat(split.own(skip_weight), HEAD_DIM)[None],
            own_gain[None],
            jnp.zeros((1, inner), jnp.float32),
        ],
        axis=0,
    )
    tri = (jnp.arange(GROUP)[:, None] >= jnp.arange(GROUP)[None, :]).astype(jnp.float32)

    step_raw = dot(normed, x_first[:, half:], ((1,), (0,)))
    step_in = step_raw + jnp.pad(own_bias, (0, lanes - heads))[None, :]
    all_rates = jnp.pad(rates, (0, lanes - heads))[None, :]
    deltas = jax.nn.softplus(step_in)
    cum = jnp.einsum(
        "ts,gsh->gth", tri, (deltas * all_rates).reshape(groups, GROUP, lanes), precision=PRECISE
    ).reshape(count, lanes)
    cum_t = cum.T
    bc_in = dot(normed, gate_first[:, half:], ((1,), (0,))).astype(bf)
    bc_params = jnp.concatenate(
        [conv_weight[:, D_INNER:], conv_bias[None, D_INNER:], jnp.zeros((3, 2 * STATE), jnp.float32)], axis=0
    )
    bc = conv_act(bc_in.astype(jnp.float32), conv_weight[:, D_INNER:], conv_bias[D_INNER:])

    pulled = dot(top_left, out_left, ((1,), (1,))) + dot(top_right, out_right, ((1,), (1,)))
    saved = []
    for part, (w_x, w_gate) in enumerate(((x_first, gate_first), (x_second, gate_second))):
        saved.append(mix_forward(part, half_heads, normed, w_x, w_gate, pulled, bc, deltas, cum, cum_t, params))
    sums = saved[0][4] + saved[1][4]
    sums = jnp.stack([jnp.sum(sums[:, :128], axis=1), jnp.sum(sums[:, 128:], axis=1)])
    sums = seq_sum(sums)
    scale = lax.rsqrt(sums[0] / D_INNER + EPS)
    lean = sums[1] * scale * scale * scale / D_INNER
    norms = jnp.pad(jnp.stack([scale, lean], axis=1), ((0, 0), (0, 126)))

    normed_out = jnp.concatenate(
        [
            (mixed * jax.nn.silu(gate) * scale[:, None] * own_gain[None, part * half : (part + 1) * half]).astype(bf)
            for part, (_, gate, mixed, _, _) in enumerate(saved)
        ],
        axis=1,
    )
    if split.staged:
        out_halves = halves(normed_out, (top_left, top_right), 2)
        out_parts = column_sum(*plane_sum(*out_halves, 2))

    w_sides = ((x_first, gate_first), (x_second, gate_second))
    gx1, ggate1, *carried, gpar1 = mix_backward(
        1, half_heads, *saved[1][:4], pulled, norms, bc, deltas, cum, cum_t, params
    )
    if split.staged:
        second_halves = halves(normed, (gx1, ggate1), 1)
        second_parts = column_sum(*plane_sum(*second_halves, 1))
    gx0, ggate0, _, _, _, gpar0, gstep, gbc, gheads, gbc_par = mix_backward(
        0, half_heads, *saved[0][:4], pulled, norms, bc, deltas, cum, cum_t, params,
        *carried, bc_in, step_in, jnp.broadcast_to(all_rates, (8, lanes)), bc_params,
    )
    grad_par = jnp.concatenate([gpar0, gpar1], axis=1)
    grads = (jnp.concatenate([gx0, gstep], axis=1), jnp.concatenate([ggate0, gbc], axis=1), gx1, ggate1)
    if split.staged:
        left_halves = halves(normed, (gx0, gstep), 2)
        right_halves = halves(normed, (ggate0, gbc), 1)
        left, near_left = plane_sum(*left_halves, 2)
        right, near_right = plane_sum(*right_halves, 1)
        gate = (near_left, near_right)
        first_parts = column_sum(jnp.concatenate([left, right], axis=-1), gate)
        kept, sent = product(at, grads, w_sides[0] + w_sides[1])
        grad_normed = kept + seq_shift(sent, 1)
    else:
        grad_normed = 0.0
        for side, weight in zip(grads, w_sides[0] + w_sides[1]):
            grad_normed = grad_normed + dot(side, weight, ((1,), (1,)))
        grad_normed = split.scatter_rows(grad_normed)

    def block_rows(to):
        rows = lax.dynamic_slice_in_dim(normed_out, to * own_rows, own_rows, 0)
        return jnp.concatenate([dot(rows, side, ((1,), (0,))) for side in (out_left, out_right)], axis=1)

    block_out = stream
    for _, piece in split.exchange(block_rows):
        block_out = block_out + piece
    _, norm_back = jax.vjp(rms_scale, stream, norm_gain)
    grad_stream, grad_norm_gain = norm_back(grad_normed)

    small = [
        jnp.concatenate([split.placed(grad_par[:CONVK]), gbc_par[:CONVK]], axis=1),
        jnp.concatenate([split.placed(grad_par[CONVK]), gbc_par[CONVK]]),
        split.placed(gheads[0, :heads]),
        split.placed(gheads[1, :heads]),
        split.placed(jnp.sum(grad_par[CONVK + 1].reshape(heads, HEAD_DIM), axis=1)),
        split.placed(grad_par[CONVK + 2]),
        grad_norm_gain,
    ]
    packed = everywhere_sum(jnp.concatenate([v.reshape(-1) for v in small]))
    summed, offset = [], 0
    for v in small:
        summed.append(packed[offset : offset + v.size].reshape(v.shape))
        offset += v.size

    if split.staged:
        out_share = arrived_sum(out_parts, gate)
        pairs = []
        for parts, after in ((first_parts, None), (second_parts, gate)):
            share = arrived_sum(parts, after)
            pair = share.reshape(peers, -1, share.shape[-1])
            pairs += [pick(pair, at, 0), seq_shift(pick(pair, 1 - at, 0), 1)]
        in_share = zip_columns(at, *pairs, half)
    else:
        empty = jnp.zeros((d_model, D_INNER), jnp.float32)
        x_low, gate_low, x_high, gate_high = (dot(normed, side, ((0,), (0,))) for side in grads)
        in_share = jnp.concatenate(
            [
                split.place(empty, jnp.concatenate([gate_low[:, :half], gate_high], axis=1)),
                split.place(empty, jnp.concatenate([x_low[:, :half], x_high], axis=1)),
                gate_low[:, half:],
                split.placed(x_low[:, half : half + heads]),
            ],
            axis=1,
        )
        in_share = lax.psum_scatter(in_share, ("dp", "seq"), scatter_dimension=0, tiled=True)
        grad_out = dot(normed_out, top, ((0,), (0,)))
        out_share = lax.psum_scatter(
            split.placed(grad_out.T).T, ("dp", "seq"), scatter_dimension=0, tiled=True
        )

    return (
        block_out[None], (grad_top + grad_stream)[None], in_share, out_share, summed[6],
        summed[0], summed[1], summed[2], summed[3], summed[4], summed[5],
    )


def solution(mesh):
    tokens, rows, whole = P("dp", "seq", None), P(("dp", "seq"), None), P()
    return jax.shard_map(
        per_device,
        mesh=mesh,
        in_specs=(tokens, tokens, rows, rows) + (whole,) * 7,
        out_specs=(tokens, tokens, rows, rows) + (whole,) * 7,
        check_vma=False,
    )
```

```python
import functools

import jax
import jax.numpy as jnp
from jax import lax
from jax.experimental import pallas as pl
from jax.experimental.pallas import tpu as pltpu
from jax.sharding import PartitionSpec as P


D_INNER = 2048
HEADS = 32
HEAD_DIM = 64
STATE = 128
CONVK = 4
GROUP = 256
CONV_CH = 2304
EPS = 1e-05
PRECISE = lax.Precision.HIGHEST
PAD = 8
PLANE = 4
NEVER = -1e30


def pick(x, index, axis):
    return lax.dynamic_index_in_dim(x, index, axis, keepdims=False)


def put(buffer, piece, index, axis):
    return lax.dynamic_update_index_in_dim(buffer, piece, index, axis)


def swapped(x, bit):
    return lax.ppermute(x, "dp", [(i, i ^ bit) for i in range(lax.axis_size("dp"))])


def column_shift(x, steps):
    size = lax.axis_size("dp")
    return lax.ppermute(x, "dp", [(i, (i + PLANE * steps) % size) for i in range(size)])


def seq_shift(x, steps):
    size = lax.axis_size("seq")
    return lax.ppermute(x, "seq", [(i, (i + steps) % size) for i in range(size)])


def seq_sum(x):
    size = lax.axis_size("seq")
    if size == 2:
        return x + seq_shift(x, 1)
    return lax.psum(x, "seq")


def dp_sum(x):
    size = lax.axis_size("dp")
    if size & (size - 1):
        return lax.psum(x, "dp")
    bit = size // 2
    while bit:
        x = x + swapped(x, bit)
        bit //= 2
    return x


def place_kernel(at_ref, *refs, moves, inputs):
    ins, outs, sems = refs[:inputs], refs[inputs:-1], refs[-1]
    copies = []
    for n, (source, columns, target, where) in enumerate(moves):
        src = ins[source] if columns is None else ins[source].at[..., slice(*columns)]
        copies.append(pltpu.make_async_copy(src, outs[target].at[where(at_ref)], sems.at[n]))
    for copy in copies:
        copy.start()
    for copy in copies:
        copy.wait()


def place(at, pieces, shapes, moves):
    return pl.pallas_call(
        functools.partial(place_kernel, moves=moves, inputs=len(pieces)),
        in_specs=[scalar()] + [pl.BlockSpec(memory_space=pl.ANY)] * len(pieces),
        out_specs=[pl.BlockSpec(memory_space=pl.ANY)] * len(shapes),
        out_shape=[jax.ShapeDtypeStruct(shape, pieces[0].dtype) for shape in shapes],
        scratch_shapes=[pltpu.SemaphoreType.DMA((len(moves),))],
    )(at, *pieces)


def gathered(block, cut, gate):
    spot = lax.axis_index("dp")
    at = jnp.stack([spot // PLANE, spot % PLANE // 2, spot % 2])
    height = lax.axis_size("dp") // PLANE
    rows, width = block.shape
    rest = width - cut
    moved = [column_shift(block, steps) for steps in range(1, height)]
    if gate is not None:
        moved, _ = lax.optimization_barrier((moved, gate))
    moves = []
    for k in range(height):
        slot = lambda ref, k=k: (lax.rem(ref[0] + (height - k), height),)
        moves += [(k, (0, cut), 0, slot), (k, (cut, width), 1, slot)]
    left, right = place(at, [block] + moved, [(height, rows, cut), (height, rows, rest)], moves)
    left_near, right_near = swapped(left, 1), swapped(right, 2)
    later = (left_near, right_near)
    every = slice(None)
    left, right = place(
        at,
        [left, left_near, right, right_near],
        [(height, 2, rows, cut), (height, 2, rows, rest)],
        [
            (0, None, 0, lambda ref: (every, ref[2])),
            (1, None, 0, lambda ref: (every, 1 - ref[2])),
            (2, None, 1, lambda ref: (every, ref[1])),
            (3, None, 1, lambda ref: (every, 1 - ref[1])),
        ],
    )
    left_far, right_far = swapped(left, 2), swapped(right, 1)
    left, right = place(
        at,
        [left, left_far, right, right_far],
        [(height, 2, 2, rows, cut), (height, 2, 2, rows, rest)],
        [
            (0, None, 0, lambda ref: (every, ref[1])),
            (1, None, 0, lambda ref: (every, 1 - ref[1])),
            (2, None, 1, lambda ref: (every, every, ref[2])),
            (3, None, 1, lambda ref: (every, every, 1 - ref[2])),
        ],
    )
    return left.reshape(-1, cut), right.reshape(-1, rest), later


def plane_sum(sent, kept, bit):
    at = lax.axis_index("dp")
    height = lax.axis_size("dp") // PLANE
    wide = jnp.float32
    near_bit = 3 - bit
    place = at % PLANE // near_bit % 2
    far = swapped(sent, bit)
    half = (kept.astype(wide) + far.astype(wide)).reshape(height, 2, -1, kept.shape[-1])
    near = swapped(pick(half, 1 - place, 1).astype(sent.dtype), near_bit)
    return pick(half, place, 1) + near.astype(wide), near


def column_sum(column, gate):
    height = lax.axis_size("dp") // PLANE
    tall = lax.axis_index("dp") // PLANE
    sent = column.astype(jnp.bfloat16)
    moved = [column_shift(pick(sent, (tall + k) % height, 0), k) for k in range(1, height)]
    return moved, pick(column, tall, 0), gate


def arrived_sum(parts, gate):
    moved, total, _ = parts
    if gate is not None:
        moved, _ = lax.optimization_barrier((moved, gate))
    for piece in moved:
        total = total + piece.astype(jnp.float32)
    return total


def dot(a, b, over):
    return lax.dot_general(a, b, ((over[0], over[1]), ((), ())), preferred_element_type=jnp.float32)


def spread(columns, width):
    lane = lax.broadcasted_iota(jnp.int32, (1, width), 1)
    out = columns[:, 0:1]
    for head in range(1, width // HEAD_DIM):
        out = jnp.where(lane >= head * HEAD_DIM, columns[:, head : head + 1], out)
    return jnp.broadcast_to(out, (columns.shape[0], width))


def conv_pre(padded_ref, weight, bias, count):
    summed = bias
    for offset in range(CONVK):
        start = PAD - (CONVK - 1) + offset
        summed = summed + weight[offset : offset + 1] * padded_ref[start : start + count, :]
    return summed


def sigmoid(v):
    return 1.0 / (1.0 + jnp.exp(-v))


def causal_mask():
    return lax.broadcasted_iota(jnp.int32, (GROUP, GROUP), 0) >= lax.broadcasted_iota(
        jnp.int32, (GROUP, GROUP), 1
    )


def own_lanes(values, lane):
    return pltpu.roll(values, (values.shape[1] - lane) % values.shape[1], 1)


def folded(values):
    total = values[:, :128]
    for at in range(128, values.shape[1], 128):
        total = total + values[:, at : at + 128]
    return total


def scan_forward(
    normed_ref, wx_ref, wg_ref, pulled_ref, bc_ref, delta_ref, cum_ref, cum_t_ref, par_ref,
    x_ref, gate_ref, mixed_ref, state_ref, sums_ref, pad_ref, *, lead,
):
    count, width = mixed_ref.shape
    bf = jnp.bfloat16
    at = lead + pl.program_id(0) * (width // HEAD_DIM)
    normed = normed_ref[...]
    conv_in = dot(normed, wx_ref[...], ((1,), (0,))).astype(bf)
    gate = dot(normed, wg_ref[...], ((1,), (0,)))
    x_ref[...] = conv_in
    gate_ref[...] = gate
    pad_ref[0:PAD, :] = jnp.zeros((PAD, width), jnp.float32)
    pad_ref[PAD : PAD + count, :] = conv_in.astype(jnp.float32)
    pre = conv_pre(pad_ref, par_ref[0:4, :], par_ref[4:5, :], count)
    acts = pre * sigmoid(pre)
    skip = par_ref[5:6, :]
    causal = causal_mask()
    lane = lax.broadcasted_iota(jnp.int32, (1, 2 * HEAD_DIM), 1)
    state = jnp.zeros((STATE, width), jnp.float32)

    @pl.when(pl.program_id(0) == 0)
    def _():
        sums_ref[...] = jnp.zeros(sums_ref.shape, jnp.float32)

    for group in range(count // GROUP):
        rows = slice(group * GROUP, (group + 1) * GROUP)
        state_ref[group] = state
        b_mat = bc_ref[rows, 0:STATE].astype(bf)
        c_mat = bc_ref[rows, STATE : 2 * STATE].astype(bf)
        inner = dot(c_mat, b_mat, ((1,), (1,)))
        x = acts[rows]
        cum = own_lanes(cum_ref[rows, :], at)
        cum_wide = spread(cum, width)
        last = cum_wide[GROUP - 1 : GROUP, :]
        xd = x * spread(own_lanes(delta_ref[rows, :], at), width)
        xdb = xd.astype(bf)
        y = dot(c_mat, state.astype(bf), ((1,), (0,))) * jnp.exp(cum_wide) + skip * x
        intra = []
        for pair in range(width // (2 * HEAD_DIM)):
            lanes = slice(pair * 2 * HEAD_DIM, (pair + 1) * 2 * HEAD_DIM)
            halves = []
            for head in (2 * pair, 2 * pair + 1):
                gap = jnp.where(causal, cum[:, head : head + 1] - cum_t_ref[pl.ds(at + head, 1), rows], NEVER)
                halves.append(dot((inner * jnp.exp(gap)).astype(bf), xdb[:, lanes], ((1,), (0,))))
            intra.append(jnp.where(lane < HEAD_DIM, halves[0], halves[1]))
        mixed = y + jnp.concatenate(intra, axis=1)
        mixed_ref[rows, :] = mixed
        tail = (xd * jnp.exp(last - cum_wide)).astype(bf)
        state = state * jnp.exp(last) + dot(b_mat, tail, ((0,), (0,)))
        part = gate[rows]
        gated = mixed * part * sigmoid(part)
        sums_ref[rows, 0:128] += folded(gated * gated)
        sums_ref[rows, 128:256] += folded(pulled_ref[rows, :] * par_ref[6:7, :] * gated)


def scan_backward(
    x_ref, gate_ref, mixed_ref, state_ref, pulled_ref, norm_ref, bc_ref, delta_ref, cum_ref, cum_t_ref, par_ref,
    *refs, lead, final,
):
    if final:
        gbc0_ref, gcum0_ref, gdelta0_ref, bcin_ref, step_ref, rate_ref, bcpar_ref = refs[:7]
        refs = refs[7:]
    gx_ref, ggate_ref, gbc_ref, gcum_ref, gdelta_ref, gpar_ref = refs[:6]
    if final:
        gstep_ref, gbcin_ref, gheads_ref, gbcpar_ref = refs[6:10]
    pad_ref, gpad_ref = refs[-2:]
    count, width = x_ref.shape
    bf = jnp.bfloat16
    heads = width // HEAD_DIM
    at = lead + pl.program_id(0) * heads
    pad_ref[0:PAD, :] = jnp.zeros((PAD, width), jnp.float32)
    pad_ref[PAD : PAD + count, :] = x_ref[...].astype(jnp.float32)
    pre = conv_pre(pad_ref, par_ref[0:4, :], par_ref[4:5, :], count)
    sig = sigmoid(pre)
    acts = pre * sig
    slope = sig * (1.0 + pre * (1.0 - sig))
    skip = par_ref[5:6, :]
    gain = par_ref[6:7, :]
    causal = causal_mask()
    lane = lax.broadcasted_iota(jnp.int32, (1, 2 * HEAD_DIM), 1)
    lane_wide = lax.broadcasted_iota(jnp.int32, (1, width), 1) // HEAD_DIM
    lane_all = lax.broadcasted_iota(jnp.int32, (1, 128), 1)
    grad_state = jnp.zeros((STATE, width), jnp.float32)
    gskip = jnp.zeros((1, width), jnp.float32)
    ggain = jnp.zeros((1, width), jnp.float32)

    @pl.when(pl.program_id(0) == 0)
    def _():
        gbc_ref[...] = gbc0_ref[...] if final else jnp.zeros(gbc_ref.shape, jnp.float32)
        gcum_ref[...] = gcum0_ref[...] if final else jnp.zeros(gcum_ref.shape, jnp.float32)
        gdelta_ref[...] = gdelta0_ref[...] if final else jnp.zeros(gdelta_ref.shape, jnp.float32)

    gpad_ref[count : count + PAD, :] = jnp.zeros((PAD, width), jnp.float32)
    for group in reversed(range(count // GROUP)):
        rows = slice(group * GROUP, (group + 1) * GROUP)
        scale, lean = norm_ref[rows, 0:1], norm_ref[rows, 1:2]
        gate, mixed, pulled = gate_ref[rows, :], mixed_ref[rows, :], pulled_ref[rows, :]
        sigma = sigmoid(gate)
        gated = mixed * gate * sigma
        ggain = ggain + jnp.sum(pulled * gated * scale, axis=0, keepdims=True)
        ggated = pulled * gain * scale - gated * lean
        ggate_ref[rows, :] = (ggated * mixed * sigma * (1.0 + gate * (1.0 - sigma))).astype(bf)
        gy = ggated * gate * sigma
        gyb = gy.astype(bf)
        b_mat = bc_ref[rows, 0:STATE].astype(bf)
        c_mat = bc_ref[rows, STATE : 2 * STATE].astype(bf)
        inner = dot(c_mat, b_mat, ((1,), (1,)))
        x = acts[rows]
        cum = own_lanes(cum_ref[rows, :], at)
        cum_wide = spread(cum, width)
        last = cum_wide[GROUP - 1 : GROUP, :]
        decay = jnp.exp(last)
        delta = spread(own_lanes(delta_ref[rows, :], at), width)
        xd = x * delta
        xdb = xd.astype(bf)
        tail = jnp.exp(last - cum_wide)
        state = state_ref[group]
        y = mixed - skip * x
        gye = (gy * jnp.exp(cum_wide)).astype(bf)
        gc = dot(gye, state.astype(bf), ((1,), (1,)))
        gsb = grad_state.astype(bf)
        gxd_tail = dot(b_mat, gsb, ((1,), (0,))) * tail
        gb = dot((xd * tail).astype(bf), gsb, ((1,), (1,)))
        xdf = xdb.astype(jnp.float32)
        glast = jnp.sum(xdf * gxd_tail, axis=0, keepdims=True) + decay * jnp.sum(
            grad_state * state, axis=0, keepdims=True
        )
        grad_state = grad_state * decay + dot(c_mat, gye, ((0,), (0,)))
        ginner = jnp.zeros((GROUP, GROUP), jnp.float32)
        intra = []
        for pair in range(width // (2 * HEAD_DIM)):
            lanes = slice(pair * 2 * HEAD_DIM, (pair + 1) * 2 * HEAD_DIM)
            halves = []
            for side in (0, 1):
                head = 2 * pair + side
                gap = jnp.where(causal, cum[:, head : head + 1] - cum_t_ref[pl.ds(at + head, 1), rows], NEVER)
                fall = jnp.exp(gap)
                weights = (inner * fall).astype(bf)
                own = (lane < HEAD_DIM) if side == 0 else (lane >= HEAD_DIM)
                gyh = jnp.where(own, gy[:, lanes], 0.0).astype(bf)
                ginner = ginner + dot(gyh, xdb[:, lanes], ((1,), (1,))) * fall
                halves.append(dot(weights, gyb[:, lanes], ((0,), (0,))))
            intra.append(jnp.where(lane < HEAD_DIM, halves[0], halves[1]))
        gxd = jnp.concatenate(intra, axis=1) + gxd_tail
        gib = ginner.astype(bf)
        gbc_ref[rows, 0:STATE] += gb + dot(gib, c_mat, ((0,), (0,)))
        gbc_ref[rows, STATE : 2 * STATE] += gc + dot(gib, b_mat, ((1,), (0,)))
        moved = gyb.astype(jnp.float32) * y - xdf * gxd
        drawn = x * gxd
        at_end = lax.broadcasted_iota(jnp.int32, (GROUP, 1), 0) == GROUP - 1
        cums = jnp.zeros((GROUP, 128), jnp.float32)
        draws = jnp.zeros((GROUP, 128), jnp.float32)
        for head in range(heads):
            mine = lane_wide == head
            here = jnp.sum(jnp.where(mine, moved, 0.0), axis=1, keepdims=True)
            end = jnp.sum(jnp.where(mine, glast, 0.0), axis=1, keepdims=True)
            place = lane_all == at + head
            cums = jnp.where(place, here + jnp.where(at_end, end, 0.0), cums)
            draws = jnp.where(place, jnp.sum(jnp.where(mine, drawn, 0.0), axis=1, keepdims=True), draws)
        gcum_ref[rows, :] += cums
        gdelta_ref[rows, :] += draws
        gskip = gskip + jnp.sum(gy * x, axis=0, keepdims=True)
        gpad_ref[rows, :] = (gxd * delta + skip * gy) * slope[rows]
    gpre = gpad_ref[0:count, :]
    total = jnp.zeros((count, width), jnp.float32)
    for offset in range(CONVK):
        ahead = CONVK - 1 - offset
        total = total + par_ref[offset : offset + 1, :] * gpad_ref[ahead : ahead + count, :]
        start = PAD - ahead
        gpar_ref[offset : offset + 1, :] = jnp.sum(
            gpre * pad_ref[start : start + count, :], axis=0, keepdims=True
        )
    gx_ref[...] = total.astype(bf)
    gpar_ref[4:5, :] = jnp.sum(gpre, axis=0, keepdims=True)
    gpar_ref[5:6, :] = gskip
    gpar_ref[6:7, :] = ggain
    gpar_ref[7:8, :] = jnp.zeros((1, width), jnp.float32)
    if not final:
        return

    @pl.when(pl.program_id(0) == pl.num_programs(0) - 1)
    def _():
        below = jnp.where(causal, 1.0, 0.0)
        step_sum = jnp.zeros((1, 128), jnp.float32)
        rate_sum = jnp.zeros((1, 128), jnp.float32)
        for group in range(count // GROUP):
            rows = slice(group * GROUP, (group + 1) * GROUP)
            ga = lax.dot_general(
                below, gcum_ref[rows, :], (((0,), (0,)), ((), ())), precision=PRECISE,
                preferred_element_type=jnp.float32,
            )
            gstep = (ga * rate_ref[0:1, :] + gdelta_ref[rows, :]) * sigmoid(step_ref[rows, :])
            gstep_ref[rows, :] = gstep.astype(bf)
            step_sum = step_sum + jnp.sum(gstep, axis=0, keepdims=True)
            rate_sum = rate_sum + jnp.sum(ga * delta_ref[rows, :], axis=0, keepdims=True)
        gheads_ref[0:1, :] = step_sum
        gheads_ref[1:2, :] = rate_sum * rate_ref[0:1, :]
        gheads_ref[2:8, :] = jnp.zeros((6, 128), jnp.float32)
        for lanes in range(0, 2 * STATE, width):
            cols = slice(lanes, lanes + width)
            pad_ref[PAD : PAD + count, :] = bcin_ref[:, cols].astype(jnp.float32)
            pre = conv_pre(pad_ref, bcpar_ref[0:4, cols], bcpar_ref[4:5, cols], count)
            sig = sigmoid(pre)
            gpre = gbc_ref[:, cols] * sig * (1.0 + pre * (1.0 - sig))
            gpad_ref[0:count, :] = gpre
            total = jnp.zeros((count, width), jnp.float32)
            for offset in range(CONVK):
                ahead = CONVK - 1 - offset
                total = total + bcpar_ref[offset : offset + 1, cols] * gpad_ref[ahead : ahead + count, :]
                start = PAD - ahead
                gbcpar_ref[offset : offset + 1, cols] = jnp.sum(
                    gpre * pad_ref[start : start + count, :], axis=0, keepdims=True
                )
            gbcin_ref[:, cols] = total.astype(bf)
            gbcpar_ref[4:5, cols] = jnp.sum(gpre, axis=0, keepdims=True)
            gbcpar_ref[5:8, cols] = jnp.zeros((3, width), jnp.float32)


def head_block(heads):
    return 4 if heads % 4 == 0 else 2


def fixed(shape):
    return pl.BlockSpec(shape, lambda i: (0,) * len(shape))


def moving(rows, width, at=0):
    return pl.BlockSpec((rows, width), lambda i: (0, i + at))


def mix_forward(part, heads, normed, w_x, w_gate, pulled, bc, delta, cum, cum_t, params):
    count, d_model = normed.shape
    block = head_block(heads)
    width = block * HEAD_DIM
    lead = heads // block * part
    groups = count // GROUP
    whole = heads * HEAD_DIM
    return pl.pallas_call(
        functools.partial(scan_forward, lead=heads * part),
        grid=(heads // block,),
        in_specs=[
            fixed((count, d_model)),
            moving(d_model, width),
            moving(d_model, width),
            moving(count, width, lead),
            fixed((count, 2 * STATE)),
            fixed((count, 128)),
            fixed((count, 128)),
            fixed((128, count)),
            moving(8, width, lead),
        ],
        out_specs=[
            moving(count, width),
            moving(count, width),
            moving(count, width),
            pl.BlockSpec((groups, STATE, width), lambda i: (0, 0, i)),
            fixed((count, 256)),
        ],
        out_shape=[
            jax.ShapeDtypeStruct((count, whole), jnp.bfloat16),
            jax.ShapeDtypeStruct((count, whole), jnp.float32),
            jax.ShapeDtypeStruct((count, whole), jnp.float32),
            jax.ShapeDtypeStruct((groups, STATE, whole), jnp.float32),
            jax.ShapeDtypeStruct((count, 256), jnp.float32),
        ],
        scratch_shapes=[pltpu.VMEM((count + PAD, width), jnp.float32)],
        name="scan",
    )(normed, w_x, w_gate, pulled, bc, delta, cum, cum_t, params)


def mix_backward(part, heads, x, gate, mixed, states, pulled, norms, bc, delta, cum, cum_t, params, *rest):
    count = x.shape[0]
    block = head_block(heads)
    width = block * HEAD_DIM
    lead = heads // block * part
    groups = count // GROUP
    whole = heads * HEAD_DIM
    f32, bf = jnp.float32, jnp.bfloat16
    in_specs = [
        moving(count, width),
        moving(count, width),
        moving(count, width),
        pl.BlockSpec((groups, STATE, width), lambda i: (0, 0, i)),
        moving(count, width, lead),
        fixed((count, 128)),
        fixed((count, 2 * STATE)),
        fixed((count, 128)),
        fixed((count, 128)),
        fixed((128, count)),
        moving(8, width, lead),
    ]
    out_specs = [moving(count, width)] * 2 + [fixed((count, 2 * STATE))] + [fixed((count, 128))] * 2
    out_specs += [moving(8, width)]
    shapes = [((count, whole), bf)] * 2 + [((count, 2 * STATE), f32)] + [((count, 128), f32)] * 2
    shapes += [((8, whole), f32)]
    if rest:
        in_specs += [fixed(v.shape) for v in rest]
        extra = [((count, 128), bf), ((count, 2 * STATE), bf), ((8, 128), f32), ((8, 2 * STATE), f32)]
        out_specs += [fixed(shape) for shape, _ in extra]
        shapes += extra
    return pl.pallas_call(
        functools.partial(scan_backward, lead=heads * part, final=bool(rest)),
        grid=(heads // block,),
        in_specs=in_specs,
        out_specs=out_specs,
        out_shape=[jax.ShapeDtypeStruct(*shape) for shape in shapes],
        scratch_shapes=[pltpu.VMEM((count + PAD, width), f32)] * 2,
        name="unscan",
    )(x, gate, mixed, states, pulled, norms, bc, delta, cum, cum_t, params, *rest)


def halves_kernel(at_ref, *refs, parts, tall):
    left, rights, (sent_ref, kept_ref) = refs[:-parts - 2], refs[-parts - 2 : -2], refs[-2:]
    low = at_ref[0] == 0
    lanes = 0
    for right_ref in rights:
        right = right_ref[...]
        cols = slice(lanes, lanes + right.shape[1])
        lanes += right.shape[1]
        if tall:
            sent_ref[:, cols] = dot(left[0][...], right, ((0,), (0,))).astype(sent_ref.dtype)
            kept_ref[:, cols] = dot(left[1][...], right, ((0,), (0,))).astype(sent_ref.dtype)
        else:
            rows = dot(left[0][...], right, ((0,), (0,)))
            for y in (0, 1):
                first = rows[128 * y : 128 * y + 64]
                second = rows[128 * y + 64 : 128 * y + 128]
                to = slice(64 * y, 64 * y + 64)
                sent_ref[to, cols] = jnp.where(low, second, first).astype(sent_ref.dtype)
                kept_ref[to, cols] = jnp.where(low, first, second).astype(sent_ref.dtype)


def halves(left, rights, bit):
    count, rows = left.shape
    tall = bit == 2
    at = (lax.axis_index("dp") % PLANE // bit % 2).reshape(1)
    if tall:
        lefts = [
            pl.BlockSpec((count, 128), lambda i, at: (0, 2 * i + 1 - at[0])),
            pl.BlockSpec((count, 128), lambda i, at: (0, 2 * i + at[0])),
        ]
    else:
        lefts = [pl.BlockSpec((count, 256), lambda i, at: (0, i))]
    width = sum(v.shape[1] for v in rights)
    shape = jax.ShapeDtypeStruct((rows // 2, width), jnp.bfloat16)
    return pl.pallas_call(
        functools.partial(halves_kernel, parts=len(rights), tall=tall),
        grid_spec=pltpu.PrefetchScalarGridSpec(
            num_scalar_prefetch=1,
            grid=(rows // 256,),
            in_specs=lefts + [pl.BlockSpec(v.shape, lambda i, at: (0, 0)) for v in rights],
            out_specs=[pl.BlockSpec((128, width), lambda i, at: (i, 0))] * 2,
        ),
        out_shape=[shape, shape],
        name="halves",
    )(at, *([left] * len(lefts)), *rights)


def product_kernel(at_ref, *refs, parts):
    lefts, rights, outs = refs[:parts], refs[parts : 2 * parts], refs[2 * parts :]
    rows = outs[0].shape[0]
    for out_ref, place in ((outs[0], at_ref[0]), (outs[1], 1 - at_ref[0])):
        total = 0.0
        for left_ref, right_ref in zip(lefts, rights):
            total = total + dot(left_ref[pl.ds(place * rows, rows), :], right_ref[...], ((1,), (1,)))
        out_ref[...] = total


def product(at, lefts, rights):
    count, width = lefts[0].shape[0], rights[0][0].shape[0]
    block = 256
    shape = jax.ShapeDtypeStruct((count // 2, width), jnp.float32)
    return pl.pallas_call(
        functools.partial(product_kernel, parts=len(lefts)),
        grid_spec=pltpu.PrefetchScalarGridSpec(
            num_scalar_prefetch=1,
            grid=(width // block,),
            in_specs=[pl.BlockSpec(v.shape, lambda i, at: (0, 0)) for v in lefts]
            + [pl.BlockSpec((block, wide), lambda i, at, n=start // wide: (i, n)) for _, wide, start in rights],
            out_specs=[pl.BlockSpec((count // 2, block), lambda i, at: (0, i))] * 2,
        ),
        out_shape=[shape, shape],
        name="product",
    )(at.reshape(1), *lefts, *(v for v, _, _ in rights))


def unzip(at_ref, in_ref, own_ref, other_ref, *, chans, half, heads):
    even = at_ref[0] == 0
    lane = lax.broadcasted_iota(jnp.int32, (1, 128), 1)
    step_at, bc_at = 2 * chans + 2 * STATE, 2 * chans
    kind = own_ref.dtype

    def emit(low, high, to):
        own_ref[:, to : to + 128] = jnp.where(even, low, high).astype(kind)
        other_ref[:, to : to + 128] = jnp.where(even, high, low).astype(kind)

    for source, starts in ((chans, (0, 2 * half + 384)), (0, (half + 128, 3 * half + 384))):
        for at in range(0, chans // 2, 128):
            a = in_ref[:, source + 2 * at : source + 2 * at + 128].astype(jnp.float32)
            b = in_ref[:, source + 2 * at + 128 : source + 2 * at + 256].astype(jnp.float32)
            low = jnp.where(lane < HEAD_DIM, a, pltpu.roll(b, HEAD_DIM, 1))
            high = jnp.where(lane < HEAD_DIM, pltpu.roll(a, HEAD_DIM, 1), b)
            emit(low, high, starts[at // half] + at % half)
    steps = in_ref[:, step_at : step_at + heads]
    row = lax.broadcasted_iota(jnp.int32, (heads, 128), 0)
    col = lax.broadcasted_iota(jnp.int32, (heads, 128), 1)
    sides = [
        dot(steps, jnp.where((row == 2 * col + side) & (col < heads // 2), 1.0, 0.0).astype(kind), ((1,), (0,)))
        for side in (0, 1)
    ]
    emit(sides[0], sides[1], half)
    bc = in_ref[:, bc_at:step_at]
    own_ref[:, 2 * half + 128 : 2 * half + 384] = bc
    other_ref[:, 2 * half + 128 : 2 * half + 384] = bc


def zipped(at_ref, own1_ref, other1_ref, own2_ref, other2_ref, out_ref, *, chans, half, heads):
    even = at_ref[0] == 0
    lane = lax.broadcasted_iota(jnp.int32, (1, 128), 1)
    bc_at, step_at = 2 * chans, 2 * chans + 2 * STATE
    for target, lead in ((chans, 0), (0, 1)):
        for at in range(0, chans // 2, 128):
            second = at >= half
            to = at % half + lead * (half if second else half + 128)
            own_ref, other_ref = (own2_ref, other2_ref) if second else (own1_ref, other1_ref)
            own, other = own_ref[:, to : to + 128], other_ref[:, to : to + 128]
            low, high = jnp.where(even, own, other), jnp.where(even, other, own)
            out_ref[:, target + 2 * at : target + 2 * at + 128] = jnp.where(
                lane < HEAD_DIM, low, pltpu.roll(high, HEAD_DIM, 1)
            )
            out_ref[:, target + 2 * at + 128 : target + 2 * at + 256] = jnp.where(
                lane < HEAD_DIM, pltpu.roll(low, HEAD_DIM, 1), high
            )
    cols = slice(2 * half + 128, 2 * half + 384)
    out_ref[:, bc_at:step_at] = own1_ref[:, cols] + other1_ref[:, cols]
    row = lax.broadcasted_iota(jnp.int32, (128, heads), 0)
    col = lax.broadcasted_iota(jnp.int32, (128, heads), 1)
    own, other = own1_ref[:, half : half + 128], other1_ref[:, half : half + 128]
    total = 0.0
    for side, values in ((0, jnp.where(even, own, other)), (1, jnp.where(even, other, own))):
        choice = jnp.where((col == 2 * row + side) & (row < heads // 2), 1.0, 0.0)
        total = total + lax.dot_general(
            values, choice, (((1,), (0,)), ((), ())), precision=PRECISE, preferred_element_type=jnp.float32
        )
    out_ref[:, step_at : step_at + heads] = total


def scalar():
    return pl.BlockSpec(memory_space=pltpu.SMEM)


def full():
    return pl.BlockSpec(memory_space=pltpu.VMEM)


def unzip_columns(at, rows, half):
    shape = jax.ShapeDtypeStruct((rows.shape[0], 4 * half + 384), rows.dtype)
    return pl.pallas_call(
        functools.partial(unzip, chans=D_INNER, half=half, heads=HEADS),
        in_specs=[scalar(), full()],
        out_specs=[full(), full()],
        out_shape=[shape, shape],
        name="unzip",
    )(at.reshape(1), rows)


def zip_columns(at, own1, other1, own2, other2, half):
    return pl.pallas_call(
        functools.partial(zipped, chans=D_INNER, half=half, heads=HEADS),
        in_specs=[scalar()] + [full()] * 4,
        out_specs=full(),
        out_shape=jax.ShapeDtypeStruct((own1.shape[0], D_INNER + CONV_CH + HEADS), jnp.float32),
        name="zip",
    )(at.reshape(1), own1, other1, own2, other2)


def rms_scale(values, gain):
    return values * lax.rsqrt(jnp.mean(values * values, axis=-1, keepdims=True) + EPS) * gain


def conv_act(values, conv_weight, conv_bias):
    count = values.shape[0]
    extended = jnp.concatenate([jnp.zeros((CONVK - 1, values.shape[1]), jnp.float32), values], axis=0)
    summed = conv_bias[None, :] + conv_weight[0][None, :] * extended[0:count]
    for offset in range(1, CONVK):
        summed = summed + conv_weight[offset][None, :] * extended[offset : offset + count]
    return jax.nn.silu(summed)


class Split:
    def __init__(self, out_rows, d_model):
        self.peers = lax.axis_size("seq")
        self.at = lax.axis_index("seq")
        blocks = lax.axis_size("dp")
        self.staged = out_rows == HEAD_DIM and blocks * HEAD_DIM == d_model and blocks % PLANE == 0 and self.peers == 2
        self.outer = blocks if self.staged else 1

    def view(self, v):
        return v.reshape(v.shape[:-1] + (self.outer, self.peers, v.shape[-1] // (self.outer * self.peers)))

    def own(self, v, at=None):
        part = pick(self.view(v), self.at if at is None else at, v.ndim)
        return part.reshape(v.shape[:-1] + (-1,))

    def place(self, whole, part, at=None):
        view = self.view(whole)
        piece = part.reshape(view.shape[:-2] + view.shape[-1:])
        return put(view, piece, self.at if at is None else at, whole.ndim).reshape(whole.shape)

    def placed(self, part):
        return self.place(jnp.zeros(part.shape[:-1] + (part.shape[-1] * self.peers,), part.dtype), part)

    def exchange(self, piece_for):
        pieces = [(self.at, piece_for(self.at))]
        for steps in range(1, self.peers):
            sent = piece_for((self.at + steps) % self.peers)
            pieces.append(((self.at - steps) % self.peers, seq_shift(sent, steps)))
        return pieces

    def scatter_rows(self, x):
        rows = x.reshape((self.peers, x.shape[0] // self.peers) + x.shape[1:])
        total = 0.0
        for _, piece in self.exchange(lambda to: pick(rows, to, 0)):
            total = total + piece
        return total


def per_device(
    hidden_in, upstream, in_weight, out_weight, norm_gain, conv_weight, conv_bias,
    step_bias, log_rate, skip_weight, gate_gain,
):
    bf = jnp.bfloat16
    split = Split(*out_weight.shape)
    peers, at = split.peers, split.at
    stream, grad_top = hidden_in[0], upstream[0]
    own_rows, d_model = stream.shape
    count = own_rows * peers
    groups = count // GROUP
    heads = HEADS // peers
    inner = D_INNER // peers
    half_heads = heads // 2
    half = inner // 2
    lanes = -(-heads // 128) * 128

    def in_columns(rows):
        x = split.own(rows[:, D_INNER : 2 * D_INNER])
        gate = split.own(rows[:, :D_INNER])
        bc = rows[:, 2 * D_INNER : D_INNER + CONV_CH]
        steps = split.own(rows[:, D_INNER + CONV_CH :])
        blank = jnp.zeros((rows.shape[0], lanes - heads), rows.dtype)
        return (
            jnp.concatenate([x[:, :half], steps, blank], axis=1),
            jnp.concatenate([gate[:, :half], bc], axis=1),
            x[:, half:],
            gate[:, half:],
        )

    first_cut = half + lanes
    first_width = first_cut + half + 2 * STATE
    if split.staged:
        own, other = unzip_columns(at, in_weight, half)
        arrived = seq_shift(other, 1)
        here = lambda ref: (ref[0],)
        there = lambda ref: (1 - ref[0],)
        total = own.shape[1]
        block_first, block_second = place(
            at.reshape(1),
            [own, arrived],
            [(peers, own.shape[0], first_width), (peers, own.shape[0], total - first_width)],
            [
                (source, columns, target, where)
                for source, where in ((0, here), (1, there))
                for target, columns in ((0, (0, first_width)), (1, (first_width, total)))
            ],
        )
        block_first = block_first.reshape(-1, first_width)
        block_second = block_second.reshape(-1, total - first_width)

    normed_own = rms_scale(stream, norm_gain).astype(bf)
    both = jnp.concatenate([normed_own, grad_top.astype(bf)], axis=1)
    half_model = d_model // 2
    if split.staged:
        arrived = seq_shift(both, 1)
        spans = ((0, d_model), (d_model, d_model + half_model), (d_model + half_model, 2 * d_model))
        normed, top_left, top_right = place(
            at.reshape(1),
            [both, arrived],
            [(peers, own_rows, stop - start) for start, stop in spans],
            [
                (source, span, target, where)
                for source, where in ((0, here), (1, there))
                for target, span in enumerate(spans)
            ],
        )
        normed, top_left, top_right = (v.reshape(count, -1) for v in (normed, top_left, top_right))
    else:
        tokens = jnp.zeros((peers,) + both.shape, bf)
        for origin, part in split.exchange(lambda to: both):
            tokens = put(tokens, part, origin, 0)
        tokens = tokens.reshape(count, -1)
        normed, top = tokens[:, :d_model], tokens[:, d_model:]
        top_left, top_right = top[:, :half_model], top[:, half_model:]

    if split.staged:
        out_left, out_right, gate = gathered(out_weight, d_model // 2, None)
        x_first, gate_first, gate = gathered(block_first, first_cut, gate)
        x_second, gate_second, _ = gathered(block_second, half, gate)
    else:
        in_all = lax.all_gather(in_weight, ("dp", "seq"), axis=0, tiled=True)
        x_first, gate_first, x_second, gate_second = in_columns(in_all)
        out_all = split.own(lax.all_gather(out_weight, ("dp", "seq"), axis=0, tiled=True).T).T
        out_left, out_right = out_all[:, : d_model // 2], out_all[:, d_model // 2 :]

    own_bias = split.own(step_bias)
    rates = -jnp.exp(split.own(log_rate))
    own_gain = split.own(gate_gain)
    conv_x = split.own(conv_weight[:, :D_INNER])
    params = jnp.concatenate(
        [
            conv_x,
            split.own(conv_bias[:D_INNER])[None],
            jnp.repeat(split.own(skip_weight), HEAD_DIM)[None],
            own_gain[None],
            jnp.zeros((1, inner), jnp.float32),
        ],
        axis=0,
    )
    tri = (jnp.arange(GROUP)[:, None] >= jnp.arange(GROUP)[None, :]).astype(jnp.float32)

    step_raw = dot(normed, x_first[:, half:], ((1,), (0,)))
    step_in = step_raw + jnp.pad(own_bias, (0, lanes - heads))[None, :]
    all_rates = jnp.pad(rates, (0, lanes - heads))[None, :]
    deltas = jax.nn.softplus(step_in)
    cum = jnp.einsum(
        "ts,gsh->gth", tri, (deltas * all_rates).reshape(groups, GROUP, lanes), precision=PRECISE
    ).reshape(count, lanes)
    cum_t = cum.T
    bc_in = dot(normed, gate_first[:, half:], ((1,), (0,))).astype(bf)
    bc_params = jnp.concatenate(
        [conv_weight[:, D_INNER:], conv_bias[None, D_INNER:], jnp.zeros((3, 2 * STATE), jnp.float32)], axis=0
    )
    bc = conv_act(bc_in.astype(jnp.float32), conv_weight[:, D_INNER:], conv_bias[D_INNER:])

    pulled = dot(top_left, out_left, ((1,), (1,))) + dot(top_right, out_right, ((1,), (1,)))
    saved = []
    for part, (w_x, w_gate) in enumerate(((x_first, gate_first), (x_second, gate_second))):
        saved.append(mix_forward(part, half_heads, normed, w_x, w_gate, pulled, bc, deltas, cum, cum_t, params))
    sums = saved[0][4] + saved[1][4]
    sums = jnp.stack([jnp.sum(sums[:, :128], axis=1), jnp.sum(sums[:, 128:], axis=1)])
    sums = seq_sum(sums)
    scale = lax.rsqrt(sums[0] / D_INNER + EPS)
    lean = sums[1] * scale * scale * scale / D_INNER
    norms = jnp.pad(jnp.stack([scale, lean], axis=1), ((0, 0), (0, 126)))

    normed_out = jnp.concatenate(
        [
            (mixed * jax.nn.silu(gate) * scale[:, None] * own_gain[None, part * half : (part + 1) * half]).astype(bf)
            for part, (_, gate, mixed, _, _) in enumerate(saved)
        ],
        axis=1,
    )
    if split.staged:
        out_halves = halves(normed_out, (top_left, top_right), 2)
        out_parts = column_sum(*plane_sum(*out_halves, 2))

    gx1, ggate1, *carried, gpar1 = mix_backward(
        1, half_heads, *saved[1][:4], pulled, norms, bc, deltas, cum, cum_t, params
    )
    if split.staged:
        second_halves = halves(normed, (gx1, ggate1), 1)
        second_parts = column_sum(*plane_sum(*second_halves, 1))
    gx0, ggate0, _, _, _, gpar0, gstep, gbc, gheads, gbc_par = mix_backward(
        0, half_heads, *saved[0][:4], pulled, norms, bc, deltas, cum, cum_t, params,
        *carried, bc_in, step_in, jnp.broadcast_to(all_rates, (8, lanes)), bc_params,
    )
    grads = (gx0, gstep, ggate0, gbc, gx1, ggate1)
    columns = (
        (x_first, half, 0), (x_first, lanes, half), (gate_first, half, 0), (gate_first, 2 * STATE, half),
        (x_second, half, 0), (gate_second, half, 0),
    )
    if split.staged:
        left_halves = halves(normed, (gx0, gstep), 2)
        right_halves = halves(normed, (ggate0, gbc), 1)
        left, near_left = plane_sum(*left_halves, 2)
        right, near_right = plane_sum(*right_halves, 1)
        gate = (near_left, near_right)
        first_parts = column_sum(jnp.concatenate([left, right], axis=-1), gate)
        kept, sent = product(at, grads, columns)
        grad_normed = kept + seq_shift(sent, 1)
    else:
        grad_normed = 0.0
        for side, (weight, width, start) in zip(grads, columns):
            grad_normed = grad_normed + dot(side, weight[:, start : start + width], ((1,), (1,)))
        grad_normed = split.scatter_rows(grad_normed)

    def block_rows(to):
        rows = lax.dynamic_slice_in_dim(normed_out, to * own_rows, own_rows, 0)
        return jnp.concatenate([dot(rows, side, ((1,), (0,))) for side in (out_left, out_right)], axis=1)

    block_out = stream
    for _, piece in split.exchange(block_rows):
        block_out = block_out + piece
    _, norm_back = jax.vjp(rms_scale, stream, norm_gain)
    grad_stream, grad_norm_gain = norm_back(grad_normed)

    small = (gpar0, gpar1, gbc_par, gheads, grad_norm_gain)
    packed = dp_sum(jnp.concatenate([v.reshape(-1, 128) for v in small]))
    other_packed = None
    if split.staged:
        other_packed = seq_shift(packed, 1)
    summed = []
    for source in (packed, other_packed):
        offset, parts = 0, []
        for v in small:
            parts.append(None if source is None else source[offset : offset + v.size // 128].reshape(v.shape))
            offset += v.size // 128
        summed.append(parts)
    mine, theirs = summed
    shared = [None, None]
    for n, k in ((0, 2), (1, 4)):
        shared[n] = mine[k] + theirs[k] if split.staged else lax.psum(mine[k], "seq")

    def spread_rows(pick_row):
        own_row = pick_row(mine)
        if split.staged:
            other_row = pick_row(theirs)
            view = own_row.shape[:-1] + (split.outer, own_row.shape[-1] // split.outer)
            own_row, other_row = own_row.reshape(view), other_row.reshape(view)
            low = jnp.where(at == 0, own_row, other_row)
            high = jnp.where(at == 0, other_row, own_row)
            return jnp.stack([low, high], axis=-2).reshape(view[:-2] + (-1,))
        return lax.psum(split.placed(own_row), "seq")

    rows = spread_rows(lambda v: jnp.concatenate([v[0], v[1]], axis=1))
    head_rows = spread_rows(lambda v: v[3][:, :heads])
    grad_bc_par = shared[0]
    small_out = (
        jnp.concatenate([rows[:CONVK], grad_bc_par[:CONVK]], axis=1),
        jnp.concatenate([rows[CONVK], grad_bc_par[CONVK]]),
        head_rows[0],
        head_rows[1],
        jnp.sum(rows[CONVK + 1].reshape(HEADS, HEAD_DIM), axis=1),
        rows[CONVK + 2],
    )

    if split.staged:
        out_share = arrived_sum(out_parts, gate)
        pairs = []
        for parts, after in ((first_parts, None), (second_parts, gate)):
            share = arrived_sum(parts, after)
            pair = share.reshape(peers, -1, share.shape[-1])
            pairs += [pick(pair, at, 0), seq_shift(pick(pair, 1 - at, 0), 1)]
        in_share = zip_columns(at, *pairs, half)
    else:
        empty = jnp.zeros((d_model, D_INNER), jnp.float32)
        x_low, step_low, gate_low, bc_low, x_high, gate_high = (dot(normed, side, ((0,), (0,))) for side in grads)
        in_share = jnp.concatenate(
            [
                split.place(empty, jnp.concatenate([gate_low, gate_high], axis=1)),
                split.place(empty, jnp.concatenate([x_low, x_high], axis=1)),
                bc_low,
                split.placed(step_low[:, :heads]),
            ],
            axis=1,
        )
        in_share = lax.psum_scatter(in_share, ("dp", "seq"), scatter_dimension=0, tiled=True)
        grad_out = dot(normed_out, jnp.concatenate([top_left, top_right], axis=1), ((0,), (0,)))
        out_share = lax.psum_scatter(
            split.placed(grad_out.T).T, ("dp", "seq"), scatter_dimension=0, tiled=True
        )

    return (
        block_out[None], (grad_top + grad_stream)[None], in_share, out_share, shared[1], *small_out,
    )


def solution(mesh):
    tokens, rows, whole = P("dp", "seq", None), P(("dp", "seq"), None), P()
    return jax.shard_map(
        per_device,
        mesh=mesh,
        in_specs=(tokens, tokens, rows, rows) + (whole,) * 7,
        out_specs=(tokens, tokens, rows, rows) + (whole,) * 7,
        check_vma=False,
    )
```

```python
import functools

import jax
import jax.numpy as jnp
from jax import lax
from jax.experimental import pallas as pl
from jax.experimental.pallas import tpu as pltpu
from jax.sharding import PartitionSpec as P


D_INNER = 2048
HEADS = 32
HEAD_DIM = 64
STATE = 128
CONVK = 4
GROUP = 256
CONV_CH = 2304
EPS = 1e-05
PRECISE = lax.Precision.HIGHEST
PAD = 8
PLANE = 4
NEVER = -1e30


def pick(x, index, axis):
    return lax.dynamic_index_in_dim(x, index, axis, keepdims=False)


def put(buffer, piece, index, axis):
    return lax.dynamic_update_index_in_dim(buffer, piece, index, axis)


def swapped(x, bit):
    return lax.ppermute(x, "dp", [(i, i ^ bit) for i in range(lax.axis_size("dp"))])


def column_shift(x, steps):
    size = lax.axis_size("dp")
    return lax.ppermute(x, "dp", [(i, (i + PLANE * steps) % size) for i in range(size)])


def seq_shift(x, steps):
    size = lax.axis_size("seq")
    return lax.ppermute(x, "seq", [(i, (i + steps) % size) for i in range(size)])


def seq_sum(x):
    size = lax.axis_size("seq")
    if size == 2:
        return x + seq_shift(x, 1)
    return lax.psum(x, "seq")


def dp_sum(x):
    size = lax.axis_size("dp")
    if size & (size - 1):
        return lax.psum(x, "dp"), x
    bit = 1
    gate = x
    while bit < size:
        x = x + swapped(x, bit)
        gate = x if bit < PLANE else gate
        bit *= 2
    return x, gate


def place_kernel(at_ref, *refs, moves, inputs):
    ins, outs = refs[:inputs], refs[inputs:]
    for source, columns, target, where in moves:
        cols = slice(None) if columns is None else slice(*columns)
        outs[target][where(at_ref)] = ins[source][..., cols]


def place(at, pieces, shapes, moves, stepped=False):
    def spec(shape):
        if not stepped:
            return full()
        return pl.BlockSpec((1,) + shape[1:], lambda i: (i,) + (0,) * (len(shape) - 1))

    return pl.pallas_call(
        functools.partial(place_kernel, moves=moves, inputs=len(pieces)),
        grid=(pieces[0].shape[0],) if stepped else (),
        in_specs=[scalar()] + [spec(v.shape) for v in pieces],
        out_specs=[spec(shape) for shape in shapes],
        out_shape=[jax.ShapeDtypeStruct(shape, pieces[0].dtype) for shape in shapes],
    )(at, *pieces)


def gathered(block, cut, gate):
    spot = lax.axis_index("dp")
    at = jnp.stack([spot // PLANE, spot % PLANE // 2, spot % 2])
    height = lax.axis_size("dp") // PLANE
    rows, width = block.shape
    rest = width - cut
    moved = [column_shift(block, steps) for steps in range(1, height)]
    if gate is not None:
        moved, _ = lax.optimization_barrier((moved, gate))
    moves = []
    for k in range(height):
        slot = lambda ref, k=k: (lax.rem(ref[0] + (height - k), height),)
        moves += [(k, (0, cut), 0, slot), (k, (cut, width), 1, slot)]
    left, right = place(at, [block] + moved, [(height, rows, cut), (height, rows, rest)], moves)
    left_near, right_near = swapped(left, 1), swapped(right, 2)
    later = (left_near, right_near)
    every = slice(None)
    left, right = place(
        at,
        [left, left_near, right, right_near],
        [(height, 2, rows, cut), (height, 2, rows, rest)],
        [
            (0, None, 0, lambda ref: (every, ref[2])),
            (1, None, 0, lambda ref: (every, 1 - ref[2])),
            (2, None, 1, lambda ref: (every, ref[1])),
            (3, None, 1, lambda ref: (every, 1 - ref[1])),
        ],
        True,
    )
    left_far, right_far = swapped(left, 2), swapped(right, 1)
    left, right = place(
        at,
        [left, left_far, right, right_far],
        [(height, 2, 2, rows, cut), (height, 2, 2, rows, rest)],
        [
            (0, None, 0, lambda ref: (every, ref[1])),
            (1, None, 0, lambda ref: (every, 1 - ref[1])),
            (2, None, 1, lambda ref: (every, every, ref[2])),
            (3, None, 1, lambda ref: (every, every, 1 - ref[2])),
        ],
        True,
    )
    return left.reshape(-1, cut), right.reshape(-1, rest), later


def plane_sum(sent, kept, bit):
    at = lax.axis_index("dp")
    height = lax.axis_size("dp") // PLANE
    wide = jnp.float32
    near_bit = 3 - bit
    place = at % PLANE // near_bit % 2
    far = swapped(sent, bit)
    half = (kept.astype(wide) + far.astype(wide)).reshape(height, 2, -1, kept.shape[-1])
    near = swapped(pick(half, 1 - place, 1).astype(sent.dtype), near_bit)
    return pick(half, place, 1) + near.astype(wide), near


def column_sum(column, gate):
    height = lax.axis_size("dp") // PLANE
    tall = lax.axis_index("dp") // PLANE
    sent = column.astype(jnp.bfloat16)
    moved = [column_shift(pick(sent, (tall + k) % height, 0), k) for k in range(1, height)]
    return moved, pick(column, tall, 0), gate


def arrived_sum(parts, gate):
    moved, total, _ = parts
    if gate is not None:
        moved, _ = lax.optimization_barrier((moved, gate))
    for piece in moved:
        total = total + piece.astype(jnp.float32)
    return total


def dot(a, b, over):
    return lax.dot_general(a, b, ((over[0], over[1]), ((), ())), preferred_element_type=jnp.float32)


def spread(columns, width):
    lane = lax.broadcasted_iota(jnp.int32, (1, width), 1)
    out = columns[:, 0:1]
    for head in range(1, width // HEAD_DIM):
        out = jnp.where(lane >= head * HEAD_DIM, columns[:, head : head + 1], out)
    return jnp.broadcast_to(out, (columns.shape[0], width))


def conv_pre(padded_ref, weight, bias, count):
    summed = bias
    for offset in range(CONVK):
        start = PAD - (CONVK - 1) + offset
        summed = summed + weight[offset : offset + 1] * padded_ref[start : start + count, :]
    return summed


def sigmoid(v):
    return 1.0 / (1.0 + jnp.exp(-v))


def causal_mask():
    return lax.broadcasted_iota(jnp.int32, (GROUP, GROUP), 0) >= lax.broadcasted_iota(
        jnp.int32, (GROUP, GROUP), 1
    )


def own_lanes(values, lane):
    return pltpu.roll(values, (values.shape[1] - lane) % values.shape[1], 1)


def folded(values):
    total = values[:, :128]
    for at in range(128, values.shape[1], 128):
        total = total + values[:, at : at + 128]
    return total


def scan_forward(
    normed_ref, wx_ref, wg_ref, pulled_ref, bc_ref, delta_ref, cum_ref, cum_t_ref, par_ref,
    x_ref, gate_ref, mixed_ref, state_ref, sums_ref, pad_ref, *, lead,
):
    count, width = mixed_ref.shape
    bf = jnp.bfloat16
    at = lead + pl.program_id(0) * (width // HEAD_DIM)
    normed = normed_ref[...]
    conv_in = dot(normed, wx_ref[...], ((1,), (0,))).astype(bf)
    gate = dot(normed, wg_ref[...], ((1,), (0,)))
    x_ref[...] = conv_in
    gate_ref[...] = gate
    pad_ref[0:PAD, :] = jnp.zeros((PAD, width), jnp.float32)
    pad_ref[PAD : PAD + count, :] = conv_in.astype(jnp.float32)
    pre = conv_pre(pad_ref, par_ref[0:4, :], par_ref[4:5, :], count)
    acts = pre * sigmoid(pre)
    skip = par_ref[5:6, :]
    causal = causal_mask()
    lane = lax.broadcasted_iota(jnp.int32, (1, 2 * HEAD_DIM), 1)
    state = jnp.zeros((STATE, width), jnp.float32)

    @pl.when(pl.program_id(0) == 0)
    def _():
        sums_ref[...] = jnp.zeros(sums_ref.shape, jnp.float32)

    for group in range(count // GROUP):
        rows = slice(group * GROUP, (group + 1) * GROUP)
        state_ref[group] = state
        b_mat = bc_ref[rows, 0:STATE].astype(bf)
        c_mat = bc_ref[rows, STATE : 2 * STATE].astype(bf)
        inner = dot(c_mat, b_mat, ((1,), (1,)))
        x = acts[rows]
        cum = own_lanes(cum_ref[rows, :], at)
        cum_wide = spread(cum, width)
        last = cum_wide[GROUP - 1 : GROUP, :]
        xd = x * spread(own_lanes(delta_ref[rows, :], at), width)
        xdb = xd.astype(bf)
        y = dot(c_mat, state.astype(bf), ((1,), (0,))) * jnp.exp(cum_wide) + skip * x
        intra = []
        for pair in range(width // (2 * HEAD_DIM)):
            lanes = slice(pair * 2 * HEAD_DIM, (pair + 1) * 2 * HEAD_DIM)
            halves = []
            for head in (2 * pair, 2 * pair + 1):
                gap = jnp.where(causal, cum[:, head : head + 1] - cum_t_ref[pl.ds(at + head, 1), rows], NEVER)
                halves.append(dot((inner * jnp.exp(gap)).astype(bf), xdb[:, lanes], ((1,), (0,))))
            intra.append(jnp.where(lane < HEAD_DIM, halves[0], halves[1]))
        mixed = y + jnp.concatenate(intra, axis=1)
        mixed_ref[rows, :] = mixed
        tail = (xd * jnp.exp(last - cum_wide)).astype(bf)
        state = state * jnp.exp(last) + dot(b_mat, tail, ((0,), (0,)))
        part = gate[rows]
        gated = mixed * part * sigmoid(part)
        sums_ref[rows, 0:128] += folded(gated * gated)
        sums_ref[rows, 128:256] += folded(pulled_ref[rows, :] * par_ref[6:7, :] * gated)


def scan_backward(
    x_ref, gate_ref, mixed_ref, state_ref, pulled_ref, norm_ref, bc_ref, delta_ref, cum_ref, cum_t_ref, par_ref,
    *refs, lead, final,
):
    if final:
        gbc0_ref, gcum0_ref, gdelta0_ref, bcin_ref, step_ref, rate_ref, bcpar_ref = refs[:7]
        refs = refs[7:]
    gx_ref, ggate_ref, gbc_ref, gcum_ref, gdelta_ref, gpar_ref = refs[:6]
    if final:
        gstep_ref, gbcin_ref, gheads_ref, gbcpar_ref = refs[6:10]
    pad_ref, gpad_ref = refs[-2:]
    count, width = x_ref.shape
    bf = jnp.bfloat16
    heads = width // HEAD_DIM
    at = lead + pl.program_id(0) * heads
    pad_ref[0:PAD, :] = jnp.zeros((PAD, width), jnp.float32)
    pad_ref[PAD : PAD + count, :] = x_ref[...].astype(jnp.float32)
    pre = conv_pre(pad_ref, par_ref[0:4, :], par_ref[4:5, :], count)
    sig = sigmoid(pre)
    acts = pre * sig
    slope = sig * (1.0 + pre * (1.0 - sig))
    skip = par_ref[5:6, :]
    gain = par_ref[6:7, :]
    causal = causal_mask()
    lane = lax.broadcasted_iota(jnp.int32, (1, 2 * HEAD_DIM), 1)
    lane_wide = lax.broadcasted_iota(jnp.int32, (1, width), 1) // HEAD_DIM
    lane_all = lax.broadcasted_iota(jnp.int32, (1, 128), 1)
    grad_state = jnp.zeros((STATE, width), jnp.float32)
    gskip = jnp.zeros((1, width), jnp.float32)
    ggain = jnp.zeros((1, width), jnp.float32)

    @pl.when(pl.program_id(0) == 0)
    def _():
        gbc_ref[...] = gbc0_ref[...] if final else jnp.zeros(gbc_ref.shape, jnp.float32)
        gcum_ref[...] = gcum0_ref[...] if final else jnp.zeros(gcum_ref.shape, jnp.float32)
        gdelta_ref[...] = gdelta0_ref[...] if final else jnp.zeros(gdelta_ref.shape, jnp.float32)

    gpad_ref[count : count + PAD, :] = jnp.zeros((PAD, width), jnp.float32)
    for group in reversed(range(count // GROUP)):
        rows = slice(group * GROUP, (group + 1) * GROUP)
        scale, lean = norm_ref[rows, 0:1], norm_ref[rows, 1:2]
        gate, mixed, pulled = gate_ref[rows, :], mixed_ref[rows, :], pulled_ref[rows, :]
        sigma = sigmoid(gate)
        gated = mixed * gate * sigma
        ggain = ggain + jnp.sum(pulled * gated * scale, axis=0, keepdims=True)
        ggated = pulled * gain * scale - gated * lean
        ggate_ref[rows, :] = (ggated * mixed * sigma * (1.0 + gate * (1.0 - sigma))).astype(bf)
        gy = ggated * gate * sigma
        gyb = gy.astype(bf)
        b_mat = bc_ref[rows, 0:STATE].astype(bf)
        c_mat = bc_ref[rows, STATE : 2 * STATE].astype(bf)
        inner = dot(c_mat, b_mat, ((1,), (1,)))
        x = acts[rows]
        cum = own_lanes(cum_ref[rows, :], at)
        cum_wide = spread(cum, width)
        last = cum_wide[GROUP - 1 : GROUP, :]
        decay = jnp.exp(last)
        delta = spread(own_lanes(delta_ref[rows, :], at), width)
        xd = x * delta
        xdb = xd.astype(bf)
        tail = jnp.exp(last - cum_wide)
        state = state_ref[group]
        y = mixed - skip * x
        gye = (gy * jnp.exp(cum_wide)).astype(bf)
        gc = dot(gye, state.astype(bf), ((1,), (1,)))
        gsb = grad_state.astype(bf)
        gxd_tail = dot(b_mat, gsb, ((1,), (0,))) * tail
        gb = dot((xd * tail).astype(bf), gsb, ((1,), (1,)))
        xdf = xdb.astype(jnp.float32)
        glast = jnp.sum(xdf * gxd_tail, axis=0, keepdims=True) + decay * jnp.sum(
            grad_state * state, axis=0, keepdims=True
        )
        grad_state = grad_state * decay + dot(c_mat, gye, ((0,), (0,)))
        ginner = jnp.zeros((GROUP, GROUP), jnp.float32)
        intra = []
        for pair in range(width // (2 * HEAD_DIM)):
            lanes = slice(pair * 2 * HEAD_DIM, (pair + 1) * 2 * HEAD_DIM)
            halves = []
            for side in (0, 1):
                head = 2 * pair + side
                gap = jnp.where(causal, cum[:, head : head + 1] - cum_t_ref[pl.ds(at + head, 1), rows], NEVER)
                fall = jnp.exp(gap)
                weights = (inner * fall).astype(bf)
                own = (lane < HEAD_DIM) if side == 0 else (lane >= HEAD_DIM)
                gyh = jnp.where(own, gy[:, lanes], 0.0).astype(bf)
                ginner = ginner + dot(gyh, xdb[:, lanes], ((1,), (1,))) * fall
                halves.append(dot(weights, gyb[:, lanes], ((0,), (0,))))
            intra.append(jnp.where(lane < HEAD_DIM, halves[0], halves[1]))
        gxd = jnp.concatenate(intra, axis=1) + gxd_tail
        gib = ginner.astype(bf)
        gbc_ref[rows, 0:STATE] += gb + dot(gib, c_mat, ((0,), (0,)))
        gbc_ref[rows, STATE : 2 * STATE] += gc + dot(gib, b_mat, ((1,), (0,)))
        moved = gyb.astype(jnp.float32) * y - xdf * gxd
        drawn = x * gxd
        at_end = lax.broadcasted_iota(jnp.int32, (GROUP, 1), 0) == GROUP - 1
        cums = jnp.zeros((GROUP, 128), jnp.float32)
        draws = jnp.zeros((GROUP, 128), jnp.float32)
        for head in range(heads):
            mine = lane_wide == head
            here = jnp.sum(jnp.where(mine, moved, 0.0), axis=1, keepdims=True)
            end = jnp.sum(jnp.where(mine, glast, 0.0), axis=1, keepdims=True)
            place = lane_all == at + head
            cums = jnp.where(place, here + jnp.where(at_end, end, 0.0), cums)
            draws = jnp.where(place, jnp.sum(jnp.where(mine, drawn, 0.0), axis=1, keepdims=True), draws)
        gcum_ref[rows, :] += cums
        gdelta_ref[rows, :] += draws
        gskip = gskip + jnp.sum(gy * x, axis=0, keepdims=True)
        gpad_ref[rows, :] = (gxd * delta + skip * gy) * slope[rows]
    gpre = gpad_ref[0:count, :]
    total = jnp.zeros((count, width), jnp.float32)
    for offset in range(CONVK):
        ahead = CONVK - 1 - offset
        total = total + par_ref[offset : offset + 1, :] * gpad_ref[ahead : ahead + count, :]
        start = PAD - ahead
        gpar_ref[offset : offset + 1, :] = jnp.sum(
            gpre * pad_ref[start : start + count, :], axis=0, keepdims=True
        )
    gx_ref[...] = total.astype(bf)
    gpar_ref[4:5, :] = jnp.sum(gpre, axis=0, keepdims=True)
    gpar_ref[5:6, :] = gskip
    gpar_ref[6:7, :] = ggain
    gpar_ref[7:8, :] = jnp.zeros((1, width), jnp.float32)
    if not final:
        return

    @pl.when(pl.program_id(0) == pl.num_programs(0) - 1)
    def _():
        below = jnp.where(causal, 1.0, 0.0)
        step_sum = jnp.zeros((1, 128), jnp.float32)
        rate_sum = jnp.zeros((1, 128), jnp.float32)
        for group in range(count // GROUP):
            rows = slice(group * GROUP, (group + 1) * GROUP)
            ga = lax.dot_general(
                below, gcum_ref[rows, :], (((0,), (0,)), ((), ())), precision=PRECISE,
                preferred_element_type=jnp.float32,
            )
            gstep = (ga * rate_ref[0:1, :] + gdelta_ref[rows, :]) * sigmoid(step_ref[rows, :])
            gstep_ref[rows, :] = gstep.astype(bf)
            step_sum = step_sum + jnp.sum(gstep, axis=0, keepdims=True)
            rate_sum = rate_sum + jnp.sum(ga * delta_ref[rows, :], axis=0, keepdims=True)
        gheads_ref[0:1, :] = step_sum
        gheads_ref[1:2, :] = rate_sum * rate_ref[0:1, :]
        gheads_ref[2:8, :] = jnp.zeros((6, 128), jnp.float32)
        for lanes in range(0, 2 * STATE, width):
            cols = slice(lanes, lanes + width)
            pad_ref[PAD : PAD + count, :] = bcin_ref[:, cols].astype(jnp.float32)
            pre = conv_pre(pad_ref, bcpar_ref[0:4, cols], bcpar_ref[4:5, cols], count)
            sig = sigmoid(pre)
            gpre = gbc_ref[:, cols] * sig * (1.0 + pre * (1.0 - sig))
            gpad_ref[0:count, :] = gpre
            total = jnp.zeros((count, width), jnp.float32)
            for offset in range(CONVK):
                ahead = CONVK - 1 - offset
                total = total + bcpar_ref[offset : offset + 1, cols] * gpad_ref[ahead : ahead + count, :]
                start = PAD - ahead
                gbcpar_ref[offset : offset + 1, cols] = jnp.sum(
                    gpre * pad_ref[start : start + count, :], axis=0, keepdims=True
                )
            gbcin_ref[:, cols] = total.astype(bf)
            gbcpar_ref[4:5, cols] = jnp.sum(gpre, axis=0, keepdims=True)
            gbcpar_ref[5:8, cols] = jnp.zeros((3, width), jnp.float32)


def head_block(heads):
    return 4 if heads % 4 == 0 else 2


def fixed(shape):
    return pl.BlockSpec(shape, lambda i: (0,) * len(shape))


def moving(rows, width, at=0):
    return pl.BlockSpec((rows, width), lambda i: (0, i + at))


def mix_forward(part, heads, normed, w_x, w_gate, pulled, bc, delta, cum, cum_t, params):
    count, d_model = normed.shape
    block = head_block(heads)
    width = block * HEAD_DIM
    lead = heads // block * part
    groups = count // GROUP
    whole = heads * HEAD_DIM
    return pl.pallas_call(
        functools.partial(scan_forward, lead=heads * part),
        grid=(heads // block,),
        in_specs=[
            fixed((count, d_model)),
            moving(d_model, width),
            moving(d_model, width),
            moving(count, width, lead),
            fixed((count, 2 * STATE)),
            fixed((count, 128)),
            fixed((count, 128)),
            fixed((128, count)),
            moving(8, width, lead),
        ],
        out_specs=[
            moving(count, width),
            moving(count, width),
            moving(count, width),
            pl.BlockSpec((groups, STATE, width), lambda i: (0, 0, i)),
            fixed((count, 256)),
        ],
        out_shape=[
            jax.ShapeDtypeStruct((count, whole), jnp.bfloat16),
            jax.ShapeDtypeStruct((count, whole), jnp.float32),
            jax.ShapeDtypeStruct((count, whole), jnp.float32),
            jax.ShapeDtypeStruct((groups, STATE, whole), jnp.float32),
            jax.ShapeDtypeStruct((count, 256), jnp.float32),
        ],
        scratch_shapes=[pltpu.VMEM((count + PAD, width), jnp.float32)],
        name="scan",
    )(normed, w_x, w_gate, pulled, bc, delta, cum, cum_t, params)


def mix_backward(part, heads, x, gate, mixed, states, pulled, norms, bc, delta, cum, cum_t, params, *rest):
    count = x.shape[0]
    block = head_block(heads)
    width = block * HEAD_DIM
    lead = heads // block * part
    groups = count // GROUP
    whole = heads * HEAD_DIM
    f32, bf = jnp.float32, jnp.bfloat16
    in_specs = [
        moving(count, width),
        moving(count, width),
        moving(count, width),
        pl.BlockSpec((groups, STATE, width), lambda i: (0, 0, i)),
        moving(count, width, lead),
        fixed((count, 128)),
        fixed((count, 2 * STATE)),
        fixed((count, 128)),
        fixed((count, 128)),
        fixed((128, count)),
        moving(8, width, lead),
    ]
    out_specs = [moving(count, width)] * 2 + [fixed((count, 2 * STATE))] + [fixed((count, 128))] * 2
    out_specs += [moving(8, width)]
    shapes = [((count, whole), bf)] * 2 + [((count, 2 * STATE), f32)] + [((count, 128), f32)] * 2
    shapes += [((8, whole), f32)]
    if rest:
        in_specs += [fixed(v.shape) for v in rest]
        extra = [((count, 128), bf), ((count, 2 * STATE), bf), ((8, 128), f32), ((8, 2 * STATE), f32)]
        out_specs += [fixed(shape) for shape, _ in extra]
        shapes += extra
    return pl.pallas_call(
        functools.partial(scan_backward, lead=heads * part, final=bool(rest)),
        grid=(heads // block,),
        in_specs=in_specs,
        out_specs=out_specs,
        out_shape=[jax.ShapeDtypeStruct(*shape) for shape in shapes],
        scratch_shapes=[pltpu.VMEM((count + PAD, width), f32)] * 2,
        name="unscan",
    )(x, gate, mixed, states, pulled, norms, bc, delta, cum, cum_t, params, *rest)


def halves_kernel(at_ref, *refs, parts, tall):
    left, rights, (sent_ref, kept_ref) = refs[:-parts - 2], refs[-parts - 2 : -2], refs[-2:]
    low = at_ref[0] == 0
    lanes = 0
    for right_ref in rights:
        right = right_ref[...]
        cols = slice(lanes, lanes + right.shape[1])
        lanes += right.shape[1]
        if tall:
            sent_ref[:, cols] = dot(left[0][...], right, ((0,), (0,))).astype(sent_ref.dtype)
            kept_ref[:, cols] = dot(left[1][...], right, ((0,), (0,))).astype(sent_ref.dtype)
        else:
            rows = dot(left[0][...], right, ((0,), (0,)))
            for y in (0, 1):
                first = rows[128 * y : 128 * y + 64]
                second = rows[128 * y + 64 : 128 * y + 128]
                to = slice(64 * y, 64 * y + 64)
                sent_ref[to, cols] = jnp.where(low, second, first).astype(sent_ref.dtype)
                kept_ref[to, cols] = jnp.where(low, first, second).astype(sent_ref.dtype)


def halves(left, rights, bit):
    count, rows = left.shape
    tall = bit == 2
    at = (lax.axis_index("dp") % PLANE // bit % 2).reshape(1)
    if tall:
        lefts = [
            pl.BlockSpec((count, 128), lambda i, at: (0, 2 * i + 1 - at[0])),
            pl.BlockSpec((count, 128), lambda i, at: (0, 2 * i + at[0])),
        ]
    else:
        lefts = [pl.BlockSpec((count, 256), lambda i, at: (0, i))]
    width = sum(v.shape[1] for v in rights)
    shape = jax.ShapeDtypeStruct((rows // 2, width), jnp.bfloat16)
    return pl.pallas_call(
        functools.partial(halves_kernel, parts=len(rights), tall=tall),
        grid_spec=pltpu.PrefetchScalarGridSpec(
            num_scalar_prefetch=1,
            grid=(rows // 256,),
            in_specs=lefts + [pl.BlockSpec(v.shape, lambda i, at: (0, 0)) for v in rights],
            out_specs=[pl.BlockSpec((128, width), lambda i, at: (i, 0))] * 2,
        ),
        out_shape=[shape, shape],
        name="halves",
    )(at, *([left] * len(lefts)), *rights)


def product_kernel(at_ref, *refs, parts):
    lefts, rights, outs = refs[:parts], refs[parts : 2 * parts], refs[2 * parts :]
    rows = outs[0].shape[0]
    for out_ref, place in ((outs[0], at_ref[0]), (outs[1], 1 - at_ref[0])):
        total = 0.0
        for left_ref, right_ref in zip(lefts, rights):
            total = total + dot(left_ref[pl.ds(place * rows, rows), :], right_ref[...], ((1,), (1,)))
        out_ref[...] = total


def product(at, lefts, rights):
    count, width = lefts[0].shape[0], rights[0][0].shape[0]
    block = 256
    shape = jax.ShapeDtypeStruct((count // 2, width), jnp.float32)
    return pl.pallas_call(
        functools.partial(product_kernel, parts=len(lefts)),
        grid_spec=pltpu.PrefetchScalarGridSpec(
            num_scalar_prefetch=1,
            grid=(width // block,),
            in_specs=[pl.BlockSpec(v.shape, lambda i, at: (0, 0)) for v in lefts]
            + [pl.BlockSpec((block, wide), lambda i, at, n=start // wide: (i, n)) for _, wide, start in rights],
            out_specs=[pl.BlockSpec((count // 2, block), lambda i, at: (0, i))] * 2,
        ),
        out_shape=[shape, shape],
        name="product",
    )(at.reshape(1), *lefts, *(v for v, _, _ in rights))


def unzip(at_ref, in_ref, own_ref, other_ref, *, chans, half, heads):
    even = at_ref[0] == 0
    lane = lax.broadcasted_iota(jnp.int32, (1, 128), 1)
    step_at, bc_at = 2 * chans + 2 * STATE, 2 * chans
    kind = own_ref.dtype

    def emit(low, high, to):
        own_ref[:, to : to + 128] = jnp.where(even, low, high).astype(kind)
        other_ref[:, to : to + 128] = jnp.where(even, high, low).astype(kind)

    for source, starts in ((chans, (0, 2 * half + 384)), (0, (half + 128, 3 * half + 384))):
        for at in range(0, chans // 2, 128):
            a = in_ref[:, source + 2 * at : source + 2 * at + 128].astype(jnp.float32)
            b = in_ref[:, source + 2 * at + 128 : source + 2 * at + 256].astype(jnp.float32)
            low = jnp.where(lane < HEAD_DIM, a, pltpu.roll(b, HEAD_DIM, 1))
            high = jnp.where(lane < HEAD_DIM, pltpu.roll(a, HEAD_DIM, 1), b)
            emit(low, high, starts[at // half] + at % half)
    steps = in_ref[:, step_at : step_at + heads]
    row = lax.broadcasted_iota(jnp.int32, (heads, 128), 0)
    col = lax.broadcasted_iota(jnp.int32, (heads, 128), 1)
    sides = [
        dot(steps, jnp.where((row == 2 * col + side) & (col < heads // 2), 1.0, 0.0).astype(kind), ((1,), (0,)))
        for side in (0, 1)
    ]
    emit(sides[0], sides[1], half)
    bc = in_ref[:, bc_at:step_at]
    own_ref[:, 2 * half + 128 : 2 * half + 384] = bc
    other_ref[:, 2 * half + 128 : 2 * half + 384] = bc


def zipped(at_ref, own1_ref, other1_ref, own2_ref, other2_ref, out_ref, *, chans, half, heads):
    even = at_ref[0] == 0
    lane = lax.broadcasted_iota(jnp.int32, (1, 128), 1)
    bc_at, step_at = 2 * chans, 2 * chans + 2 * STATE
    for target, lead in ((chans, 0), (0, 1)):
        for at in range(0, chans // 2, 128):
            second = at >= half
            to = at % half + lead * (half if second else half + 128)
            own_ref, other_ref = (own2_ref, other2_ref) if second else (own1_ref, other1_ref)
            own, other = own_ref[:, to : to + 128], other_ref[:, to : to + 128]
            low, high = jnp.where(even, own, other), jnp.where(even, other, own)
            out_ref[:, target + 2 * at : target + 2 * at + 128] = jnp.where(
                lane < HEAD_DIM, low, pltpu.roll(high, HEAD_DIM, 1)
            )
            out_ref[:, target + 2 * at + 128 : target + 2 * at + 256] = jnp.where(
                lane < HEAD_DIM, pltpu.roll(low, HEAD_DIM, 1), high
            )
    cols = slice(2 * half + 128, 2 * half + 384)
    out_ref[:, bc_at:step_at] = own1_ref[:, cols] + other1_ref[:, cols]
    row = lax.broadcasted_iota(jnp.int32, (128, heads), 0)
    col = lax.broadcasted_iota(jnp.int32, (128, heads), 1)
    own, other = own1_ref[:, half : half + 128], other1_ref[:, half : half + 128]
    total = 0.0
    for side, values in ((0, jnp.where(even, own, other)), (1, jnp.where(even, other, own))):
        choice = jnp.where((col == 2 * row + side) & (row < heads // 2), 1.0, 0.0)
        total = total + lax.dot_general(
            values, choice, (((1,), (0,)), ((), ())), precision=PRECISE, preferred_element_type=jnp.float32
        )
    out_ref[:, step_at : step_at + heads] = total


def own_params(at_ref, rows_ref, heads_ref, own_ref, own_heads_ref):
    even = at_ref[0] == 0
    lane = lax.broadcasted_iota(jnp.int32, (1, 128), 1)
    for at in range(0, own_ref.shape[1], 128):
        a, b = rows_ref[:, 2 * at : 2 * at + 128], rows_ref[:, 2 * at + 128 : 2 * at + 256]
        low = jnp.where(lane < HEAD_DIM, a, pltpu.roll(b, HEAD_DIM, 1))
        high = jnp.where(lane < HEAD_DIM, pltpu.roll(a, HEAD_DIM, 1), b)
        own_ref[:, at : at + 128] = jnp.where(even, low, high)
    heads = heads_ref.shape[1]
    row = lax.broadcasted_iota(jnp.int32, (heads, 128), 0)
    col = lax.broadcasted_iota(jnp.int32, (heads, 128), 1)
    choice = jnp.where((row == 2 * col + at_ref[0]) & (col < heads // 2), 1.0, 0.0)
    own_heads_ref[...] = lax.dot_general(
        heads_ref[...], choice, (((1,), (0,)), ((), ())), precision=PRECISE, preferred_element_type=jnp.float32
    )


def scalar():
    return pl.BlockSpec(memory_space=pltpu.SMEM)


def full():
    return pl.BlockSpec(memory_space=pltpu.VMEM)


def unzip_columns(at, rows, half):
    shape = jax.ShapeDtypeStruct((rows.shape[0], 4 * half + 384), rows.dtype)
    return pl.pallas_call(
        functools.partial(unzip, chans=D_INNER, half=half, heads=HEADS),
        in_specs=[scalar(), full()],
        out_specs=[full(), full()],
        out_shape=[shape, shape],
        name="unzip",
    )(at.reshape(1), rows)


def zip_columns(at, own1, other1, own2, other2, half):
    return pl.pallas_call(
        functools.partial(zipped, chans=D_INNER, half=half, heads=HEADS),
        in_specs=[scalar()] + [full()] * 4,
        out_specs=full(),
        out_shape=jax.ShapeDtypeStruct((own1.shape[0], D_INNER + CONV_CH + HEADS), jnp.float32),
        name="zip",
    )(at.reshape(1), own1, other1, own2, other2)


def rms_scale(values, gain):
    return values * lax.rsqrt(jnp.mean(values * values, axis=-1, keepdims=True) + EPS) * gain


def conv_act(values, conv_weight, conv_bias):
    count = values.shape[0]
    extended = jnp.concatenate([jnp.zeros((CONVK - 1, values.shape[1]), jnp.float32), values], axis=0)
    summed = conv_bias[None, :] + conv_weight[0][None, :] * extended[0:count]
    for offset in range(1, CONVK):
        summed = summed + conv_weight[offset][None, :] * extended[offset : offset + count]
    return jax.nn.silu(summed)


class Split:
    def __init__(self, out_rows, d_model):
        self.peers = lax.axis_size("seq")
        self.at = lax.axis_index("seq")
        blocks = lax.axis_size("dp")
        self.staged = out_rows == HEAD_DIM and blocks * HEAD_DIM == d_model and blocks % PLANE == 0 and self.peers == 2
        self.outer = blocks if self.staged else 1

    def view(self, v):
        return v.reshape(v.shape[:-1] + (self.outer, self.peers, v.shape[-1] // (self.outer * self.peers)))

    def own(self, v, at=None):
        part = pick(self.view(v), self.at if at is None else at, v.ndim)
        return part.reshape(v.shape[:-1] + (-1,))

    def place(self, whole, part, at=None):
        view = self.view(whole)
        piece = part.reshape(view.shape[:-2] + view.shape[-1:])
        return put(view, piece, self.at if at is None else at, whole.ndim).reshape(whole.shape)

    def placed(self, part):
        return self.place(jnp.zeros(part.shape[:-1] + (part.shape[-1] * self.peers,), part.dtype), part)

    def exchange(self, piece_for):
        pieces = [(self.at, piece_for(self.at))]
        for steps in range(1, self.peers):
            sent = piece_for((self.at + steps) % self.peers)
            pieces.append(((self.at - steps) % self.peers, seq_shift(sent, steps)))
        return pieces

    def scatter_rows(self, x):
        rows = x.reshape((self.peers, x.shape[0] // self.peers) + x.shape[1:])
        total = 0.0
        for _, piece in self.exchange(lambda to: pick(rows, to, 0)):
            total = total + piece
        return total


def per_device(
    hidden_in, upstream, in_weight, out_weight, norm_gain, conv_weight, conv_bias,
    step_bias, log_rate, skip_weight, gate_gain,
):
    bf = jnp.bfloat16
    split = Split(*out_weight.shape)
    peers, at = split.peers, split.at
    stream, grad_top = hidden_in[0], upstream[0]
    own_rows, d_model = stream.shape
    count = own_rows * peers
    groups = count // GROUP
    heads = HEADS // peers
    inner = D_INNER // peers
    half_heads = heads // 2
    half = inner // 2
    lanes = -(-heads // 128) * 128

    def in_columns(rows):
        x = split.own(rows[:, D_INNER : 2 * D_INNER])
        gate = split.own(rows[:, :D_INNER])
        bc = rows[:, 2 * D_INNER : D_INNER + CONV_CH]
        steps = split.own(rows[:, D_INNER + CONV_CH :])
        blank = jnp.zeros((rows.shape[0], lanes - heads), rows.dtype)
        return (
            jnp.concatenate([x[:, :half], steps, blank], axis=1),
            jnp.concatenate([gate[:, :half], bc], axis=1),
            x[:, half:],
            gate[:, half:],
        )

    first_cut = half + lanes
    first_width = first_cut + half + 2 * STATE
    if split.staged:
        own, other = unzip_columns(at, in_weight, half)
        arrived = seq_shift(other, 1)
        here = lambda ref: (ref[0],)
        there = lambda ref: (1 - ref[0],)
        total = own.shape[1]
        block_first, block_second = place(
            at.reshape(1),
            [own, arrived],
            [(peers, own.shape[0], first_width), (peers, own.shape[0], total - first_width)],
            [
                (source, columns, target, where)
                for source, where in ((0, here), (1, there))
                for target, columns in ((0, (0, first_width)), (1, (first_width, total)))
            ],
        )
        block_first = block_first.reshape(-1, first_width)
        block_second = block_second.reshape(-1, total - first_width)

    normed_own = rms_scale(stream, norm_gain).astype(bf)
    both = jnp.concatenate([normed_own, grad_top.astype(bf)], axis=1)
    half_model = d_model // 2
    if split.staged:
        arrived = seq_shift(both, 1)
        spans = ((0, d_model), (d_model, d_model + half_model), (d_model + half_model, 2 * d_model))
        normed, top_left, top_right = place(
            at.reshape(1),
            [both, arrived],
            [(peers, own_rows, stop - start) for start, stop in spans],
            [
                (source, span, target, where)
                for source, where in ((0, here), (1, there))
                for target, span in enumerate(spans)
            ],
        )
        normed, top_left, top_right = (v.reshape(count, -1) for v in (normed, top_left, top_right))
    else:
        tokens = jnp.zeros((peers,) + both.shape, bf)
        for origin, part in split.exchange(lambda to: both):
            tokens = put(tokens, part, origin, 0)
        tokens = tokens.reshape(count, -1)
        normed, top = tokens[:, :d_model], tokens[:, d_model:]
        top_left, top_right = top[:, :half_model], top[:, half_model:]

    if split.staged:
        out_left, out_right, gate = gathered(out_weight, d_model // 2, None)
        x_first, gate_first, gate = gathered(block_first, first_cut, gate)
        x_second, gate_second, _ = gathered(block_second, half, gate)
    else:
        in_all = lax.all_gather(in_weight, ("dp", "seq"), axis=0, tiled=True)
        x_first, gate_first, x_second, gate_second = in_columns(in_all)
        out_all = split.own(lax.all_gather(out_weight, ("dp", "seq"), axis=0, tiled=True).T).T
        out_left, out_right = out_all[:, : d_model // 2], out_all[:, d_model // 2 :]

    rows = jnp.concatenate(
        [
            conv_weight[:, :D_INNER],
            conv_bias[None, :D_INNER],
            jnp.repeat(skip_weight, HEAD_DIM)[None],
            gate_gain[None],
            jnp.zeros((1, D_INNER), jnp.float32),
        ],
        axis=0,
    )
    head_pair = jnp.concatenate([step_bias[None], log_rate[None], jnp.zeros((6, HEADS), jnp.float32)], axis=0)
    if split.staged:
        params, head_pair = pl.pallas_call(
            own_params,
            in_specs=[scalar(), full(), full()],
            out_specs=[full(), full()],
            out_shape=[
                jax.ShapeDtypeStruct((8, inner), jnp.float32),
                jax.ShapeDtypeStruct((8, lanes), jnp.float32),
            ],
            name="own",
        )(at.reshape(1), rows, head_pair)
    else:
        params = split.own(rows)
        head_pair = jnp.pad(split.own(head_pair), ((0, 0), (0, lanes - heads)))
    own_gain = params[CONVK + 2]
    own_bias = head_pair[0:1]
    all_rates = jnp.where(jnp.arange(lanes)[None, :] < heads, -jnp.exp(head_pair[1:2]), 0.0)
    tri = (jnp.arange(GROUP)[:, None] >= jnp.arange(GROUP)[None, :]).astype(jnp.float32)

    bc_params = jnp.concatenate(
        [conv_weight[:, D_INNER:], conv_bias[None, D_INNER:], jnp.zeros((3, 2 * STATE), jnp.float32)], axis=0
    )
    step_raw = dot(normed, x_first[:, half:], ((1,), (0,)))
    step_in = step_raw + own_bias
    deltas = jax.nn.softplus(step_in)
    cum = jnp.einsum(
        "ts,gsh->gth", tri, (deltas * all_rates).reshape(groups, GROUP, lanes), precision=PRECISE
    ).reshape(count, lanes)
    cum_t = cum.T
    bc_in = dot(normed, gate_first[:, half:], ((1,), (0,))).astype(bf)
    bc = conv_act(bc_in.astype(jnp.float32), bc_params[:CONVK], bc_params[CONVK])

    pulled = dot(top_left, out_left, ((1,), (1,))) + dot(top_right, out_right, ((1,), (1,)))
    saved = []
    for part, (w_x, w_gate) in enumerate(((x_first, gate_first), (x_second, gate_second))):
        saved.append(mix_forward(part, half_heads, normed, w_x, w_gate, pulled, bc, deltas, cum, cum_t, params))
    sums = saved[0][4] + saved[1][4]
    sums = jnp.stack([jnp.sum(sums[:, :128], axis=1), jnp.sum(sums[:, 128:], axis=1)])
    sums = seq_sum(sums)
    scale = lax.rsqrt(sums[0] / D_INNER + EPS)
    lean = sums[1] * scale * scale * scale / D_INNER
    norms = jnp.pad(jnp.stack([scale, lean], axis=1), ((0, 0), (0, 126)))

    normed_out = jnp.concatenate(
        [
            (mixed * jax.nn.silu(gate) * scale[:, None] * own_gain[None, part * half : (part + 1) * half]).astype(bf)
            for part, (_, gate, mixed, _, _) in enumerate(saved)
        ],
        axis=1,
    )
    if split.staged:
        out_halves = halves(normed_out, (top_left, top_right), 2)
        out_column, _ = plane_sum(*out_halves, 2)

    gx1, ggate1, *carried, gpar1 = mix_backward(
        1, half_heads, *saved[1][:4], pulled, norms, bc, deltas, cum, cum_t, params
    )
    if split.staged:
        second_halves = halves(normed, (gx1, ggate1), 1)
        second_column, gate = plane_sum(*second_halves, 1)
        second_parts = column_sum(jnp.concatenate([out_column, second_column], axis=-1), gate)
    gx0, ggate0, _, _, _, gpar0, gstep, gbc, gheads, gbc_par = mix_backward(
        0, half_heads, *saved[0][:4], pulled, norms, bc, deltas, cum, cum_t, params,
        *carried, bc_in, step_in, jnp.broadcast_to(all_rates, (8, lanes)), bc_params,
    )
    grads = (gx0, gstep, ggate0, gbc, gx1, ggate1)
    columns = (
        (x_first, half, 0), (x_first, lanes, half), (gate_first, half, 0), (gate_first, 2 * STATE, half),
        (x_second, half, 0), (gate_second, half, 0),
    )
    if split.staged:
        left_halves = halves(normed, (gx0, gstep), 2)
        right_halves = halves(normed, (ggate0, gbc), 1)
        left, near_left = plane_sum(*left_halves, 2)
        right, near_right = plane_sum(*right_halves, 1)
        gate = (near_left, near_right)
        first_parts = column_sum(jnp.concatenate([left, right], axis=-1), gate)
        kept, sent = product(at, grads, columns)
        grad_normed = kept + seq_shift(sent, 1)
    else:
        grad_normed = 0.0
        for side, (weight, width, start) in zip(grads, columns):
            grad_normed = grad_normed + dot(side, weight[:, start : start + width], ((1,), (1,)))
        grad_normed = split.scatter_rows(grad_normed)

    def block_rows(to):
        rows = lax.dynamic_slice_in_dim(normed_out, to * own_rows, own_rows, 0)
        return jnp.concatenate([dot(rows, side, ((1,), (0,))) for side in (out_left, out_right)], axis=1)

    block_out = stream
    for _, piece in split.exchange(block_rows):
        block_out = block_out + piece
    _, norm_back = jax.vjp(rms_scale, stream, norm_gain)
    grad_stream, grad_norm_gain = norm_back(grad_normed)

    small = (gpar0, gpar1, gbc_par, gheads, grad_norm_gain)
    packed, packed_gate = dp_sum(jnp.concatenate([v.reshape(-1, 128) for v in small]))
    other_packed = None
    if split.staged:
        other_packed = seq_shift(packed, 1)
    summed = []
    for source in (packed, other_packed):
        offset, parts = 0, []
        for v in small:
            parts.append(None if source is None else source[offset : offset + v.size // 128].reshape(v.shape))
            offset += v.size // 128
        summed.append(parts)
    mine, theirs = summed
    shared = [None, None]
    for n, k in ((0, 2), (1, 4)):
        shared[n] = mine[k] + theirs[k] if split.staged else lax.psum(mine[k], "seq")

    def spread_rows(pick_row):
        own_row = pick_row(mine)
        if split.staged:
            other_row = pick_row(theirs)
            view = own_row.shape[:-1] + (split.outer, own_row.shape[-1] // split.outer)
            own_row, other_row = own_row.reshape(view), other_row.reshape(view)
            low = jnp.where(at == 0, own_row, other_row)
            high = jnp.where(at == 0, other_row, own_row)
            return jnp.stack([low, high], axis=-2).reshape(view[:-2] + (-1,))
        return lax.psum(split.placed(own_row), "seq")

    rows = spread_rows(lambda v: jnp.concatenate([v[0], v[1]], axis=1))
    head_rows = spread_rows(lambda v: v[3][:, :heads])
    grad_bc_par = shared[0]
    small_out = (
        jnp.concatenate([rows[:CONVK], grad_bc_par[:CONVK]], axis=1),
        jnp.concatenate([rows[CONVK], grad_bc_par[CONVK]]),
        head_rows[0],
        head_rows[1],
        jnp.sum(rows[CONVK + 1].reshape(HEADS, HEAD_DIM), axis=1),
        rows[CONVK + 2],
    )

    if split.staged:
        both_share = arrived_sum(second_parts, gate)
        out_share = both_share[:, :d_model]
        pairs = []
        for share in (arrived_sum(first_parts, packed_gate), both_share[:, d_model:]):
            pair = share.reshape(peers, -1, share.shape[-1])
            pairs += [pick(pair, at, 0), seq_shift(pick(pair, 1 - at, 0), 1)]
        in_share = zip_columns(at, *pairs, half)
    else:
        empty = jnp.zeros((d_model, D_INNER), jnp.float32)
        x_low, step_low, gate_low, bc_low, x_high, gate_high = (dot(normed, side, ((0,), (0,))) for side in grads)
        in_share = jnp.concatenate(
            [
                split.place(empty, jnp.concatenate([gate_low, gate_high], axis=1)),
                split.place(empty, jnp.concatenate([x_low, x_high], axis=1)),
                bc_low,
                split.placed(step_low[:, :heads]),
            ],
            axis=1,
        )
        in_share = lax.psum_scatter(in_share, ("dp", "seq"), scatter_dimension=0, tiled=True)
        grad_out = dot(normed_out, jnp.concatenate([top_left, top_right], axis=1), ((0,), (0,)))
        out_share = lax.psum_scatter(
            split.placed(grad_out.T).T, ("dp", "seq"), scatter_dimension=0, tiled=True
        )

    return (
        block_out[None], (grad_top + grad_stream)[None], in_share, out_share, shared[1], *small_out,
    )


def solution(mesh):
    tokens, rows, whole = P("dp", "seq", None), P(("dp", "seq"), None), P()
    return jax.shard_map(
        per_device,
        mesh=mesh,
        in_specs=(tokens, tokens, rows, rows) + (whole,) * 7,
        out_specs=(tokens, tokens, rows, rows) + (whole,) * 7,
        check_vma=False,
    )
```
